128 devices in a mesh: prow: 8 (over y, core), pcol: 16 (over x, z).
Axes of the slice: x: 4, y: 4, z: 4, core: 2. Of those that a mesh axis runs over, the one named last changes fastest.
Arguments:
- assembly: float32 [8, 512, 2, 128, 128], P('prow', 'pcol'), may hold values from -6 to 6
- slot_tile: int32 [8, 512], P('prow', 'pcol'), may hold values from 0 to 511, as said below
- pivots: int32 [2, 128], replicated, may hold values from 0 to 16383, as said below
- inverses: float32 [2, 2, 128, 128], replicated, may hold values from -0.046875 to 0.046875
Outputs:
- factored: float32 [2, 16384, 4096], P(None, 'prow', 'pcol')
The draws below stay inside these ranges and needn't reach their ends.
Inputs may be any that keep to these rules, and one draw needn't show every extreme that they name: `slot_tile`: row p lists tile ids t = i*32 + b, i the row tile among those of prow p and b the column tile; each of prow p's tiles appears in exactly one slot. A device's 32 slots hold at most 3 tiles whose column owner b % 16 is one index, and every device holds exactly 3 for some owner. `pivots`: entry j of panel k is either k*128 + j (no swap) or a row at or past 2*128; the rows named in one panel differ.
All inputs are finite; a program needn't handle non-finite values.
Results may differ from the reference program's by a relative error of at most 0.00013.
Values sent between devices are 32-bit elements; how exact they have to be, the bound alone decides.
A program may use at most 128 MiB of HBM per device.

```python
import jax
import jax.numpy as jnp
import numpy as np
from jax import lax

NB = 128
CBLK = 2
RT_DEV = 16
GRID_ROWS = 8
GRID_COLS = 16
M = 16384
NC = 4096
NCB = 32
SLOTS_DEV = 32
CAP = 3


def count_table():
    mean_load = CAP - 1
    counts = [CAP, mean_load - 1]
    remaining = SLOTS_DEV - 2 * mean_load
    for owner in range(2, GRID_COLS):
        take = min(mean_load, max(remaining, 0))
        counts.append(take)
        remaining = remaining - take
    return np.array(counts, np.int32)


def draw_slot_tile(key, part):
    base = jnp.array(count_table())
    slots = jnp.arange(SLOTS_DEV, dtype=jnp.int32)

    def one_row(prow_index):
        row_key = jax.random.fold_in(key, prow_index)
        counts = base[jax.random.permutation(jax.random.fold_in(row_key, 1), GRID_COLS)]
        ends = jnp.cumsum(counts)
        offset = jnp.sum((slots[:, None] >= ends[None, :]).astype(jnp.int32), axis=1)

        def dest_order(dest):
            return jax.random.permutation(jax.random.fold_in(row_key, 100 + dest), SLOTS_DEV)
        orders = jax.vmap(dest_order)(jnp.arange(GRID_COLS, dtype=jnp.int32))

        def one_source(source):
            dest = (source + offset) % GRID_COLS
            owned = orders[dest, slots]
            tile_ids = owned // CBLK * NCB + owned % CBLK * GRID_COLS + dest
            shuffle = jax.random.permutation(jax.random.fold_in(row_key, 5000 + source), SLOTS_DEV)
            return tile_ids[shuffle]
        return jax.vmap(one_source)(jnp.arange(GRID_COLS, dtype=jnp.int32)).reshape(-1)
    return jax.vmap(one_row)(jnp.arange(GRID_ROWS, dtype=jnp.int32)).astype(jnp.int32)


def draw_pivots(key, part):

    def one_panel(panel):
        panel_key = jax.random.fold_in(key, 7 + panel)
        rows = jax.random.permutation(jax.random.fold_in(panel_key, 1), M - 2 * NB - 1)[:NB - 1] + 2 * NB
        rows = jnp.concatenate([rows.astype(jnp.int32), jnp.array([M - 1], jnp.int32)])
        order = jax.random.permutation(jax.random.fold_in(panel_key, 2), NB)
        rows = rows[order]
        stay = (jax.random.randint(jax.random.fold_in(panel_key, 3), (NB,), 0, 4) == 0) & (order != NB - 1)
        return jnp.where(stay, panel * NB + jnp.arange(NB, dtype=jnp.int32), rows)
    return jax.vmap(one_panel)(jnp.arange(2, dtype=jnp.int32)).astype(jnp.int32)


def block_levels(own_key, extent, pieces, low, top_value):
    def one(dim, shards_of):
        draws = jax.random.uniform(jax.random.fold_in(jax.random.fold_in(own_key, 6), dim), (shards_of,), jnp.float32, low / len(pieces), top_value / len(pieces))
        return jnp.repeat(jnp.exp(draws), extent[dim] // shards_of).reshape((-1,) + (1,) * (len(extent) - dim - 1))

    factor_of = one(*pieces[0])
    for cut in pieces[1:]:
        factor_of = factor_of * one(*cut)
    return factor_of


def normal_values(key, shape, width, reach, split=(), kind=jnp.bfloat16):
    factor_of = block_levels(key, shape, split, -0.22, 0.18) if split else 1.0
    values = jax.random.normal(key, shape, jnp.float32) * width * factor_of
    return jnp.minimum(jnp.maximum(values, -reach), reach).astype(kind)


def setup_inputs(seed: int = 0) -> dict:
    key_list = jax.random.split(jax.random.key(seed), 5)
    assembly = normal_values(key_list[0], (GRID_ROWS, GRID_COLS * SLOTS_DEV, 2, NB, NB), 1.0, 6.0, ((0, 8), (1, 16)), jnp.float32)
    slot_tile = draw_slot_tile(jax.random.fold_in(key_list[4], 71), 0)
    pivots = draw_pivots(jax.random.fold_in(key_list[4], 71), 0)
    inverses = normal_values(key_list[3], (2, 2, NB, NB), (NB * NB) ** -0.5, 0.046875, (), jnp.float32)
    return {"assembly": assembly, "slot_tile": slot_tile, "pivots": pivots, "inverses": inverses}


def complex_product(left, right):
    def dot(a, b):
        return jnp.matmul(a, b, precision=lax.Precision.HIGHEST)
    real = dot(left[0], right[0]) - dot(left[1], right[1])
    imag = dot(left[0], right[1]) + dot(left[1], right[0])
    return jnp.stack([real, imag])


def reference(assembly, slot_tile, pivots, inverses):
    stacked = []
    for prow_index in range(GRID_ROWS):
        holder = jnp.zeros((RT_DEV * NCB, 2, NB, NB), assembly.dtype)
        holder = holder.at[slot_tile[prow_index]].set(assembly[prow_index])
        stacked.append(holder.reshape(RT_DEV, NCB, 2, NB, NB))
    grid = jnp.stack(stacked)
    matrix = grid.transpose(3, 1, 0, 4, 2, 5).reshape(2, M, NC)
    for panel in range(2):
        start = panel * NB
        diag_rows = start + jnp.arange(NB, dtype=jnp.int32)
        chosen = pivots[panel]
        old_top = matrix[:, diag_rows, :]
        picked = matrix[:, chosen, :]
        matrix = matrix.at[:, chosen, :].set(old_top)
        matrix = matrix.at[:, diag_rows, :].set(picked)
        upper = matrix[:, start:start + NB, start + NB:]
        lower = complex_product(matrix[:, start + NB:, start:start + NB], inverses[panel])
        matrix = matrix.at[:, start + NB:, start:start + NB].set(lower)
        matrix = matrix.at[:, start + NB:, start + NB:].add(-complex_product(lower, upper))
    stored = matrix.reshape(2, RT_DEV, GRID_ROWS, NB, CBLK, GRID_COLS, NB)
    stored = stored.transpose(0, 2, 1, 3, 5, 4, 6).reshape(2, M, NC)
    return stored
```

```python
import functools

import jax
import jax.numpy as jnp
from jax import lax
from jax.experimental import pallas as pl
from jax.experimental.pallas import tpu as pltpu
from jax.sharding import PartitionSpec as P

CBLK = 2
NB = 128
MESH = pl.DeviceIdType.MESH
HI = lax.Precision.HIGHEST


def comm_kernel(
    dims, idx_ref, piv_ref, lab_ref, asm_hbm,
    m_hbm, ag_hbm, fin_hbm, wfin_hbm,
    asm, sendb, recvb, labs, mat, pb, ag, pk, rb, fin, wfin, place,
    out_sem, lab_s, lab_r, a_s, a_r, sc_s, sc_r, rs_s, rs_r, t_s, t_r, y_s, y_r, wb_s, wb_r, wy_s, wy_r,
    g1_s, g1_r, g2_s, g2_r,
):
    rows_n, nx, nz, cap, row_tiles = dims
    cols_n = nx * nz
    sl = NB // rows_n
    half = NB // 2
    me_r = lax.axis_index("prow")
    me_c = lax.axis_index("pcol")
    me_x = me_c // nz
    me_z = me_c % nz

    def remote(src, dst, ssem, rsem, row, col):
        return pltpu.make_async_remote_copy(
            src_ref=src, dst_ref=dst, send_sem=ssem, recv_sem=rsem,
            device_id=(row, col), device_id_type=MESH)

    load = pltpu.make_async_copy(asm_hbm, asm, out_sem.at[4])
    load.start()

    barrier = pltpu.get_barrier_semaphore()

    def greet_col(k, c):
        pl.semaphore_signal(barrier, inc=1, device_id=(me_r, (me_c + k) % cols_n), device_id_type=MESH)
        return c

    def greet_row(k, c):
        pl.semaphore_signal(barrier, inc=1, device_id=((me_r + k) % rows_n, me_c), device_id_type=MESH)
        return c

    lax.fori_loop(1, cols_n, greet_col, 0)
    lax.fori_loop(1, rows_n, greet_row, 0)
    pl.semaphore_wait(barrier, cols_n - 1 + rows_n - 1)

    def lab_copy(d):
        return remote(lab_ref, labs.at[me_c], lab_s.at[d], lab_r.at[me_c], me_r, d)

    def lab_start(k, c):
        lab_copy((me_c + k) % cols_n).start()
        return c

    lax.fori_loop(1, cols_n, lab_start, 0)
    labs[me_c] = lab_ref[...]
    load.wait()

    def a_copy(d):
        return remote(sendb.at[d], recvb.at[me_c], a_s.at[d], a_r.at[me_c], me_r, d)

    for r in range(cap):
        recvb[me_c, r] = asm[idx_ref[me_c * cap + r]]

    def pack(k, c):
        d = (me_c + k) % cols_n
        for r in range(cap):
            sendb[d, r] = asm[idx_ref[d * cap + r]]

        @pl.when(k > 1)
        def _():
            a_copy((me_c + k - 1) % cols_n).start()
        return c

    lax.fori_loop(1, cols_n, pack, 0)
    a_copy((me_c + cols_n - 1) % cols_n).start()

    def lab_wait(k, c):
        s = (me_c + k) % cols_n
        remote(lab_ref, labs.at[s], lab_s.at[s], lab_r.at[s], me_r, s).wait_recv()
        return c

    lax.fori_loop(1, cols_n, lab_wait, 0)
    seen = labs[:, 0, :]
    lane = lax.broadcasted_iota(jnp.int32, seen.shape, 1) - me_c * cap
    code = lax.broadcasted_iota(jnp.int32, seen.shape, 0) * cap + lane
    code = jnp.where((lane >= 0) & (lane < cap), code, 0)
    valid = jnp.where((lane >= 0) & (lane < cap), seen, -1)

    def find(t, c):
        place[t] = jnp.minimum(jnp.sum(jnp.where(valid == t, code, 0)), cols_n * cap - 1)
        return c

    lax.fori_loop(0, row_tiles * CBLK, find, 0)

    def a_wait(k, c):
        s = (me_c + k) % cols_n
        remote(sendb.at[s], recvb.at[s], a_s.at[s], a_r.at[s], me_r, s).wait_recv()
        return c

    lax.fori_loop(1, cols_n, a_wait, 0)

    def put(i, c):
        rows = pl.ds(pl.multiple_of(i * NB, NB), NB)
        for m in range(CBLK):
            at = place[i * CBLK + m]
            s = at // cap
            r = at - s * cap
            re = recvb[s, r, 0]
            im = recvb[s, r, 1]
            mat[rows, m * NB:(m + 1) * NB] = re
            mat[rows, (CBLK + m) * NB:(CBLK + m + 1) * NB] = im
            if m == 0:
                pb[i, :, 0:NB] = re
                pb[i, :, NB:2 * NB] = im
        return c

    lax.fori_loop(0, row_tiles, put, 0)
    m_out = pltpu.make_async_copy(mat, m_hbm, out_sem.at[0])
    m_out.start()

    def sc_copy(b, d):
        return remote(pb.at[d], ag.at[b, d // nz, d % nz], sc_s.at[d], sc_r.at[b], me_r, d)

    for b in range(2):
        @pl.when(me_c == b)
        def _():
            def go(k, c):
                sc_copy(b, (b + k) % cols_n).start()
                return c
            lax.fori_loop(1, cols_n, go, 0)
            ag[b, b // nz, b % nz] = pb[b]

    def pick(d, c):
        def one(jj, c2):
            for k in range(2):
                r = piv_ref[k, d * sl + jj]
                tile = r // NB
                mine = (tile % rows_n) == me_r
                loc = tile // rows_n * NB + r % NB
                row = mat[pl.ds(loc, 1), :]
                pk[d, pl.ds(k * sl + jj, 1), :] = jnp.where(mine, row, 0.0)
            return c2
        return lax.fori_loop(0, sl, one, c)

    lax.fori_loop(0, rows_n, pick, 0)

    def rs_copy(d):
        return remote(pk.at[d], rb.at[me_r], rs_s.at[d], rs_r.at[me_r], d, me_c)

    def rs_start(k, c):
        rs_copy((me_r + k) % rows_n).start()
        return c

    lax.fori_loop(1, rows_n, rs_start, 0)

    def t_copy(s, d):
        rows = pl.ds(pl.multiple_of(d * sl, sl), sl)
        return remote(mat.at[rows, :], fin.at[d, pl.ds((2 + s) * sl, sl), :], t_s.at[d], t_r.at[s], d, me_c)

    for s in range(2):
        @pl.when(me_r == s)
        def _():
            def go(k, c):
                t_copy(s, (s + k) % rows_n).start()
                return c
            lax.fori_loop(1, rows_n, go, 0)
            fin[s, (2 + s) * sl:(3 + s) * sl, :] = mat[s * sl:(s + 1) * sl, :]

    def rs_wait(k, c):
        s = (me_r + k) % rows_n
        remote(pk.at[s], rb.at[s], rs_s.at[s], rs_r.at[s], s, me_c).wait_recv()
        return c

    lax.fori_loop(1, rows_n, rs_wait, 0)
    total = pk[me_r]

    def add(k, acc):
        return acc + rb[(me_r + k) % rows_n]

    fin[me_r, 0:2 * sl, :] = lax.fori_loop(1, rows_n, add, total)
    for s in range(2):
        @pl.when(me_r != s)
        def _():
            part = fin.at[me_r, pl.ds((2 + s) * sl, sl), :]
            remote(part, part, t_s.at[s], t_r.at[s], s, me_c).wait_recv()

    def y_copy(d):
        return remote(fin.at[me_r], fin.at[me_r], y_s.at[d], y_r.at[me_r], d, me_c)

    def y_start(k, c):
        y_copy((me_r + k) % rows_n).start()
        return c

    lax.fori_loop(1, rows_n, y_start, 0)

    def wb_copy(b, d):
        return remote(wfin.at[b, me_r], wfin.at[b, me_r], wb_s.at[d], wb_r.at[b], me_r, d)

    for b in range(2):
        @pl.when(me_c == b)
        def _():
            wfin[b, me_r, :, 0:NB] = fin[me_r, :, 0:NB]
            wfin[b, me_r, :, NB:2 * NB] = fin[me_r, :, CBLK * NB:(CBLK + 1) * NB]

            def go(k, c):
                wb_copy(b, (b + k) % cols_n).start()
                return c
            lax.fori_loop(1, cols_n, go, 0)

    for b in range(2):
        @pl.when(me_c != b)
        def _():
            part = ag.at[b, me_x, me_z]
            remote(part, part, sc_s.at[b], sc_r.at[b], me_r, b).wait_recv()

    lo = pl.ds(0, half)
    hi = pl.ds(half, half)

    def g1x(dx):
        part = ag.at[:, me_x, me_z, lo, :]
        return remote(part, part, g1_s.at[0, dx], g1_r.at[0, me_x], me_r, dx * nz + me_z)

    def g1z(dz):
        part = ag.at[:, me_x, me_z, hi, :]
        return remote(part, part, g1_s.at[1, dz], g1_r.at[1, me_z], me_r, me_x * nz + dz)

    def g2z(dz):
        part = ag.at[:, :, me_z, lo, :]
        return remote(part, part, g2_s.at[0, dz], g2_r.at[0, me_z], me_r, me_x * nz + dz)

    def g2x(dx):
        part = ag.at[:, me_x, :, hi, :]
        return remote(part, part, g2_s.at[1, dx], g2_r.at[1, me_x], me_r, dx * nz + me_z)

    for k in range(1, nx):
        g1x((me_x + k) % nx).start()
    for k in range(1, nz):
        g1z((me_z + k) % nz).start()

    for b in range(2):
        @pl.when(me_c != b)
        def _():
            part = wfin.at[b, me_r]
            remote(part, part, wb_s.at[b], wb_r.at[b], me_r, b).wait_recv()

    def wy_copy(d):
        part = wfin.at[:, me_r]
        return remote(part, part, wy_s.at[d], wy_r.at[me_r], d, me_c)

    def wy_start(k, c):
        wy_copy((me_r + k) % rows_n).start()
        return c

    lax.fori_loop(1, rows_n, wy_start, 0)

    for k in range(1, nx):
        sx = (me_x + k) % nx
        part = ag.at[:, sx, me_z, lo, :]
        remote(part, part, g1_s.at[0, sx], g1_r.at[0, sx], me_r, sx * nz + me_z).wait_recv()
    for k in range(1, nz):
        g2z((me_z + k) % nz).start()
    for k in range(1, nz):
        sz = (me_z + k) % nz
        part = ag.at[:, me_x, sz, hi, :]
        remote(part, part, g1_s.at[1, sz], g1_r.at[1, sz], me_r, me_x * nz + sz).wait_recv()
    for k in range(1, nx):
        g2x((me_x + k) % nx).start()

    def y_wait(k, c):
        s = (me_r + k) % rows_n
        part = fin.at[s]
        remote(part, part, y_s.at[s], y_r.at[s], s, me_c).wait_recv()
        part = wfin.at[:, s]
        remote(part, part, wy_s.at[s], wy_r.at[s], s, me_c).wait_recv()
        return c

    lax.fori_loop(1, rows_n, y_wait, 0)
    f_out = pltpu.make_async_copy(fin, fin_hbm, out_sem.at[1])
    f_out.start()
    w_out = pltpu.make_async_copy(wfin, wfin_hbm, out_sem.at[2])
    w_out.start()

    for k in range(1, nz):
        sz = (me_z + k) % nz
        part = ag.at[:, :, sz, lo, :]
        remote(part, part, g2_s.at[0, sz], g2_r.at[0, sz], me_r, me_x * nz + sz).wait_recv()
    for k in range(1, nx):
        sx = (me_x + k) % nx
        part = ag.at[:, sx, :, hi, :]
        remote(part, part, g2_s.at[1, sx], g2_r.at[1, sx], me_r, sx * nz + me_z).wait_recv()
    g_out = pltpu.make_async_copy(ag, ag_hbm, out_sem.at[3])
    g_out.start()

    def sent_col(k, c):
        d = (me_c + k) % cols_n
        lab_copy(d).wait_send()
        a_copy(d).wait_send()
        return c

    lax.fori_loop(1, cols_n, sent_col, 0)

    def sent_row(k, c):
        d = (me_r + k) % rows_n
        rs_copy(d).wait_send()
        y_copy(d).wait_send()
        wy_copy(d).wait_send()
        return c

    lax.fori_loop(1, rows_n, sent_row, 0)
    for b in range(2):
        @pl.when(me_c == b)
        def _():
            def go(k, c):
                d = (b + k) % cols_n
                sc_copy(b, d).wait_send()
                wb_copy(b, d).wait_send()
                return c
            lax.fori_loop(1, cols_n, go, 0)

        @pl.when(me_r == b)
        def _():
            def go(k, c):
                t_copy(b, (b + k) % rows_n).wait_send()
                return c
            lax.fori_loop(1, rows_n, go, 0)
    for k in range(1, nx):
        g1x((me_x + k) % nx).wait_send()
        g2x((me_x + k) % nx).wait_send()
    for k in range(1, nz):
        g1z((me_z + k) % nz).wait_send()
        g2z((me_z + k) % nz).wait_send()
    m_out.wait()
    f_out.wait()
    w_out.wait()
    g_out.wait()


def cmat(re, im):
    return jnp.concatenate([jnp.concatenate([re, im], 1), jnp.concatenate([-im, re], 1)], 0)


def dot(a, b):
    return jnp.dot(a, b, precision=HI, preferred_element_type=jnp.float32)


def per_device(dims, assembly, slot_tile, pivots, inverses):
    rows_n, nx, nz, cap, row_tiles = dims
    cols_n = nx * nz
    tiles = assembly[0]
    slots = tiles.shape[0]
    width_tiles = CBLK * cols_n
    ident = slot_tile[0]
    column_tile = ident % width_tiles
    target = column_tile % cols_n
    local_id = ident // width_tiles * CBLK + column_tile // cols_n
    num = jnp.arange(slots, dtype=jnp.int32)
    rank = jnp.sum(((target[:, None] == target[None, :]) & (num[None, :] < num[:, None])).astype(jnp.int32), axis=1)
    position = target * cap + rank
    hit = position[None, :] == jnp.arange(128, dtype=jnp.int32)[:, None]
    send_idx = jnp.sum(jnp.where(hit, num[None, :], 0), axis=1)
    labels = jnp.sum(jnp.where(hit, local_id[None, :] + 1, 0), axis=1) - 1
    labels = jnp.broadcast_to(labels[None, :], (8, 128))

    sl = NB // rows_n
    rows = row_tiles * NB
    wide = 2 * CBLK * NB
    f32 = jnp.float32
    dma = pltpu.SemaphoreType.DMA
    hbm = pl.BlockSpec(memory_space=pl.ANY)
    smem = pl.BlockSpec(memory_space=pltpu.SMEM)
    n = max(nx, nz)
    m_raw, ag, fin, wfin = pl.pallas_call(
        functools.partial(comm_kernel, dims),
        out_shape=(
            jax.ShapeDtypeStruct((rows, wide), f32),
            jax.ShapeDtypeStruct((2, nx, nz, NB, 2 * NB), f32),
            jax.ShapeDtypeStruct((rows_n, 4 * sl, wide), f32),
            jax.ShapeDtypeStruct((2, rows_n, 4 * sl, 2 * NB), f32),
        ),
        in_specs=[smem, smem, pl.BlockSpec(memory_space=pltpu.VMEM), hbm],
        out_specs=(hbm, hbm, hbm, hbm),
        scratch_shapes=[
            pltpu.VMEM((slots, 2, NB, NB), f32),
            pltpu.VMEM((cols_n, cap, 2, NB, NB), f32),
            pltpu.VMEM((cols_n, cap, 2, NB, NB), f32),
            pltpu.VMEM((cols_n, 8, 128), jnp.int32),
            pltpu.VMEM((rows, wide), f32),
            pltpu.VMEM((row_tiles, NB, 2 * NB), f32),
            pltpu.VMEM((2, nx, nz, NB, 2 * NB), f32),
            pltpu.VMEM((rows_n, 2 * sl, wide), f32),
            pltpu.VMEM((rows_n, 2 * sl, wide), f32),
            pltpu.VMEM((rows_n, 4 * sl, wide), f32),
            pltpu.VMEM((2, rows_n, 4 * sl, 2 * NB), f32),
            pltpu.SMEM((slots,), jnp.int32),
            dma((5,)),
            dma((cols_n,)), dma((cols_n,)),
            dma((cols_n,)), dma((cols_n,)),
            dma((cols_n,)), dma((2,)),
            dma((rows_n,)), dma((rows_n,)),
            dma((rows_n,)), dma((2,)),
            dma((rows_n,)), dma((rows_n,)),
            dma((cols_n,)), dma((2,)),
            dma((rows_n,)), dma((rows_n,)),
            dma((2, n)), dma((2, n)),
            dma((2, n)), dma((2, n)),
        ],
        compiler_params=pltpu.CompilerParams(
            collective_id=0, has_side_effects=True, vmem_limit_bytes=60 * 1024 * 1024),
        name="exchange",
    )(send_idx, pivots, labels, tiles)

    my_col = lax.axis_index("pcol")
    my_row = lax.axis_index("prow")
    sets = fin.reshape(rows_n, 4, sl, wide).transpose(1, 0, 2, 3).reshape(4, NB, wide)
    wsets = wfin.reshape(2, rows_n, 4, sl, 2 * NB).transpose(0, 2, 1, 3, 4).reshape(2, 4, NB, 2 * NB)
    wall = jnp.concatenate([sets, wsets[0], wsets[1]], -1)
    p0, p1, t0, t1 = wall[0], wall[1], wall[2], wall[3]
    i0 = cmat(inverses[0, 0], inverses[0, 1])
    i1 = cmat(inverses[1, 0], inverses[1, 1])

    def unpack(v):
        h = v.shape[1] // 2
        return cmat(v[:, :h], v[:, h:])

    both = (pivots[1][:, None] == pivots[0][None, :])
    e = both.astype(f32)
    p1 = jnp.where(jnp.any(both, 1)[:, None], dot(e, t0), p1)
    u0 = p0[:, :wide]
    u0b1 = p0[:, wide + 2 * NB:]
    l0p1 = dot(p1[:, wide:wide + 2 * NB], i0)
    u1 = p1[:, :wide] - dot(l0p1, unpack(u0))
    g = dot(dot(i0, unpack(u0b1)), i1)
    ru0, ru1 = unpack(u0), unpack(u1)
    h_lo = dot(i1, ru1)
    h_hi = dot(i0, ru0) - dot(g, ru1)
    col = jnp.arange(wide) % (CBLK * NB) // NB * cols_n + my_col
    is0 = col == 0
    is1 = col == 1

    def spreadc(v):
        pad = jnp.zeros((v.shape[0], NB), f32)
        return jnp.concatenate([v[:, :NB], pad, v[:, NB:], pad], 1)
    h_hi = jnp.where(is0[None, :], -spreadc(i0), jnp.where(is1[None, :], spreadc(g), h_hi))
    h_lo = jnp.where(is0[None, :], 0.0, jnp.where(is1[None, :], -spreadc(i1), h_lo))
    h = jnp.concatenate([h_hi, h_lo], 0)

    row_global = (jnp.arange(rows) // NB * rows_n + my_row) * NB + jnp.arange(rows) % NB
    hit0 = (row_global[:, None] == pivots[0][None, :]) & (row_global >= 2 * NB)[:, None]
    hit1 = (row_global[:, None] == pivots[1][None, :]) & (row_global >= 2 * NB)[:, None]
    in1 = jnp.any(hit1, 1)
    in0 = jnp.any(hit0, 1)
    hit0 = hit0 & ~in1[:, None]
    swap = dot(jnp.concatenate([hit0, hit1], 1).astype(f32), jnp.concatenate([t0, t1], 0))
    raw = jnp.concatenate([m_raw, ag[0].reshape(rows, 2 * NB), ag[1].reshape(rows, 2 * NB)], 1)
    z = jnp.where((in0 | in1)[:, None], swap, raw)
    out = jnp.where((is0 | is1)[None, :], 0.0, z[:, :wide]) - dot(z[:, wide:], h)
    row1 = jnp.where(is0[None, :], spreadc(l0p1), u1)
    top = jnp.where(my_row == 0, u0, jnp.where(my_row == 1, row1, out[:NB]))
    out = jnp.concatenate([top, out[NB:]], 0)
    return jnp.stack([out[:, :CBLK * NB], out[:, CBLK * NB:]])


def grid_of(cols_n):
    nx = 1
    while nx * nx < cols_n:
        nx *= 2
    return nx, cols_n // nx


def solution(mesh):
    rows_n, cols_n = mesh.shape["prow"], mesh.shape["pcol"]
    nx, nz = grid_of(cols_n)

    def body(assembly, slot_tile, pivots, inverses):
        slots = assembly.shape[1]
        cap = (slots + cols_n - 1) // cols_n + 1
        dims = (rows_n, nx, nz, cap, slots // CBLK)
        return per_device(dims, assembly, slot_tile, pivots, inverses)

    in_specs = (P("prow", "pcol", None, None, None), P("prow", "pcol"), P(), P())
    out_specs = P(None, "prow", "pcol")
    return jax.shard_map(body, mesh=mesh, in_specs=in_specs, out_specs=out_specs, check_vma=False)
```

```python
import functools

import jax
import jax.numpy as jnp
from jax import lax
from jax.experimental import pallas as pl
from jax.experimental.pallas import tpu as pltpu
from jax.sharding import PartitionSpec as P

CBLK = 2
NB = 128
MESH = pl.DeviceIdType.MESH
HI = lax.Precision.HIGHEST


def comm_kernel(
    dims, idx_ref, piv_ref, lab_ref, asm_hbm,
    m_hbm, ag_hbm, fin_hbm, wfin_hbm,
    asm, sendb, mid, recvb, labs, mat, pb, ag, pk, rb, fin, wfin, place,
    out_sem, lab_s, lab_r, a_s, a_r, b_s, b_r, sc_s, sc_r, rs_s, rs_r, t_s, t_r, y_s, y_r, wb_s, wb_r, wy_s, wy_r,
    g1_s, g1_r, g2_s, g2_r,
):
    rows_n, nx, nz, cap, row_tiles = dims
    cols_n = nx * nz
    sl = NB // rows_n
    half = NB // 2
    me_r = lax.axis_index("prow")
    me_c = lax.axis_index("pcol")
    me_x = me_c // nz
    me_z = me_c % nz

    def remote(src, dst, ssem, rsem, row, col):
        return pltpu.make_async_remote_copy(
            src_ref=src, dst_ref=dst, send_sem=ssem, recv_sem=rsem,
            device_id=(row, col), device_id_type=MESH)

    load = pltpu.make_async_copy(asm_hbm, asm, out_sem.at[4])
    load.start()

    barrier = pltpu.get_barrier_semaphore()

    def greet_col(k, c):
        pl.semaphore_signal(barrier, inc=1, device_id=(me_r, (me_c + k) % cols_n), device_id_type=MESH)
        return c

    def greet_row(k, c):
        pl.semaphore_signal(barrier, inc=1, device_id=((me_r + k) % rows_n, me_c), device_id_type=MESH)
        return c

    lax.fori_loop(1, cols_n, greet_col, 0)
    lax.fori_loop(1, rows_n, greet_row, 0)
    pl.semaphore_wait(barrier, cols_n - 1 + rows_n - 1)

    def lab_copy(d):
        return remote(lab_ref, labs.at[me_c], lab_s.at[d], lab_r.at[me_c], me_r, d)

    def lab_start(k, c):
        lab_copy((me_c + k) % cols_n).start()
        return c

    lax.fori_loop(1, cols_n, lab_start, 0)
    labs[me_c] = lab_ref[...]
    load.wait()

    def first_hop(c, d):
        dx, dz = d // nz, d % nz
        if c == 0:
            return remote(sendb.at[0, d], mid.at[0, me_x * nz + dz], a_s.at[0, d], b_r.at[0, me_x * nz + dz],
                          me_r, dx * nz + me_z)
        return remote(sendb.at[1, d], mid.at[1, dx * nz + me_z], a_s.at[1, d], b_r.at[1, dx * nz + me_z],
                      me_r, me_x * nz + dz)

    def direct(c, d):
        return remote(sendb.at[c, d], recvb.at[c, me_c], a_s.at[c, d], a_r.at[c, me_c], me_r, d)

    def relay_in(c, dx, dz):
        if c == 0:
            sx = (me_x + nx - dx) % nx
            at = sx * nz + (me_z + dz) % nz
            return remote(sendb.at[0, at], mid.at[0, at], b_s.at[0, at], b_r.at[0, at], me_r, sx * nz + me_z)
        sz = (me_z + nz - dz) % nz
        at = (me_x + dx) % nx * nz + sz
        return remote(sendb.at[1, at], mid.at[1, at], b_s.at[1, at], b_r.at[1, at], me_r, me_x * nz + sz)

    def relay_out(c, dx, dz):
        if c == 0:
            sx = (me_x + nx - dx) % nx
            tz = (me_z + dz) % nz
            at = sx * nz + tz
            src = sx * nz + me_z
            return remote(mid.at[0, at], recvb.at[0, src], b_s.at[0, at], a_r.at[0, src], me_r, me_x * nz + tz)
        sz = (me_z + nz - dz) % nz
        tx = (me_x + dx) % nx
        at = tx * nz + sz
        src = me_x * nz + sz
        return remote(mid.at[1, at], recvb.at[1, src], b_s.at[1, at], a_r.at[1, src], me_r, tx * nz + me_z)

    def offset(k):
        return k % (nx - 1) + 1, k // (nx - 1) + 1

    def peer(dx, dz):
        return (me_x + dx) % nx * nz + (me_z + dz) % nz

    def pack_to(dst, d, e):
        for r in range(cap):
            t = idx_ref[d * cap + r]
            for c in range(2):
                dst[c, e, r] = asm[t, c]

    def pack(k, c0):
        d = peer(*offset(k))
        pack_to(sendb, d, d)

        @pl.when(k > 0)
        def _():
            p = peer(*offset(jnp.maximum(k - 1, 0)))
            first_hop(0, p).start()
            first_hop(1, p).start()
        return c0

    relays = (nx - 1) * (nz - 1)
    lax.fori_loop(0, relays, pack, 0)
    axis_peers = [(dx, 0) for dx in range(1, nx)] + [(0, dz) for dz in range(1, nz)]
    for n, (dx, dz) in enumerate(axis_peers):
        d = peer(dx, dz)
        pack_to(sendb, d, d)
        if n == 0:
            p = peer(*offset(relays - 1))
            first_hop(0, p).start()
            first_hop(1, p).start()
        else:
            p = peer(*axis_peers[n - 1])
            direct(0, p).start()
            direct(1, p).start()
    pack_to(recvb, me_c, me_c)
    direct(0, peer(*axis_peers[-1])).start()
    direct(1, peer(*axis_peers[-1])).start()

    def relay(k, c0):
        dx, dz = offset(k)
        for c in range(2):
            relay_in(c, dx, dz).wait_recv()
            relay_out(c, dx, dz).start()
        return c0

    lax.fori_loop(0, relays, relay, 0)

    def lab_wait(k, c):
        s = (me_c + k) % cols_n
        remote(lab_ref, labs.at[s], lab_s.at[s], lab_r.at[s], me_r, s).wait_recv()
        return c

    lax.fori_loop(1, cols_n, lab_wait, 0)
    seen = labs[:, 0, :]
    lane = lax.broadcasted_iota(jnp.int32, seen.shape, 1) - me_c * cap
    code = lax.broadcasted_iota(jnp.int32, seen.shape, 0) * cap + lane
    code = jnp.where((lane >= 0) & (lane < cap), code, 0)
    valid = jnp.where((lane >= 0) & (lane < cap), seen, -1)

    def find(t, c):
        place[t] = jnp.minimum(jnp.sum(jnp.where(valid == t, code, 0)), cols_n * cap - 1)
        return c

    lax.fori_loop(0, row_tiles * CBLK, find, 0)

    def a_wait(k, c):
        s = (me_c + k) % cols_n
        for h in range(2):
            remote(sendb.at[h, s], recvb.at[h, s], a_s.at[h, s], a_r.at[h, s], me_r, s).wait_recv()
        return c

    lax.fori_loop(1, cols_n, a_wait, 0)

    def put(i, c):
        rows = pl.ds(pl.multiple_of(i * NB, NB), NB)
        for m in range(CBLK):
            at = place[i * CBLK + m]
            s = at // cap
            r = at - s * cap
            re = recvb[0, s, r]
            im = recvb[1, s, r]
            mat[rows, m * NB:(m + 1) * NB] = re
            mat[rows, (CBLK + m) * NB:(CBLK + m + 1) * NB] = im
            if m == 0:
                pb[i, :, 0:NB] = re
                pb[i, :, NB:2 * NB] = im
        return c

    lax.fori_loop(0, row_tiles, put, 0)
    m_out = pltpu.make_async_copy(mat, m_hbm, out_sem.at[0])
    m_out.start()

    def sc_copy(b, d):
        return remote(pb.at[d], ag.at[b, d // nz, d % nz], sc_s.at[d], sc_r.at[b], me_r, d)

    for b in range(2):
        @pl.when(me_c == b)
        def _():
            def go(k, c):
                sc_copy(b, (b + k) % cols_n).start()
                return c
            lax.fori_loop(1, cols_n, go, 0)
            ag[b, b // nz, b % nz] = pb[b]

    def pick(d, c):
        def one(jj, c2):
            for k in range(2):
                r = piv_ref[k, d * sl + jj]
                tile = r // NB
                mine = (tile % rows_n) == me_r
                loc = tile // rows_n * NB + r % NB
                row = mat[pl.ds(loc, 1), :]
                pk[d, pl.ds(k * sl + jj, 1), :] = jnp.where(mine, row, 0.0)
            return c2
        return lax.fori_loop(0, sl, one, c)

    lax.fori_loop(0, rows_n, pick, 0)

    def rs_copy(d):
        return remote(pk.at[d], rb.at[me_r], rs_s.at[d], rs_r.at[me_r], d, me_c)

    def rs_start(k, c):
        rs_copy((me_r + k) % rows_n).start()
        return c

    lax.fori_loop(1, rows_n, rs_start, 0)

    def t_copy(s, d):
        rows = pl.ds(pl.multiple_of(d * sl, sl), sl)
        return remote(mat.at[rows, :], fin.at[d, pl.ds((2 + s) * sl, sl), :], t_s.at[d], t_r.at[s], d, me_c)

    for s in range(2):
        @pl.when(me_r == s)
        def _():
            def go(k, c):
                t_copy(s, (s + k) % rows_n).start()
                return c
            lax.fori_loop(1, rows_n, go, 0)
            fin[s, (2 + s) * sl:(3 + s) * sl, :] = mat[s * sl:(s + 1) * sl, :]

    def rs_wait(k, c):
        s = (me_r + k) % rows_n
        remote(pk.at[s], rb.at[s], rs_s.at[s], rs_r.at[s], s, me_c).wait_recv()
        return c

    lax.fori_loop(1, rows_n, rs_wait, 0)
    total = pk[me_r]

    def add(k, acc):
        return acc + rb[(me_r + k) % rows_n]

    fin[me_r, 0:2 * sl, :] = lax.fori_loop(1, rows_n, add, total)
    for s in range(2):
        @pl.when(me_r != s)
        def _():
            part = fin.at[me_r, pl.ds((2 + s) * sl, sl), :]
            remote(part, part, t_s.at[s], t_r.at[s], s, me_c).wait_recv()

    def y_copy(d):
        return remote(fin.at[me_r], fin.at[me_r], y_s.at[d], y_r.at[me_r], d, me_c)

    def y_start(k, c):
        y_copy((me_r + k) % rows_n).start()
        return c

    lax.fori_loop(1, rows_n, y_start, 0)

    def wb_copy(b, d):
        return remote(wfin.at[b, me_r], wfin.at[b, me_r], wb_s.at[d], wb_r.at[b], me_r, d)

    for b in range(2):
        @pl.when(me_c == b)
        def _():
            wfin[b, me_r, :, 0:NB] = fin[me_r, :, 0:NB]
            wfin[b, me_r, :, NB:2 * NB] = fin[me_r, :, CBLK * NB:(CBLK + 1) * NB]

            def go(k, c):
                wb_copy(b, (b + k) % cols_n).start()
                return c
            lax.fori_loop(1, cols_n, go, 0)

    for b in range(2):
        @pl.when(me_c != b)
        def _():
            part = ag.at[b, me_x, me_z]
            remote(part, part, sc_s.at[b], sc_r.at[b], me_r, b).wait_recv()

    lo = pl.ds(0, half)
    hi = pl.ds(half, half)

    def g1x(dx):
        part = ag.at[:, me_x, me_z, lo, :]
        return remote(part, part, g1_s.at[0, dx], g1_r.at[0, me_x], me_r, dx * nz + me_z)

    def g1z(dz):
        part = ag.at[:, me_x, me_z, hi, :]
        return remote(part, part, g1_s.at[1, dz], g1_r.at[1, me_z], me_r, me_x * nz + dz)

    def g2z(dz):
        part = ag.at[:, :, me_z, lo, :]
        return remote(part, part, g2_s.at[0, dz], g2_r.at[0, me_z], me_r, me_x * nz + dz)

    def g2x(dx):
        part = ag.at[:, me_x, :, hi, :]
        return remote(part, part, g2_s.at[1, dx], g2_r.at[1, me_x], me_r, dx * nz + me_z)

    for k in range(1, nx):
        g1x((me_x + k) % nx).start()
    for k in range(1, nz):
        g1z((me_z + k) % nz).start()

    for b in range(2):
        @pl.when(me_c != b)
        def _():
            part = wfin.at[b, me_r]
            remote(part, part, wb_s.at[b], wb_r.at[b], me_r, b).wait_recv()

    def wy_copy(d):
        part = wfin.at[:, me_r]
        return remote(part, part, wy_s.at[d], wy_r.at[me_r], d, me_c)

    def wy_start(k, c):
        wy_copy((me_r + k) % rows_n).start()
        return c

    lax.fori_loop(1, rows_n, wy_start, 0)

    for k in range(1, nx):
        sx = (me_x + k) % nx
        part = ag.at[:, sx, me_z, lo, :]
        remote(part, part, g1_s.at[0, sx], g1_r.at[0, sx], me_r, sx * nz + me_z).wait_recv()
    for k in range(1, nz):
        g2z((me_z + k) % nz).start()
    for k in range(1, nz):
        sz = (me_z + k) % nz
        part = ag.at[:, me_x, sz, hi, :]
        remote(part, part, g1_s.at[1, sz], g1_r.at[1, sz], me_r, me_x * nz + sz).wait_recv()
    for k in range(1, nx):
        g2x((me_x + k) % nx).start()

    def y_wait(k, c):
        s = (me_r + k) % rows_n
        part = fin.at[s]
        remote(part, part, y_s.at[s], y_r.at[s], s, me_c).wait_recv()
        part = wfin.at[:, s]
        remote(part, part, wy_s.at[s], wy_r.at[s], s, me_c).wait_recv()
        return c

    lax.fori_loop(1, rows_n, y_wait, 0)
    f_out = pltpu.make_async_copy(fin, fin_hbm, out_sem.at[1])
    f_out.start()
    w_out = pltpu.make_async_copy(wfin, wfin_hbm, out_sem.at[2])
    w_out.start()

    for k in range(1, nz):
        sz = (me_z + k) % nz
        part = ag.at[:, :, sz, lo, :]
        remote(part, part, g2_s.at[0, sz], g2_r.at[0, sz], me_r, me_x * nz + sz).wait_recv()
    for k in range(1, nx):
        sx = (me_x + k) % nx
        part = ag.at[:, sx, :, hi, :]
        remote(part, part, g2_s.at[1, sx], g2_r.at[1, sx], me_r, sx * nz + me_z).wait_recv()
    g_out = pltpu.make_async_copy(ag, ag_hbm, out_sem.at[3])
    g_out.start()

    def sent_col(k, c):
        d = (me_c + k) % cols_n
        lab_copy(d).wait_send()
        direct(0, d).wait_send()
        direct(1, d).wait_send()
        return c

    lax.fori_loop(1, cols_n, sent_col, 0)

    def sent_relay(k, c0):
        for c in range(2):
            relay_out(c, *offset(k)).wait_send()
        return c0

    lax.fori_loop(0, relays, sent_relay, 0)

    def sent_row(k, c):
        d = (me_r + k) % rows_n
        rs_copy(d).wait_send()
        y_copy(d).wait_send()
        wy_copy(d).wait_send()
        return c

    lax.fori_loop(1, rows_n, sent_row, 0)
    for b in range(2):
        @pl.when(me_c == b)
        def _():
            def go(k, c):
                d = (b + k) % cols_n
                sc_copy(b, d).wait_send()
                wb_copy(b, d).wait_send()
                return c
            lax.fori_loop(1, cols_n, go, 0)

        @pl.when(me_r == b)
        def _():
            def go(k, c):
                t_copy(b, (b + k) % rows_n).wait_send()
                return c
            lax.fori_loop(1, rows_n, go, 0)
    for k in range(1, nx):
        g1x((me_x + k) % nx).wait_send()
        g2x((me_x + k) % nx).wait_send()
    for k in range(1, nz):
        g1z((me_z + k) % nz).wait_send()
        g2z((me_z + k) % nz).wait_send()
    m_out.wait()
    f_out.wait()
    w_out.wait()
    g_out.wait()


def cmat(re, im):
    return jnp.concatenate([jnp.concatenate([re, im], 1), jnp.concatenate([-im, re], 1)], 0)


def dot(a, b):
    return jnp.dot(a, b, precision=HI, preferred_element_type=jnp.float32)


def per_device(dims, assembly, slot_tile, pivots, inverses):
    rows_n, nx, nz, cap, row_tiles = dims
    cols_n = nx * nz
    tiles = assembly[0]
    slots = tiles.shape[0]
    width_tiles = CBLK * cols_n
    ident = slot_tile[0]
    column_tile = ident % width_tiles
    target = column_tile % cols_n
    local_id = ident // width_tiles * CBLK + column_tile // cols_n
    num = jnp.arange(slots, dtype=jnp.int32)
    rank = jnp.sum(((target[:, None] == target[None, :]) & (num[None, :] < num[:, None])).astype(jnp.int32), axis=1)
    position = target * cap + rank
    hit = position[None, :] == jnp.arange(128, dtype=jnp.int32)[:, None]
    send_idx = jnp.sum(jnp.where(hit, num[None, :], 0), axis=1)
    labels = jnp.sum(jnp.where(hit, local_id[None, :] + 1, 0), axis=1) - 1
    labels = jnp.broadcast_to(labels[None, :], (8, 128))

    sl = NB // rows_n
    rows = row_tiles * NB
    wide = 2 * CBLK * NB
    f32 = jnp.float32
    dma = pltpu.SemaphoreType.DMA
    hbm = pl.BlockSpec(memory_space=pl.ANY)
    smem = pl.BlockSpec(memory_space=pltpu.SMEM)
    n = max(nx, nz)
    m_raw, ag, fin, wfin = pl.pallas_call(
        functools.partial(comm_kernel, dims),
        out_shape=(
            jax.ShapeDtypeStruct((rows, wide), f32),
            jax.ShapeDtypeStruct((2, nx, nz, NB, 2 * NB), f32),
            jax.ShapeDtypeStruct((rows_n, 4 * sl, wide), f32),
            jax.ShapeDtypeStruct((2, rows_n, 4 * sl, 2 * NB), f32),
        ),
        in_specs=[smem, smem, pl.BlockSpec(memory_space=pltpu.VMEM), hbm],
        out_specs=(hbm, hbm, hbm, hbm),
        scratch_shapes=[
            pltpu.VMEM((slots, 2, NB, NB), f32),
            pltpu.VMEM((2, cols_n, cap, NB, NB), f32),
            pltpu.VMEM((2, cols_n, cap, NB, NB), f32),
            pltpu.VMEM((2, cols_n, cap, NB, NB), f32),
            pltpu.VMEM((cols_n, 8, 128), jnp.int32),
            pltpu.VMEM((rows, wide), f32),
            pltpu.VMEM((row_tiles, NB, 2 * NB), f32),
            pltpu.VMEM((2, nx, nz, NB, 2 * NB), f32),
            pltpu.VMEM((rows_n, 2 * sl, wide), f32),
            pltpu.VMEM((rows_n, 2 * sl, wide), f32),
            pltpu.VMEM((rows_n, 4 * sl, wide), f32),
            pltpu.VMEM((2, rows_n, 4 * sl, 2 * NB), f32),
            pltpu.SMEM((slots,), jnp.int32),
            dma((5,)),
            dma((cols_n,)), dma((cols_n,)),
            dma((2, cols_n)), dma((2, cols_n)),
            dma((2, cols_n)), dma((2, cols_n)),
            dma((cols_n,)), dma((2,)),
            dma((rows_n,)), dma((rows_n,)),
            dma((rows_n,)), dma((2,)),
            dma((rows_n,)), dma((rows_n,)),
            dma((cols_n,)), dma((2,)),
            dma((rows_n,)), dma((rows_n,)),
            dma((2, n)), dma((2, n)),
            dma((2, n)), dma((2, n)),
        ],
        compiler_params=pltpu.CompilerParams(
            collective_id=0, has_side_effects=True, vmem_limit_bytes=60 * 1024 * 1024),
        name="exchange",
    )(send_idx, pivots, labels, tiles)

    my_col = lax.axis_index("pcol")
    my_row = lax.axis_index("prow")
    sets = fin.reshape(rows_n, 4, sl, wide).transpose(1, 0, 2, 3).reshape(4, NB, wide)
    wsets = wfin.reshape(2, rows_n, 4, sl, 2 * NB).transpose(0, 2, 1, 3, 4).reshape(2, 4, NB, 2 * NB)
    wall = jnp.concatenate([sets, wsets[0], wsets[1]], -1)
    p0, p1, t0, t1 = wall[0], wall[1], wall[2], wall[3]
    i0 = cmat(inverses[0, 0], inverses[0, 1])
    i1 = cmat(inverses[1, 0], inverses[1, 1])

    def unpack(v):
        h = v.shape[1] // 2
        return cmat(v[:, :h], v[:, h:])

    both = (pivots[1][:, None] == pivots[0][None, :])
    e = both.astype(f32)
    p1 = jnp.where(jnp.any(both, 1)[:, None], dot(e, t0), p1)
    u0 = p0[:, :wide]
    u0b1 = p0[:, wide + 2 * NB:]
    l0p1 = dot(p1[:, wide:wide + 2 * NB], i0)
    u1 = p1[:, :wide] - dot(l0p1, unpack(u0))
    g = dot(dot(i0, unpack(u0b1)), i1)
    ru0, ru1 = unpack(u0), unpack(u1)
    h_lo = dot(i1, ru1)
    h_hi = dot(i0, ru0) - dot(g, ru1)
    col = jnp.arange(wide) % (CBLK * NB) // NB * cols_n + my_col
    is0 = col == 0
    is1 = col == 1

    def spreadc(v):
        pad = jnp.zeros((v.shape[0], NB), f32)
        return jnp.concatenate([v[:, :NB], pad, v[:, NB:], pad], 1)
    h_hi = jnp.where(is0[None, :], -spreadc(i0), jnp.where(is1[None, :], spreadc(g), h_hi))
    h_lo = jnp.where(is0[None, :], 0.0, jnp.where(is1[None, :], -spreadc(i1), h_lo))
    h = jnp.concatenate([h_hi, h_lo], 0)

    row_global = (jnp.arange(rows) // NB * rows_n + my_row) * NB + jnp.arange(rows) % NB
    hit0 = (row_global[:, None] == pivots[0][None, :]) & (row_global >= 2 * NB)[:, None]
    hit1 = (row_global[:, None] == pivots[1][None, :]) & (row_global >= 2 * NB)[:, None]
    in1 = jnp.any(hit1, 1)
    in0 = jnp.any(hit0, 1)
    hit0 = hit0 & ~in1[:, None]
    swap = dot(jnp.concatenate([hit0, hit1], 1).astype(f32), jnp.concatenate([t0, t1], 0))
    raw = jnp.concatenate([m_raw, ag[0].reshape(rows, 2 * NB), ag[1].reshape(rows, 2 * NB)], 1)
    z = jnp.where((in0 | in1)[:, None], swap, raw)
    out = jnp.where((is0 | is1)[None, :], 0.0, z[:, :wide]) - dot(z[:, wide:], h)
    row1 = jnp.where(is0[None, :], spreadc(l0p1), u1)
    top = jnp.where(my_row == 0, u0, jnp.where(my_row == 1, row1, out[:NB]))
    out = jnp.concatenate([top, out[NB:]], 0)
    return jnp.stack([out[:, :CBLK * NB], out[:, CBLK * NB:]])


def grid_of(cols_n):
    nx = 1
    while nx * nx < cols_n:
        nx *= 2
    return nx, cols_n // nx


def solution(mesh):
    rows_n, cols_n = mesh.shape["prow"], mesh.shape["pcol"]
    nx, nz = grid_of(cols_n)

    def body(assembly, slot_tile, pivots, inverses):
        slots = assembly.shape[1]
        cap = (slots + cols_n - 1) // cols_n + 1
        dims = (rows_n, nx, nz, cap, slots // CBLK)
        return per_device(dims, assembly, slot_tile, pivots, inverses)

    in_specs = (P("prow", "pcol", None, None, None), P("prow", "pcol"), P(), P())
    out_specs = P(None, "prow", "pcol")
    return jax.shard_map(body, mesh=mesh, in_specs=in_specs, out_specs=out_specs, check_vma=False)
```

```python
import functools

import jax
import jax.numpy as jnp
from jax import lax
from jax.experimental import pallas as pl
from jax.experimental.pallas import tpu as pltpu
from jax.sharding import PartitionSpec as P

CBLK = 2
NB = 128
MESH = pl.DeviceIdType.MESH
HI = lax.Precision.HIGHEST


def comm_kernel(
    dims, idx_ref, piv_ref, lab_ref, asm_hbm,
    m_hbm, ag_hbm, fin_hbm, wfin_hbm,
    asm, sendb, mid, recvb, labs, mat, pb, ag, pk, rb, fin, wfin, place,
    out_sem, lab_s, lab_r, a_s, a_r, b_s, b_r, sc_s, sc_r, rs_s, rs_r, t_s, t_r, y_s, y_r, wb_s, wb_r, wy_s, wy_r,
    g1_s, g1_r, g2_s, g2_r,
):
    rows_n, nx, nz, cap, row_tiles = dims
    cols_n = nx * nz
    sl = NB // rows_n
    half = NB // 2
    me_r = lax.axis_index("prow")
    me_c = lax.axis_index("pcol")
    me_x = me_c // nz
    me_z = me_c % nz

    def remote(src, dst, ssem, rsem, row, col):
        return pltpu.make_async_remote_copy(
            src_ref=src, dst_ref=dst, send_sem=ssem, recv_sem=rsem,
            device_id=(row, col), device_id_type=MESH)

    load = pltpu.make_async_copy(asm_hbm, asm, out_sem.at[4])
    load.start()

    barrier = pltpu.get_barrier_semaphore()

    def greet_col(k, c):
        pl.semaphore_signal(barrier, inc=1, device_id=(me_r, (me_c + k) % cols_n), device_id_type=MESH)
        return c

    def greet_row(k, c):
        pl.semaphore_signal(barrier, inc=1, device_id=((me_r + k) % rows_n, me_c), device_id_type=MESH)
        return c

    lax.fori_loop(1, cols_n, greet_col, 0)
    lax.fori_loop(1, rows_n, greet_row, 0)
    pl.semaphore_wait(barrier, cols_n - 1 + rows_n - 1)

    def lab_copy(d):
        return remote(lab_ref, labs.at[me_c], lab_s.at[d], lab_r.at[me_c], me_r, d)

    def lab_start(k, c):
        lab_copy((me_c + k) % cols_n).start()
        return c

    lax.fori_loop(1, cols_n, lab_start, 0)
    labs[me_c] = lab_ref[...]
    load.wait()

    def first_hop(c, d):
        dx, dz = d // nz, d % nz
        if c == 0:
            return remote(sendb.at[0, d], mid.at[0, me_x * nz + dz], a_s.at[0, d], b_r.at[0, me_x * nz + dz],
                          me_r, dx * nz + me_z)
        return remote(sendb.at[1, d], mid.at[1, dx * nz + me_z], a_s.at[1, d], b_r.at[1, dx * nz + me_z],
                      me_r, me_x * nz + dz)

    def direct(c, d):
        return remote(sendb.at[c, d], recvb.at[c, me_c], a_s.at[c, d], a_r.at[c, me_c], me_r, d)

    def relay_in(c, dx, dz):
        if c == 0:
            sx = (me_x + nx - dx) % nx
            at = sx * nz + (me_z + dz) % nz
            return remote(sendb.at[0, at], mid.at[0, at], b_s.at[0, at], b_r.at[0, at], me_r, sx * nz + me_z)
        sz = (me_z + nz - dz) % nz
        at = (me_x + dx) % nx * nz + sz
        return remote(sendb.at[1, at], mid.at[1, at], b_s.at[1, at], b_r.at[1, at], me_r, me_x * nz + sz)

    def relay_out(c, dx, dz):
        if c == 0:
            sx = (me_x + nx - dx) % nx
            tz = (me_z + dz) % nz
            at = sx * nz + tz
            src = sx * nz + me_z
            return remote(mid.at[0, at], recvb.at[0, src], b_s.at[0, at], a_r.at[0, src], me_r, me_x * nz + tz)
        sz = (me_z + nz - dz) % nz
        tx = (me_x + dx) % nx
        at = tx * nz + sz
        src = me_x * nz + sz
        return remote(mid.at[1, at], recvb.at[1, src], b_s.at[1, at], a_r.at[1, src], me_r, tx * nz + me_z)

    def offset(k):
        return k % (nx - 1) + 1, k // (nx - 1) + 1

    def peer(dx, dz):
        return (me_x + dx) % nx * nz + (me_z + dz) % nz

    def pack_to(dst, d, e):
        for r in range(cap):
            t = idx_ref[d * cap + r]
            for c in range(2):
                dst[c, e, r] = asm[t, c]

    def pack(k, c0):
        d = peer(*offset(k))
        pack_to(sendb, d, d)

        @pl.when(k > 0)
        def _():
            p = peer(*offset(jnp.maximum(k - 1, 0)))
            first_hop(0, p).start()
            first_hop(1, p).start()
        return c0

    relays = (nx - 1) * (nz - 1)
    lax.fori_loop(0, relays, pack, 0)
    axis_peers = [(dx, 0) for dx in range(1, nx)] + [(0, dz) for dz in range(1, nz)]
    for n, (dx, dz) in enumerate(axis_peers):
        d = peer(dx, dz)
        pack_to(sendb, d, d)
        if n == 0:
            p = peer(*offset(relays - 1))
            first_hop(0, p).start()
            first_hop(1, p).start()
        else:
            p = peer(*axis_peers[n - 1])
            direct(0, p).start()
            direct(1, p).start()
    pack_to(recvb, me_c, me_c)
    direct(0, peer(*axis_peers[-1])).start()
    direct(1, peer(*axis_peers[-1])).start()

    def relay(k, c0):
        dx, dz = offset(k)
        for c in range(2):
            relay_in(c, dx, dz).wait_recv()
            relay_out(c, dx, dz).start()
        return c0

    lax.fori_loop(0, relays, relay, 0)

    def lab_wait(k, c):
        s = (me_c + k) % cols_n
        remote(lab_ref, labs.at[s], lab_s.at[s], lab_r.at[s], me_r, s).wait_recv()
        return c

    lax.fori_loop(1, cols_n, lab_wait, 0)
    seen = labs[:, 0, :]
    lane = lax.broadcasted_iota(jnp.int32, seen.shape, 1) - me_c * cap
    code = lax.broadcasted_iota(jnp.int32, seen.shape, 0) * cap + lane
    code = jnp.where((lane >= 0) & (lane < cap), code, 0)
    valid = jnp.where((lane >= 0) & (lane < cap), seen, -1)

    def find(t, c):
        place[t] = jnp.minimum(jnp.sum(jnp.where(valid == t, code, 0)), cols_n * cap - 1)
        return c

    lax.fori_loop(0, row_tiles * CBLK, find, 0)

    def a_wait(k, c):
        s = (me_c + k) % cols_n
        for h in range(2):
            remote(sendb.at[h, s], recvb.at[h, s], a_s.at[h, s], a_r.at[h, s], me_r, s).wait_recv()
        return c

    lax.fori_loop(1, cols_n, a_wait, 0)

    def put(i, c):
        rows = pl.ds(pl.multiple_of(i * NB, NB), NB)
        for m in range(CBLK):
            at = place[i * CBLK + m]
            s = at // cap
            r = at - s * cap
            re = recvb[0, s, r]
            im = recvb[1, s, r]
            mat[rows, m * NB:(m + 1) * NB] = re
            mat[rows, (CBLK + m) * NB:(CBLK + m + 1) * NB] = im
            if m == 0:
                pb[i, :, 0:NB] = re
                pb[i, :, NB:2 * NB] = im
        return c

    lax.fori_loop(0, row_tiles, put, 0)
    m_out = pltpu.make_async_copy(mat, m_hbm, out_sem.at[0])
    m_out.start()

    def sc_copy(b, d):
        return remote(pb.at[d], ag.at[b, d // nz, d % nz], sc_s.at[d], sc_r.at[b], me_r, d)

    for b in range(2):
        @pl.when(me_c == b)
        def _():
            def go(k, c):
                sc_copy(b, (b + k) % cols_n).start()
                return c
            lax.fori_loop(1, cols_n, go, 0)
            ag[b, b // nz, b % nz] = pb[b]

    def pick(d, c):
        def one(jj, c2):
            for k in range(2):
                r = piv_ref[k, d * sl + jj]
                tile = r // NB
                mine = (tile % rows_n) == me_r
                loc = tile // rows_n * NB + r % NB
                row = mat[pl.ds(loc, 1), :]
                pk[d, pl.ds(k * sl + jj, 1), :] = jnp.where(mine, row, 0.0)
            return c2
        return lax.fori_loop(0, sl, one, c)

    lax.fori_loop(0, rows_n, pick, 0)

    def rs_copy(d):
        return remote(pk.at[d], rb.at[me_r], rs_s.at[d], rs_r.at[me_r], d, me_c)

    def rs_start(k, c):
        rs_copy((me_r + k) % rows_n).start()
        return c

    lax.fori_loop(1, rows_n, rs_start, 0)

    def t_copy(s, d):
        rows = pl.ds(pl.multiple_of(d * sl, sl), sl)
        return remote(mat.at[rows, :], fin.at[2 + s, rows, :], t_s.at[d], t_r.at[s], d, me_c)

    for s in range(2):
        @pl.when(me_r == s)
        def _():
            def go(k, c):
                t_copy(s, (s + k) % rows_n).start()
                return c
            lax.fori_loop(1, rows_n, go, 0)
            fin[2 + s, s * sl:(s + 1) * sl, :] = mat[s * sl:(s + 1) * sl, :]

    def rs_wait(k, c):
        s = (me_r + k) % rows_n
        remote(pk.at[s], rb.at[s], rs_s.at[s], rs_r.at[s], s, me_c).wait_recv()
        return c

    lax.fori_loop(1, rows_n, rs_wait, 0)
    total = pk[me_r]

    def add(k, acc):
        return acc + rb[(me_r + k) % rows_n]

    total = lax.fori_loop(1, rows_n, add, total)
    mine_rows = pl.ds(pl.multiple_of(me_r * sl, sl), sl)
    fin[0, mine_rows, :] = total[:sl]
    fin[1, mine_rows, :] = total[sl:]
    for s in range(2):
        @pl.when(me_r != s)
        def _():
            part = fin.at[2 + s, mine_rows, :]
            remote(part, part, t_s.at[s], t_r.at[s], s, me_c).wait_recv()

    def y_copy(d):
        part = fin.at[:, mine_rows, :]
        return remote(part, part, y_s.at[d], y_r.at[me_r], d, me_c)

    def y_start(k, c):
        y_copy((me_r + k) % rows_n).start()
        return c

    lax.fori_loop(1, rows_n, y_start, 0)

    def wb_copy(b, d):
        part = wfin.at[b, :, mine_rows, :]
        return remote(part, part, wb_s.at[d], wb_r.at[b], me_r, d)

    for b in range(2):
        @pl.when(me_c == b)
        def _():
            wfin[b, :, mine_rows, 0:NB] = fin[:, mine_rows, 0:NB]
            wfin[b, :, mine_rows, NB:2 * NB] = fin[:, mine_rows, CBLK * NB:(CBLK + 1) * NB]

            def go(k, c):
                wb_copy(b, (b + k) % cols_n).start()
                return c
            lax.fori_loop(1, cols_n, go, 0)

    for b in range(2):
        @pl.when(me_c != b)
        def _():
            part = ag.at[b, me_x, me_z]
            remote(part, part, sc_s.at[b], sc_r.at[b], me_r, b).wait_recv()

    lo = pl.ds(0, half)
    hi = pl.ds(half, half)

    def g1x(dx):
        part = ag.at[:, me_x, me_z, lo, :]
        return remote(part, part, g1_s.at[0, dx], g1_r.at[0, me_x], me_r, dx * nz + me_z)

    def g1z(dz):
        part = ag.at[:, me_x, me_z, hi, :]
        return remote(part, part, g1_s.at[1, dz], g1_r.at[1, me_z], me_r, me_x * nz + dz)

    def g2z(dz):
        part = ag.at[:, :, me_z, lo, :]
        return remote(part, part, g2_s.at[0, dz], g2_r.at[0, me_z], me_r, me_x * nz + dz)

    def g2x(dx):
        part = ag.at[:, me_x, :, hi, :]
        return remote(part, part, g2_s.at[1, dx], g2_r.at[1, me_x], me_r, dx * nz + me_z)

    for k in range(1, nx):
        g1x((me_x + k) % nx).start()
    for k in range(1, nz):
        g1z((me_z + k) % nz).start()

    for b in range(2):
        @pl.when(me_c != b)
        def _():
            part = wfin.at[b, :, mine_rows, :]
            remote(part, part, wb_s.at[b], wb_r.at[b], me_r, b).wait_recv()

    def wy_copy(d):
        part = wfin.at[:, :, mine_rows, :]
        return remote(part, part, wy_s.at[d], wy_r.at[me_r], d, me_c)

    def wy_start(k, c):
        wy_copy((me_r + k) % rows_n).start()
        return c

    lax.fori_loop(1, rows_n, wy_start, 0)

    for k in range(1, nx):
        sx = (me_x + k) % nx
        part = ag.at[:, sx, me_z, lo, :]
        remote(part, part, g1_s.at[0, sx], g1_r.at[0, sx], me_r, sx * nz + me_z).wait_recv()
    for k in range(1, nz):
        g2z((me_z + k) % nz).start()
    for k in range(1, nz):
        sz = (me_z + k) % nz
        part = ag.at[:, me_x, sz, hi, :]
        remote(part, part, g1_s.at[1, sz], g1_r.at[1, sz], me_r, me_x * nz + sz).wait_recv()
    for k in range(1, nx):
        g2x((me_x + k) % nx).start()

    def y_wait(k, c):
        s = (me_r + k) % rows_n
        rows = pl.ds(pl.multiple_of(s * sl, sl), sl)
        part = fin.at[:, rows, :]
        remote(part, part, y_s.at[s], y_r.at[s], s, me_c).wait_recv()
        part = wfin.at[:, :, rows, :]
        remote(part, part, wy_s.at[s], wy_r.at[s], s, me_c).wait_recv()
        return c

    lax.fori_loop(1, rows_n, y_wait, 0)
    f_out = pltpu.make_async_copy(fin, fin_hbm, out_sem.at[1])
    f_out.start()
    w_out = pltpu.make_async_copy(wfin, wfin_hbm, out_sem.at[2])
    w_out.start()

    for k in range(1, nz):
        sz = (me_z + k) % nz
        part = ag.at[:, :, sz, lo, :]
        remote(part, part, g2_s.at[0, sz], g2_r.at[0, sz], me_r, me_x * nz + sz).wait_recv()
    for k in range(1, nx):
        sx = (me_x + k) % nx
        part = ag.at[:, sx, :, hi, :]
        remote(part, part, g2_s.at[1, sx], g2_r.at[1, sx], me_r, sx * nz + me_z).wait_recv()
    g_out = pltpu.make_async_copy(ag, ag_hbm, out_sem.at[3])
    g_out.start()

    def sent_col(k, c):
        d = (me_c + k) % cols_n
        lab_copy(d).wait_send()
        direct(0, d).wait_send()
        direct(1, d).wait_send()
        return c

    lax.fori_loop(1, cols_n, sent_col, 0)

    def sent_relay(k, c0):
        for c in range(2):
            relay_out(c, *offset(k)).wait_send()
        return c0

    lax.fori_loop(0, relays, sent_relay, 0)

    def sent_row(k, c):
        d = (me_r + k) % rows_n
        rs_copy(d).wait_send()
        y_copy(d).wait_send()
        wy_copy(d).wait_send()
        return c

    lax.fori_loop(1, rows_n, sent_row, 0)
    for b in range(2):
        @pl.when(me_c == b)
        def _():
            def go(k, c):
                d = (b + k) % cols_n
                sc_copy(b, d).wait_send()
                wb_copy(b, d).wait_send()
                return c
            lax.fori_loop(1, cols_n, go, 0)

        @pl.when(me_r == b)
        def _():
            def go(k, c):
                t_copy(b, (b + k) % rows_n).wait_send()
                return c
            lax.fori_loop(1, rows_n, go, 0)
    for k in range(1, nx):
        g1x((me_x + k) % nx).wait_send()
        g2x((me_x + k) % nx).wait_send()
    for k in range(1, nz):
        g1z((me_z + k) % nz).wait_send()
        g2z((me_z + k) % nz).wait_send()
    m_out.wait()
    f_out.wait()
    w_out.wait()
    g_out.wait()


def cmat(v):
    h = v.shape[1] // 2
    re, im = v[:, :h], v[:, h:]
    return jnp.concatenate([v, jnp.concatenate([-im, re], 1)], 0)


def dot(a, b):
    return jnp.dot(a, b, precision=HI, preferred_element_type=jnp.float32)


def mm(a, b):
    return jnp.dot(a, b, preferred_element_type=jnp.float32)


def split(v):
    hi = v.astype(jnp.bfloat16)
    return hi, (v - hi.astype(jnp.float32)).astype(jnp.bfloat16)


def finish_kernel(rows_n, tiles_step, piv_ref, inv_ref, fin_ref, wfin_ref, m_ref, g_ref, o_ref, h, h_hi, h_lo, t3, u1_ref):
    i = pl.program_id(0)
    my_col = lax.axis_index("pcol")
    my_row = lax.axis_index("prow")
    wide = m_ref.shape[1]
    f32 = jnp.float32
    bf16 = jnp.bfloat16
    spots = (slice(0, NB), slice(wide // 2, wide // 2 + NB))

    @pl.when(i == 0)
    def _():
        for s in range(2):
            rest = jnp.concatenate([fin_ref[2 + s], wfin_ref[0, 2 + s], wfin_ref[1, 2 + s]], 1)
            for k in range(3):
                piece = rest.astype(bf16)
                t3[k, s * NB:(s + 1) * NB, :] = piece
                rest = rest - piece.astype(f32)
        first = jnp.broadcast_to(piv_ref[0:1, :].astype(f32), (NB, NB))
        second = jnp.broadcast_to(piv_ref[1:2, :].astype(f32), (NB, NB)).T
        both = (first == second).astype(f32)
        e = both.astype(bf16)
        from_t = mm(e, t3[2, :NB, :]) + mm(e, t3[1, :NB, :]) + mm(e, t3[0, :NB, :])
        taken = jnp.max(both, axis=1, keepdims=True) > 0
        p1 = jnp.where(taken, from_t, jnp.concatenate([fin_ref[1], wfin_ref[0, 1], wfin_ref[1, 1]], 1))
        i0 = jnp.concatenate([inv_ref[0, 0], inv_ref[0, 1]], 1)
        i1 = jnp.concatenate([inv_ref[1, 0], inv_ref[1, 1]], 1)
        c0 = cmat(fin_ref[0])
        l0p1 = dot(p1[:, wide:wide + 2 * NB], cmat(i0))
        u1 = p1[:, :wide] - dot(l0p1, c0)
        c1 = cmat(u1)
        g = dot(dot(i0, cmat(wfin_ref[1, 0])), cmat(i1))
        h[0:2 * NB] = cmat(dot(i0, c0) - dot(g, c1))
        h[2 * NB:] = cmat(dot(i1, c1))
        u1_ref[...] = u1

        @pl.when(my_col == 0)
        def _():
            ci = cmat(i0)
            for k, lanes in enumerate(spots):
                h[0:2 * NB, lanes] = -ci[:, k * NB:(k + 1) * NB]
                h[2 * NB:, lanes] = jnp.zeros((2 * NB, NB), f32)
                u1_ref[:, lanes] = l0p1[:, k * NB:(k + 1) * NB]

        @pl.when(my_col == 1)
        def _():
            cg = cmat(g)
            ci = cmat(i1)
            for k, lanes in enumerate(spots):
                h[0:2 * NB, lanes] = cg[:, k * NB:(k + 1) * NB]
                h[2 * NB:, lanes] = -ci[:, k * NB:(k + 1) * NB]

        hi, lo = split(h[...])
        h_hi[...] = hi
        h_lo[...] = lo

    step = tiles_step * NB
    r = lax.broadcasted_iota(jnp.int32, (step, NB), 0)
    row = ((i * tiles_step + r // NB) * rows_n + my_row) * NB + r % NB
    moved = row >= 2 * NB
    hit0 = jnp.where((row == piv_ref[0:1, :]) & moved, 1.0, 0.0)
    hit1 = jnp.where((row == piv_ref[1:2, :]) & moved, 1.0, 0.0)
    in0 = jnp.max(hit0, axis=1, keepdims=True)
    in1 = jnp.max(hit1, axis=1, keepdims=True)
    s = jnp.concatenate([hit0 * (1.0 - in1), hit1], 1).astype(bf16)
    swap = mm(s, t3[2]) + mm(s, t3[1]) + mm(s, t3[0])
    raw = jnp.concatenate([m_ref[...], g_ref[0].reshape(step, 2 * NB), g_ref[1].reshape(step, 2 * NB)], 1)
    z = jnp.where(in0 + in1 > 0, swap, raw)
    hi, lo = split(z[:, wide:])
    update = mm(hi, h_hi[...]) + (mm(hi, h_lo[...]) + mm(lo, h_hi[...]))
    lane = lax.broadcasted_iota(jnp.int32, (step, wide), 1)
    panel = ((lane % (wide // 2)) < NB) & (my_col < 2)
    out = jnp.where(panel, 0.0, z[:, :wide]) - update
    for c in range(2):
        o_ref[c] = out[:, c * (wide // 2):(c + 1) * (wide // 2)]

    @pl.when((i == 0) & (my_row == 0))
    def _():
        for c in range(2):
            o_ref[c, 0:NB] = fin_ref[0, :, c * (wide // 2):(c + 1) * (wide // 2)]

    @pl.when((i == 0) & (my_row == 1))
    def _():
        for c in range(2):
            o_ref[c, 0:NB] = u1_ref[:, c * (wide // 2):(c + 1) * (wide // 2)]


def per_device(dims, assembly, slot_tile, pivots, inverses):
    rows_n, nx, nz, cap, row_tiles = dims
    cols_n = nx * nz
    tiles = assembly[0]
    slots = tiles.shape[0]
    width_tiles = CBLK * cols_n
    ident = slot_tile[0]
    column_tile = ident % width_tiles
    target = column_tile % cols_n
    local_id = ident // width_tiles * CBLK + column_tile // cols_n
    num = jnp.arange(slots, dtype=jnp.int32)
    rank = jnp.sum(((target[:, None] == target[None, :]) & (num[None, :] < num[:, None])).astype(jnp.int32), axis=1)
    position = target * cap + rank
    hit = position[None, :] == jnp.arange(128, dtype=jnp.int32)[:, None]
    send_idx = jnp.sum(jnp.where(hit, num[None, :], 0), axis=1)
    labels = jnp.sum(jnp.where(hit, local_id[None, :] + 1, 0), axis=1) - 1
    labels = jnp.broadcast_to(labels[None, :], (8, 128))

    sl = NB // rows_n
    rows = row_tiles * NB
    wide = 2 * CBLK * NB
    f32 = jnp.float32
    dma = pltpu.SemaphoreType.DMA
    hbm = pl.BlockSpec(memory_space=pl.ANY)
    smem = pl.BlockSpec(memory_space=pltpu.SMEM)
    n = max(nx, nz)
    m_raw, ag, fin, wfin = pl.pallas_call(
        functools.partial(comm_kernel, dims),
        out_shape=(
            jax.ShapeDtypeStruct((rows, wide), f32),
            jax.ShapeDtypeStruct((2, nx, nz, NB, 2 * NB), f32),
            jax.ShapeDtypeStruct((4, NB, wide), f32),
            jax.ShapeDtypeStruct((2, 4, NB, 2 * NB), f32),
        ),
        in_specs=[smem, smem, pl.BlockSpec(memory_space=pltpu.VMEM), hbm],
        out_specs=(hbm, hbm, hbm, hbm),
        scratch_shapes=[
            pltpu.VMEM((slots, 2, NB, NB), f32),
            pltpu.VMEM((2, cols_n, cap, NB, NB), f32),
            pltpu.VMEM((2, cols_n, cap, NB, NB), f32),
            pltpu.VMEM((2, cols_n, cap, NB, NB), f32),
            pltpu.VMEM((cols_n, 8, 128), jnp.int32),
            pltpu.VMEM((rows, wide), f32),
            pltpu.VMEM((row_tiles, NB, 2 * NB), f32),
            pltpu.VMEM((2, nx, nz, NB, 2 * NB), f32),
            pltpu.VMEM((rows_n, 2 * sl, wide), f32),
            pltpu.VMEM((rows_n, 2 * sl, wide), f32),
            pltpu.VMEM((4, NB, wide), f32),
            pltpu.VMEM((2, 4, NB, 2 * NB), f32),
            pltpu.SMEM((slots,), jnp.int32),
            dma((5,)),
            dma((cols_n,)), dma((cols_n,)),
            dma((2, cols_n)), dma((2, cols_n)),
            dma((2, cols_n)), dma((2, cols_n)),
            dma((cols_n,)), dma((2,)),
            dma((rows_n,)), dma((rows_n,)),
            dma((rows_n,)), dma((2,)),
            dma((rows_n,)), dma((rows_n,)),
            dma((cols_n,)), dma((2,)),
            dma((rows_n,)), dma((rows_n,)),
            dma((2, n)), dma((2, n)),
            dma((2, n)), dma((2, n)),
        ],
        compiler_params=pltpu.CompilerParams(
            collective_id=0, has_side_effects=True, vmem_limit_bytes=63 * 1024 * 1024),
        name="exchange",
    )(send_idx, pivots, labels, tiles)

    tiles_step = 2
    step = tiles_step * NB
    whole = lambda *shape: pl.BlockSpec(shape, lambda i: (0,) * len(shape))
    return pl.pallas_call(
        functools.partial(finish_kernel, rows_n, tiles_step),
        grid=(row_tiles // tiles_step,),
        out_shape=jax.ShapeDtypeStruct((2, rows, CBLK * NB), f32),
        in_specs=[
            whole(2, NB), whole(2, 2, NB, NB), whole(4, NB, wide), whole(2, 4, NB, 2 * NB),
            pl.BlockSpec((step, wide), lambda i: (i, 0)),
            pl.BlockSpec((2, tiles_step, NB, 2 * NB), lambda i: (0, i, 0, 0)),
        ],
        out_specs=pl.BlockSpec((2, step, CBLK * NB), lambda i: (0, i, 0)),
        scratch_shapes=[
            pltpu.VMEM((4 * NB, wide), f32),
            pltpu.VMEM((4 * NB, wide), jnp.bfloat16),
            pltpu.VMEM((4 * NB, wide), jnp.bfloat16),
            pltpu.VMEM((3, 2 * NB, 2 * wide), jnp.bfloat16),
            pltpu.VMEM((NB, wide), f32),
        ],
        compiler_params=pltpu.CompilerParams(dimension_semantics=("arbitrary",), vmem_limit_bytes=63 * 1024 * 1024),
        name="finish",
    )(pivots, inverses, fin, wfin, m_raw, ag.reshape(2, row_tiles, NB, 2 * NB))


def grid_of(cols_n):
    nx = 1
    while nx * nx < cols_n:
        nx *= 2
    return nx, cols_n // nx


def solution(mesh):
    rows_n, cols_n = mesh.shape["prow"], mesh.shape["pcol"]
    nx, nz = grid_of(cols_n)

    def body(assembly, slot_tile, pivots, inverses):
        slots = assembly.shape[1]
        cap = (slots + cols_n - 1) // cols_n + 1
        dims = (rows_n, nx, nz, cap, slots // CBLK)
        return per_device(dims, assembly, slot_tile, pivots, inverses)

    in_specs = (P("prow", "pcol", None, None, None), P("prow", "pcol"), P(), P())
    out_specs = P(None, "prow", "pcol")
    return jax.shard_map(body, mesh=mesh, in_specs=in_specs, out_specs=out_specs, check_vma=False)
```

```python
import functools

import jax
import jax.numpy as jnp
from jax import lax
from jax.experimental import pallas as pl
from jax.experimental.pallas import tpu as pltpu
from jax.sharding import PartitionSpec as P

CBLK = 2
NB = 128
MESH = pl.DeviceIdType.MESH
HI = lax.Precision.HIGHEST


def comm_kernel(
    dims, idx_ref, piv_ref, lab_ref, asm_hbm,
    m_hbm, ag_hbm, fin_hbm, wfin_hbm,
    asm, sendb, mid, recvb, labs, mat, pb, ag, st, pk, pr, ps, rb, fin, wfin, place,
    out_sem, lab_s, lab_r, a_s, a_r, b_s, b_r, sx_s, sd_s, sr_s, st_r, sc_r, pk_s, pk_r, rs_s, rs_r, t_s, t_r,
    y_s, y_r, k_s, k_r, wb_s, wb_r, g1_s, g1_r, g2_s, g2_r,
):
    rows_n, nx, nz, cap, row_tiles = dims
    cols_n = nx * nz
    sl = NB // rows_n
    half = NB // 2
    me_r = lax.axis_index("prow")
    me_c = lax.axis_index("pcol")
    me_x = me_c // nz
    me_z = me_c % nz

    def remote(src, dst, ssem, rsem, row, col):
        return pltpu.make_async_remote_copy(
            src_ref=src, dst_ref=dst, send_sem=ssem, recv_sem=rsem,
            device_id=(row, col), device_id_type=MESH)

    load = pltpu.make_async_copy(asm_hbm, asm, out_sem.at[4])
    load.start()

    barrier = pltpu.get_barrier_semaphore()

    def greet_col(k, c):
        pl.semaphore_signal(barrier, inc=1, device_id=(me_r, (me_c + k) % cols_n), device_id_type=MESH)
        return c

    def greet_row(k, c):
        pl.semaphore_signal(barrier, inc=1, device_id=((me_r + k) % rows_n, me_c), device_id_type=MESH)
        return c

    lax.fori_loop(1, cols_n, greet_col, 0)
    lax.fori_loop(1, rows_n, greet_row, 0)
    pl.semaphore_wait(barrier, cols_n - 1 + rows_n - 1)

    def lab_copy(d):
        return remote(lab_ref, labs.at[me_c], lab_s.at[d], lab_r.at[me_c], me_r, d)

    def lab_start(k, c):
        lab_copy((me_c + k) % cols_n).start()
        return c

    lax.fori_loop(1, cols_n, lab_start, 0)
    labs[me_c] = lab_ref[...]
    load.wait()

    def first_hop(c, d):
        dx, dz = d // nz, d % nz
        if c == 0:
            return remote(sendb.at[0, d], mid.at[0, me_x * nz + dz], a_s.at[0, d], b_r.at[0, me_x * nz + dz],
                          me_r, dx * nz + me_z)
        return remote(sendb.at[1, d], mid.at[1, dx * nz + me_z], a_s.at[1, d], b_r.at[1, dx * nz + me_z],
                      me_r, me_x * nz + dz)

    def direct(c, d):
        return remote(sendb.at[c, d], recvb.at[c, me_c], a_s.at[c, d], a_r.at[c, me_c], me_r, d)

    def relay_in(c, dx, dz):
        if c == 0:
            sx = (me_x + nx - dx) % nx
            at = sx * nz + (me_z + dz) % nz
            return remote(sendb.at[0, at], mid.at[0, at], b_s.at[0, at], b_r.at[0, at], me_r, sx * nz + me_z)
        sz = (me_z + nz - dz) % nz
        at = (me_x + dx) % nx * nz + sz
        return remote(sendb.at[1, at], mid.at[1, at], b_s.at[1, at], b_r.at[1, at], me_r, me_x * nz + sz)

    def relay_out(c, dx, dz):
        if c == 0:
            sx = (me_x + nx - dx) % nx
            tz = (me_z + dz) % nz
            at = sx * nz + tz
            src = sx * nz + me_z
            return remote(mid.at[0, at], recvb.at[0, src], b_s.at[0, at], a_r.at[0, src], me_r, me_x * nz + tz)
        sz = (me_z + nz - dz) % nz
        tx = (me_x + dx) % nx
        at = tx * nz + sz
        src = me_x * nz + sz
        return remote(mid.at[1, at], recvb.at[1, src], b_s.at[1, at], a_r.at[1, src], me_r, tx * nz + me_z)

    def offset(k):
        return k % (nx - 1) + 1, k // (nx - 1) + 1

    def peer(dx, dz):
        return (me_x + dx) % nx * nz + (me_z + dz) % nz

    def pack_to(dst, d, e):
        for r in range(cap):
            t = idx_ref[d * cap + r]
            for c in range(2):
                dst[c, e, r] = asm[t, c]

    def pack(k, c0):
        d = peer(*offset(k))
        pack_to(sendb, d, d)

        @pl.when(k > 0)
        def _():
            p = peer(*offset(jnp.maximum(k - 1, 0)))
            first_hop(0, p).start()
            first_hop(1, p).start()
        return c0

    relays = (nx - 1) * (nz - 1)
    lax.fori_loop(0, relays, pack, 0)
    axis_peers = [(dx, 0) for dx in range(1, nx)] + [(0, dz) for dz in range(1, nz)]
    for n, (dx, dz) in enumerate(axis_peers):
        d = peer(dx, dz)
        pack_to(sendb, d, d)
        if n == 0:
            p = peer(*offset(relays - 1))
            first_hop(0, p).start()
            first_hop(1, p).start()
        else:
            p = peer(*axis_peers[n - 1])
            direct(0, p).start()
            direct(1, p).start()
    pack_to(recvb, me_c, me_c)
    direct(0, peer(*axis_peers[-1])).start()
    direct(1, peer(*axis_peers[-1])).start()

    def relay(k, c0):
        dx, dz = offset(k)
        for c in range(2):
            relay_in(c, dx, dz).wait_recv()
            relay_out(c, dx, dz).start()
        return c0

    lax.fori_loop(0, relays, relay, 0)

    def lab_wait(k, c):
        s = (me_c + k) % cols_n
        remote(lab_ref, labs.at[s], lab_s.at[s], lab_r.at[s], me_r, s).wait_recv()
        return c

    lax.fori_loop(1, cols_n, lab_wait, 0)
    seen = labs[:, 0, :]
    lane = lax.broadcasted_iota(jnp.int32, seen.shape, 1) - me_c * cap
    code = lax.broadcasted_iota(jnp.int32, seen.shape, 0) * cap + lane
    code = jnp.where((lane >= 0) & (lane < cap), code, 0)
    valid = jnp.where((lane >= 0) & (lane < cap), seen, -1)

    def find(t, c):
        place[t] = jnp.minimum(jnp.sum(jnp.where(valid == t, code, 0)), cols_n * cap - 1)
        return c

    lax.fori_loop(0, row_tiles * CBLK, find, 0)

    def a_wait(k, c):
        s = (me_c + k) % cols_n
        for h in range(2):
            remote(sendb.at[h, s], recvb.at[h, s], a_s.at[h, s], a_r.at[h, s], me_r, s).wait_recv()
        return c

    lax.fori_loop(1, cols_n, a_wait, 0)

    def put(i, c):
        rows = pl.ds(pl.multiple_of(i * NB, NB), NB)
        for m in range(CBLK):
            at = place[i * CBLK + m]
            s = at // cap
            r = at - s * cap
            re = recvb[0, s, r]
            im = recvb[1, s, r]
            mat[rows, m * NB:(m + 1) * NB] = re
            mat[rows, (CBLK + m) * NB:(CBLK + m + 1) * NB] = im
            if m == 0:
                pb[i // nz, i % nz, :, 0:NB] = re
                pb[i // nz, i % nz, :, NB:2 * NB] = im
        return c

    lax.fori_loop(0, row_tiles, put, 0)
    m_out = pltpu.make_async_copy(mat, m_hbm, out_sem.at[0])
    m_out.start()

    lo = pl.ds(0, half)
    hi = pl.ds(half, half)

    def root(b):
        return b // nz, b % nz

    def out_x(b, dx):
        return remote(pb.at[dx, :, lo, :], st.at[0, b, pl.ds(0, nz)], sx_s.at[0, dx], st_r.at[0, b],
                      me_r, dx * nz + root(b)[1])

    def out_z(b, dz):
        return remote(pb.at[:, dz, hi, :], st.at[1, b, pl.ds(0, nx)], sx_s.at[1, dz], st_r.at[1, b],
                      me_r, root(b)[0] * nz + dz)

    def lo_to(b, src, ssem, dx, dz):
        return remote(src, ag.at[b, dx, dz, lo, :], ssem, sc_r.at[0, b], me_r, dx * nz + dz)

    def hi_to(b, src, ssem, dx, dz):
        return remote(src, ag.at[b, dx, dz, hi, :], ssem, sc_r.at[1, b], me_r, dx * nz + dz)

    def root_copies(b):
        x0, z0 = root(b)
        copies = []
        for k in range(1, max(nx, nz)):
            if k < nx:
                copies.append(out_x(b, (x0 + k) % nx))
            if k < nz:
                copies.append(out_z(b, (z0 + k) % nz))
        for k in range(1, nz):
            dz = (z0 + k) % nz
            copies.append(lo_to(b, pb.at[x0, dz, lo, :], sd_s.at[0, dz], x0, dz))
        for k in range(1, nx):
            dx = (x0 + k) % nx
            copies.append(hi_to(b, pb.at[dx, z0, hi, :], sd_s.at[1, dx], dx, z0))
        return copies

    def relay_x_copies(b):
        x0, z0 = root(b)
        return [lo_to(b, st.at[0, b, (z0 + k) % nz], sr_s.at[0, b, k], me_x, (z0 + k) % nz) for k in range(1, nz)]

    def relay_z_copies(b):
        x0, z0 = root(b)
        return [hi_to(b, st.at[1, b, (x0 + k) % nx], sr_s.at[1, b, k], (x0 + k) % nx, me_z) for k in range(1, nx)]

    def is_relay_x(b):
        x0, z0 = root(b)
        return (me_z == z0) & (me_x != x0)

    def is_relay_z(b):
        x0, z0 = root(b)
        return (me_x == x0) & (me_z != z0)

    for b in range(2):
        @pl.when(me_c == b)
        def _():
            for copy in root_copies(b):
                copy.start()
            ag[b, root(b)[0], root(b)[1]] = pb[root(b)[0], root(b)[1]]

    def t_copy(s, d):
        rows = pl.ds(pl.multiple_of(d * sl, sl), sl)
        return remote(mat.at[rows, :], fin.at[2 + s, rows, :], t_s.at[d], t_r.at[s], d, me_c)

    for s in range(2):
        @pl.when(me_r == s)
        def _():
            def go(k, c):
                t_copy(s, (s + k) % rows_n).start()
                return c
            lax.fori_loop(1, rows_n, go, 0)
            fin[2 + s, s * sl:(s + 1) * sl, :] = mat[s * sl:(s + 1) * sl, :]

    def pick(d, c):
        def one(jj, c2):
            for k in range(2):
                r = piv_ref[k, d * sl + jj]
                tile = r // NB
                mine = (tile % rows_n) == me_r
                loc = tile // rows_n * NB + r % NB
                row = mat[pl.ds(loc, 1), :]
                pk[d % 2, d // 2, pl.ds(k * sl + jj, 1), :] = jnp.where(mine, row, 0.0)
            return c2
        return lax.fori_loop(0, sl, one, c)

    lax.fori_loop(0, rows_n, pick, 0)
    me_y = me_r // 2
    me_k = me_r % 2
    partner = me_y * 2 + 1 - me_k
    ny = rows_n // 2

    pk_copy = remote(pk.at[1 - me_k], pr, pk_s, pk_r, partner, me_c)
    pk_copy.start()

    for b in range(2):
        x0, z0 = root(b)

        @pl.when(is_relay_x(b))
        def _():
            part = st.at[0, b, pl.ds(0, nz)]
            remote(part, part, sr_s.at[0, b, 0], st_r.at[0, b], me_r, b).wait_recv()
            for copy in relay_x_copies(b):
                copy.start()
            ag[b, me_x, z0, 0:half] = st[0, b, z0]

        @pl.when(is_relay_z(b))
        def _():
            part = st.at[1, b, pl.ds(0, nx)]
            remote(part, part, sr_s.at[1, b, 0], st_r.at[1, b], me_r, b).wait_recv()
            for copy in relay_z_copies(b):
                copy.start()
            ag[b, x0, me_z, half:NB] = st[1, b, x0]

    remote(pr, pr, pk_s, pk_r, partner, me_c).wait_recv()
    ps[...] = pk[me_k] + pr[...]

    def rs_copy(ty):
        return remote(ps.at[ty], rb.at[me_y], rs_s.at[ty], rs_r.at[me_y], ty * 2 + me_k, me_c)

    for k in range(1, ny):
        rs_copy((me_y + k) % ny).start()

    def g1x(dx):
        part = ag.at[:, me_x, me_z, lo, :]
        return remote(part, part, g1_s.at[0, dx], g1_r.at[0, me_x], me_r, dx * nz + me_z)

    def g1z(dz):
        part = ag.at[:, me_x, me_z, hi, :]
        return remote(part, part, g1_s.at[1, dz], g1_r.at[1, me_z], me_r, me_x * nz + dz)

    def g2z(dz):
        part = ag.at[:, :, me_z, lo, :]
        return remote(part, part, g2_s.at[0, dz], g2_r.at[0, me_z], me_r, me_x * nz + dz)

    def g2x(dx):
        part = ag.at[:, me_x, :, hi, :]
        return remote(part, part, g2_s.at[1, dx], g2_r.at[1, me_x], me_r, dx * nz + me_z)

    for b in range(2):
        x0, z0 = root(b)

        @pl.when(me_z != z0)
        def _():
            part = ag.at[b, me_x, me_z, lo, :]
            remote(part, part, sd_s.at[0, 0], sc_r.at[0, b], me_r, me_x * nz + z0).wait_recv()

    for k in range(1, nx):
        g1x((me_x + k) % nx).start()
    for b in range(2):
        x0, z0 = root(b)

        @pl.when(me_x != x0)
        def _():
            part = ag.at[b, me_x, me_z, hi, :]
            remote(part, part, sd_s.at[1, 0], sc_r.at[1, b], me_r, x0 * nz + me_z).wait_recv()

    for k in range(1, nz):
        g1z((me_z + k) % nz).start()

    mine_rows = pl.ds(pl.multiple_of(me_r * sl, sl), sl)
    total = ps[me_y]
    for k in range(1, ny):
        sy = (me_y + k) % ny
        remote(ps.at[sy], rb.at[sy], rs_s.at[sy], rs_r.at[sy], sy * 2 + me_k, me_c).wait_recv()
        total = total + rb[sy]
    fin[0, mine_rows, :] = total[:sl]
    fin[1, mine_rows, :] = total[sl:]
    for s in range(2):
        @pl.when(me_r != s)
        def _():
            part = fin.at[2 + s, mine_rows, :]
            remote(part, part, t_s.at[s], t_r.at[s], s, me_c).wait_recv()

    def wb_copy(b, d):
        part = wfin.at[b, :, mine_rows, :]
        return remote(part, part, wb_s.at[d], wb_r.at[b], me_r, d)

    for b in range(2):
        @pl.when(me_c == b)
        def _():
            wfin[b, :, mine_rows, 0:NB] = fin[:, mine_rows, 0:NB]
            wfin[b, :, mine_rows, NB:2 * NB] = fin[:, mine_rows, CBLK * NB:(CBLK + 1) * NB]

            def go(k, c):
                wb_copy(b, (b + k) % cols_n).start()
                return c
            lax.fori_loop(1, cols_n, go, 0)

    def rows_of(w, r):
        rows = pl.ds(pl.multiple_of(r * sl, sl), sl)
        return wfin.at[:, :, rows, :] if w else fin.at[:, rows, :]

    def y_copy(w, ty):
        part = rows_of(w, me_r)
        return remote(part, part, y_s.at[w, ty], y_r.at[w, me_y], ty * 2 + me_k, me_c)

    def k_copy(w, sy):
        part = rows_of(w, sy * 2 + me_k)
        return remote(part, part, k_s.at[w, sy], k_r.at[w, sy], partner, me_c)

    def y_start(w):
        for k in range(1, ny):
            y_copy(w, (me_y + k) % ny).start()
        k_copy(w, me_y).start()

    def y_pass(w):
        for k in range(1, ny):
            sy = (me_y + k) % ny
            part = rows_of(w, sy * 2 + me_k)
            remote(part, part, y_s.at[w, sy], y_r.at[w, sy], sy * 2 + me_k, me_c).wait_recv()
            k_copy(w, sy).start()

    def y_end(w):
        for sy in range(ny):
            part = rows_of(w, sy * 2 + 1 - me_k)
            remote(part, part, k_s.at[w, sy], k_r.at[w, sy], partner, me_c).wait_recv()

    y_start(0)

    for k in range(1, nx):
        sx = (me_x + k) % nx
        part = ag.at[:, sx, me_z, lo, :]
        remote(part, part, g1_s.at[0, sx], g1_r.at[0, sx], me_r, sx * nz + me_z).wait_recv()
    for k in range(1, nz):
        g2z((me_z + k) % nz).start()
    for k in range(1, nz):
        sz = (me_z + k) % nz
        part = ag.at[:, me_x, sz, hi, :]
        remote(part, part, g1_s.at[1, sz], g1_r.at[1, sz], me_r, me_x * nz + sz).wait_recv()
    for k in range(1, nx):
        g2x((me_x + k) % nx).start()

    for b in range(2):
        @pl.when(me_c != b)
        def _():
            part = wfin.at[b, :, mine_rows, :]
            remote(part, part, wb_s.at[b], wb_r.at[b], me_r, b).wait_recv()

    y_start(1)
    y_pass(0)
    y_end(0)
    f_out = pltpu.make_async_copy(fin, fin_hbm, out_sem.at[1])
    f_out.start()
    y_pass(1)
    y_end(1)
    w_out = pltpu.make_async_copy(wfin, wfin_hbm, out_sem.at[2])
    w_out.start()

    for k in range(1, nz):
        sz = (me_z + k) % nz
        part = ag.at[:, :, sz, lo, :]
        remote(part, part, g2_s.at[0, sz], g2_r.at[0, sz], me_r, me_x * nz + sz).wait_recv()
    for k in range(1, nx):
        sx = (me_x + k) % nx
        part = ag.at[:, sx, :, hi, :]
        remote(part, part, g2_s.at[1, sx], g2_r.at[1, sx], me_r, sx * nz + me_z).wait_recv()
    g_out = pltpu.make_async_copy(ag, ag_hbm, out_sem.at[3])
    g_out.start()

    def sent_col(k, c):
        d = (me_c + k) % cols_n
        lab_copy(d).wait_send()
        direct(0, d).wait_send()
        direct(1, d).wait_send()
        return c

    lax.fori_loop(1, cols_n, sent_col, 0)

    def sent_relay(k, c0):
        for c in range(2):
            relay_out(c, *offset(k)).wait_send()
        return c0

    lax.fori_loop(0, relays, sent_relay, 0)
    pk_copy.wait_send()
    for k in range(1, ny):
        rs_copy((me_y + k) % ny).wait_send()
    for w in range(2):
        for k in range(1, ny):
            y_copy(w, (me_y + k) % ny).wait_send()
        for sy in range(ny):
            k_copy(w, sy).wait_send()
    for b in range(2):
        @pl.when(me_c == b)
        def _():
            for copy in root_copies(b):
                copy.wait_send()

            def go(k, c):
                wb_copy(b, (b + k) % cols_n).wait_send()
                return c
            lax.fori_loop(1, cols_n, go, 0)

        @pl.when(is_relay_x(b))
        def _():
            for copy in relay_x_copies(b):
                copy.wait_send()

        @pl.when(is_relay_z(b))
        def _():
            for copy in relay_z_copies(b):
                copy.wait_send()

        @pl.when(me_r == b)
        def _():
            def go(k, c):
                t_copy(b, (b + k) % rows_n).wait_send()
                return c
            lax.fori_loop(1, rows_n, go, 0)
    for k in range(1, nx):
        g1x((me_x + k) % nx).wait_send()
        g2x((me_x + k) % nx).wait_send()
    for k in range(1, nz):
        g1z((me_z + k) % nz).wait_send()
        g2z((me_z + k) % nz).wait_send()
    m_out.wait()
    f_out.wait()
    w_out.wait()
    g_out.wait()


def cmat(v):
    h = v.shape[1] // 2
    re, im = v[:, :h], v[:, h:]
    return jnp.concatenate([v, jnp.concatenate([-im, re], 1)], 0)


def dot(a, b):
    return jnp.dot(a, b, precision=HI, preferred_element_type=jnp.float32)


def mm(a, b):
    return jnp.dot(a, b, preferred_element_type=jnp.float32)


def split(v):
    hi = v.astype(jnp.bfloat16)
    return hi, (v - hi.astype(jnp.float32)).astype(jnp.bfloat16)


def finish_kernel(rows_n, tiles_step, piv_ref, inv_ref, fin_ref, wfin_ref, m_ref, g_ref, o_ref, h, h_hi, h_lo, t3, u1_ref):
    i = pl.program_id(0)
    my_col = lax.axis_index("pcol")
    my_row = lax.axis_index("prow")
    wide = m_ref.shape[1]
    f32 = jnp.float32
    bf16 = jnp.bfloat16
    spots = (slice(0, NB), slice(wide // 2, wide // 2 + NB))

    @pl.when(i == 0)
    def _():
        for s in range(2):
            rest = jnp.concatenate([fin_ref[2 + s], wfin_ref[0, 2 + s], wfin_ref[1, 2 + s]], 1)
            for k in range(3):
                piece = rest.astype(bf16)
                t3[k, s * NB:(s + 1) * NB, :] = piece
                rest = rest - piece.astype(f32)
        first = jnp.broadcast_to(piv_ref[0:1, :].astype(f32), (NB, NB))
        second = jnp.broadcast_to(piv_ref[1:2, :].astype(f32), (NB, NB)).T
        both = (first == second).astype(f32)
        e = both.astype(bf16)
        from_t = mm(e, t3[2, :NB, :]) + mm(e, t3[1, :NB, :]) + mm(e, t3[0, :NB, :])
        taken = jnp.max(both, axis=1, keepdims=True) > 0
        p1 = jnp.where(taken, from_t, jnp.concatenate([fin_ref[1], wfin_ref[0, 1], wfin_ref[1, 1]], 1))
        i0 = jnp.concatenate([inv_ref[0, 0], inv_ref[0, 1]], 1)
        i1 = jnp.concatenate([inv_ref[1, 0], inv_ref[1, 1]], 1)
        c0 = cmat(fin_ref[0])
        l0p1 = dot(p1[:, wide:wide + 2 * NB], cmat(i0))
        u1 = p1[:, :wide] - dot(l0p1, c0)
        c1 = cmat(u1)
        g = dot(dot(i0, cmat(wfin_ref[1, 0])), cmat(i1))
        h[0:2 * NB] = cmat(dot(i0, c0) - dot(g, c1))
        h[2 * NB:] = cmat(dot(i1, c1))
        u1_ref[...] = u1

        @pl.when(my_col == 0)
        def _():
            ci = cmat(i0)
            for k, lanes in enumerate(spots):
                h[0:2 * NB, lanes] = -ci[:, k * NB:(k + 1) * NB]
                h[2 * NB:, lanes] = jnp.zeros((2 * NB, NB), f32)
                u1_ref[:, lanes] = l0p1[:, k * NB:(k + 1) * NB]

        @pl.when(my_col == 1)
        def _():
            cg = cmat(g)
            ci = cmat(i1)
            for k, lanes in enumerate(spots):
                h[0:2 * NB, lanes] = cg[:, k * NB:(k + 1) * NB]
                h[2 * NB:, lanes] = -ci[:, k * NB:(k + 1) * NB]

        hi, lo = split(h[...])
        h_hi[...] = hi
        h_lo[...] = lo

    step = tiles_step * NB
    r = lax.broadcasted_iota(jnp.int32, (step, NB), 0)
    row = ((i * tiles_step + r // NB) * rows_n + my_row) * NB + r % NB
    moved = row >= 2 * NB
    hit0 = jnp.where((row == piv_ref[0:1, :]) & moved, 1.0, 0.0)
    hit1 = jnp.where((row == piv_ref[1:2, :]) & moved, 1.0, 0.0)
    in0 = jnp.max(hit0, axis=1, keepdims=True)
    in1 = jnp.max(hit1, axis=1, keepdims=True)
    s = jnp.concatenate([hit0 * (1.0 - in1), hit1], 1).astype(bf16)
    swap = mm(s, t3[2]) + mm(s, t3[1]) + mm(s, t3[0])
    raw = jnp.concatenate([m_ref[...], g_ref[0].reshape(step, 2 * NB), g_ref[1].reshape(step, 2 * NB)], 1)
    z = jnp.where(in0 + in1 > 0, swap, raw)
    hi, lo = split(z[:, wide:])
    update = mm(hi, h_hi[...]) + (mm(hi, h_lo[...]) + mm(lo, h_hi[...]))
    lane = lax.broadcasted_iota(jnp.int32, (step, wide), 1)
    panel = ((lane % (wide // 2)) < NB) & (my_col < 2)
    out = jnp.where(panel, 0.0, z[:, :wide]) - update
    for c in range(2):
        o_ref[c] = out[:, c * (wide // 2):(c + 1) * (wide // 2)]

    @pl.when((i == 0) & (my_row == 0))
    def _():
        for c in range(2):
            o_ref[c, 0:NB] = fin_ref[0, :, c * (wide // 2):(c + 1) * (wide // 2)]

    @pl.when((i == 0) & (my_row == 1))
    def _():
        for c in range(2):
            o_ref[c, 0:NB] = u1_ref[:, c * (wide // 2):(c + 1) * (wide // 2)]


def per_device(dims, assembly, slot_tile, pivots, inverses):
    rows_n, nx, nz, cap, row_tiles = dims
    cols_n = nx * nz
    tiles = assembly[0]
    slots = tiles.shape[0]
    width_tiles = CBLK * cols_n
    ident = slot_tile[0]
    column_tile = ident % width_tiles
    target = column_tile % cols_n
    local_id = ident // width_tiles * CBLK + column_tile // cols_n
    num = jnp.arange(slots, dtype=jnp.int32)
    rank = jnp.sum(((target[:, None] == target[None, :]) & (num[None, :] < num[:, None])).astype(jnp.int32), axis=1)
    position = target * cap + rank
    hit = position[None, :] == jnp.arange(128, dtype=jnp.int32)[:, None]
    send_idx = jnp.sum(jnp.where(hit, num[None, :], 0), axis=1)
    labels = jnp.sum(jnp.where(hit, local_id[None, :] + 1, 0), axis=1) - 1
    labels = jnp.broadcast_to(labels[None, :], (8, 128))

    sl = NB // rows_n
    rows = row_tiles * NB
    wide = 2 * CBLK * NB
    f32 = jnp.float32
    dma = pltpu.SemaphoreType.DMA
    hbm = pl.BlockSpec(memory_space=pl.ANY)
    smem = pl.BlockSpec(memory_space=pltpu.SMEM)
    n = max(nx, nz)
    ny = rows_n // 2
    m_raw, ag, fin, wfin = pl.pallas_call(
        functools.partial(comm_kernel, dims),
        out_shape=(
            jax.ShapeDtypeStruct((rows, wide), f32),
            jax.ShapeDtypeStruct((2, nx, nz, NB, 2 * NB), f32),
            jax.ShapeDtypeStruct((4, NB, wide), f32),
            jax.ShapeDtypeStruct((2, 4, NB, 2 * NB), f32),
        ),
        in_specs=[smem, smem, pl.BlockSpec(memory_space=pltpu.VMEM), hbm],
        out_specs=(hbm, hbm, hbm, hbm),
        scratch_shapes=[
            pltpu.VMEM((slots, 2, NB, NB), f32),
            pltpu.VMEM((2, cols_n, cap, NB, NB), f32),
            pltpu.VMEM((2, cols_n, cap, NB, NB), f32),
            pltpu.VMEM((2, cols_n, cap, NB, NB), f32),
            pltpu.VMEM((cols_n, 8, 128), jnp.int32),
            pltpu.VMEM((rows, wide), f32),
            pltpu.VMEM((nx, nz, NB, 2 * NB), f32),
            pltpu.VMEM((2, nx, nz, NB, 2 * NB), f32),
            pltpu.VMEM((2, 2, n, NB // 2, 2 * NB), f32),
            pltpu.VMEM((2, ny, 2 * sl, wide), f32),
            pltpu.VMEM((ny, 2 * sl, wide), f32),
            pltpu.VMEM((ny, 2 * sl, wide), f32),
            pltpu.VMEM((ny, 2 * sl, wide), f32),
            pltpu.VMEM((4, NB, wide), f32),
            pltpu.VMEM((2, 4, NB, 2 * NB), f32),
            pltpu.SMEM((slots,), jnp.int32),
            dma((5,)),
            dma((cols_n,)), dma((cols_n,)),
            dma((2, cols_n)), dma((2, cols_n)),
            dma((2, cols_n)), dma((2, cols_n)),
            dma((2, n)), dma((2, n)), dma((2, 2, n)), dma((2, 2)), dma((2, 2)),
            dma, dma,
            dma((ny,)), dma((ny,)),
            dma((rows_n,)), dma((2,)),
            dma((2, ny)), dma((2, ny)), dma((2, ny)), dma((2, ny)),
            dma((cols_n,)), dma((2,)),
            dma((2, n)), dma((2, n)),
            dma((2, n)), dma((2, n)),
        ],
        compiler_params=pltpu.CompilerParams(
            collective_id=0, has_side_effects=True, vmem_limit_bytes=63 * 1024 * 1024),
        name="exchange",
    )(send_idx, pivots, labels, tiles)

    tiles_step = 2
    step = tiles_step * NB
    whole = lambda *shape: pl.BlockSpec(shape, lambda i: (0,) * len(shape))
    return pl.pallas_call(
        functools.partial(finish_kernel, rows_n, tiles_step),
        grid=(row_tiles // tiles_step,),
        out_shape=jax.ShapeDtypeStruct((2, rows, CBLK * NB), f32),
        in_specs=[
            whole(2, NB), whole(2, 2, NB, NB), whole(4, NB, wide), whole(2, 4, NB, 2 * NB),
            pl.BlockSpec((step, wide), lambda i: (i, 0)),
            pl.BlockSpec((2, tiles_step, NB, 2 * NB), lambda i: (0, i, 0, 0)),
        ],
        out_specs=pl.BlockSpec((2, step, CBLK * NB), lambda i: (0, i, 0)),
        scratch_shapes=[
            pltpu.VMEM((4 * NB, wide), f32),
            pltpu.VMEM((4 * NB, wide), jnp.bfloat16),
            pltpu.VMEM((4 * NB, wide), jnp.bfloat16),
            pltpu.VMEM((3, 2 * NB, 2 * wide), jnp.bfloat16),
            pltpu.VMEM((NB, wide), f32),
        ],
        compiler_params=pltpu.CompilerParams(dimension_semantics=("arbitrary",), vmem_limit_bytes=63 * 1024 * 1024),
        name="finish",
    )(pivots, inverses, fin, wfin, m_raw, ag.reshape(2, row_tiles, NB, 2 * NB))


def grid_of(cols_n):
    nx = 1
    while nx * nx < cols_n:
        nx *= 2
    return nx, cols_n // nx


def solution(mesh):
    rows_n, cols_n = mesh.shape["prow"], mesh.shape["pcol"]
    nx, nz = grid_of(cols_n)

    def body(assembly, slot_tile, pivots, inverses):
        slots = assembly.shape[1]
        cap = (slots + cols_n - 1) // cols_n + 1
        dims = (rows_n, nx, nz, cap, slots // CBLK)
        return per_device(dims, assembly, slot_tile, pivots, inverses)

    in_specs = (P("prow", "pcol", None, None, None), P("prow", "pcol"), P(), P())
    out_specs = P(None, "prow", "pcol")
    return jax.shard_map(body, mesh=mesh, in_specs=in_specs, out_specs=out_specs, check_vma=False)
```

```python
import functools

import jax
import jax.numpy as jnp
from jax import lax
from jax.experimental import pallas as pl
from jax.experimental.pallas import tpu as pltpu
from jax.sharding import PartitionSpec as P

CBLK = 2
NB = 128
CHUNKS = 1
MESH = pl.DeviceIdType.MESH
HI = lax.Precision.HIGHEST


def comm_kernel(
    dims, slot_ref, piv_ref, piv_row, inv_ref, asm_hbm,
    m_hbm, ag_hbm, hh_hbm, hl_hbm, done_hbm, tops_hbm,
    asm, sendb, mid, recvb, labs, mat, pb, ag, st, pk, pr, ps, rb, fin, wfin, h, h_hi, h_lo, done, tops, plan, lab_ref, idx_ref, place,
    out_sem, lab_s, lab_r, a_s, a_r, b_s, b_r, sx_s, sd_s, sr_s, st_r, sc_r, pk_s, pk_r, rs_s, rs_r, t_s, t_r,
    y_s, y_r, k_s, k_r, wb_s, wb_r, g1_s, g1_r, g2_s, g2_r,
):
    rows_n, nx, nz, cap, row_tiles = dims
    cols_n = nx * nz
    sl = NB // rows_n
    half = NB // 2
    me_r = lax.axis_index("prow")
    me_c = lax.axis_index("pcol")
    me_x = me_c // nz
    me_z = me_c % nz

    def remote(src, dst, ssem, rsem, row, col):
        return pltpu.make_async_remote_copy(
            src_ref=src, dst_ref=dst, send_sem=ssem, recv_sem=rsem,
            device_id=(row, col), device_id_type=MESH)

    load = pltpu.make_async_copy(asm_hbm, asm, out_sem.at[6])
    load.start()

    slots = slot_ref.shape[1]
    ident = slot_ref[...]
    column_tile = ident % (CBLK * cols_n)
    target = column_tile % cols_n
    local = ident // (CBLK * cols_n) * CBLK + column_tile // cols_n
    across = jnp.broadcast_to(target, (slots, slots))
    down = across.T
    before = lax.broadcasted_iota(jnp.int32, (slots, slots), 1) < lax.broadcasted_iota(jnp.int32, (slots, slots), 0)
    rank = jnp.sum(jnp.where((across == down) & before, 1, 0), axis=1, keepdims=True)
    position = down[:, 0:1] * cap + rank
    hit = position == lax.broadcasted_iota(jnp.int32, (slots, NB), 1)
    slot_at = lax.broadcasted_iota(jnp.int32, (slots, NB), 0)
    local_at = jnp.broadcast_to(local, (slots, slots)).T[:, 0:1]
    order = jnp.sum(jnp.where(hit, slot_at, 0), axis=0, keepdims=True)
    names = jnp.sum(jnp.where(hit, local_at + 1, 0), axis=0, keepdims=True) - 1
    plan[...] = jnp.broadcast_to(order, (8, NB))
    lab_ref[...] = jnp.broadcast_to(names, (8, NB))
    to_smem = pltpu.make_async_copy(plan, idx_ref, out_sem.at[0])
    to_smem.start()

    barrier = pltpu.get_barrier_semaphore()

    def greet_col(k, c):
        pl.semaphore_signal(barrier, inc=1, device_id=(me_r, (me_c + k) % cols_n), device_id_type=MESH)
        return c

    def greet_row(k, c):
        pl.semaphore_signal(barrier, inc=1, device_id=((me_r + k) % rows_n, me_c), device_id_type=MESH)
        return c

    lax.fori_loop(1, cols_n, greet_col, 0)
    lax.fori_loop(1, rows_n, greet_row, 0)
    pl.semaphore_wait(barrier, cols_n - 1 + rows_n - 1)

    def lab_copy(d):
        return remote(lab_ref, labs.at[me_c], lab_s.at[d], lab_r.at[me_c], me_r, d)

    def lab_start(k, c):
        lab_copy((me_c + k) % cols_n).start()
        return c

    lax.fori_loop(1, cols_n, lab_start, 0)
    labs[me_c] = lab_ref[...]
    to_smem.wait()
    load.wait()

    def first_hop(c, d):
        dx, dz = d // nz, d % nz
        if c == 0:
            return remote(sendb.at[0, d], mid.at[0, me_x * nz + dz], a_s.at[0, d], b_r.at[0, me_x * nz + dz],
                          me_r, dx * nz + me_z)
        return remote(sendb.at[1, d], mid.at[1, dx * nz + me_z], a_s.at[1, d], b_r.at[1, dx * nz + me_z],
                      me_r, me_x * nz + dz)

    def direct(c, d):
        return remote(sendb.at[c, d], recvb.at[c, me_c], a_s.at[c, d], a_r.at[c, me_c], me_r, d)

    def relay_in(c, dx, dz):
        if c == 0:
            sx = (me_x + nx - dx) % nx
            at = sx * nz + (me_z + dz) % nz
            return remote(sendb.at[0, at], mid.at[0, at], b_s.at[0, at], b_r.at[0, at], me_r, sx * nz + me_z)
        sz = (me_z + nz - dz) % nz
        at = (me_x + dx) % nx * nz + sz
        return remote(sendb.at[1, at], mid.at[1, at], b_s.at[1, at], b_r.at[1, at], me_r, me_x * nz + sz)

    def relay_out(c, dx, dz):
        if c == 0:
            sx = (me_x + nx - dx) % nx
            tz = (me_z + dz) % nz
            at = sx * nz + tz
            src = sx * nz + me_z
            return remote(mid.at[0, at], recvb.at[0, src], b_s.at[0, at], a_r.at[0, src], me_r, me_x * nz + tz)
        sz = (me_z + nz - dz) % nz
        tx = (me_x + dx) % nx
        at = tx * nz + sz
        src = me_x * nz + sz
        return remote(mid.at[1, at], recvb.at[1, src], b_s.at[1, at], a_r.at[1, src], me_r, tx * nz + me_z)

    def offset(k):
        return k % (nx - 1) + 1, k // (nx - 1) + 1

    def peer(dx, dz):
        return (me_x + dx) % nx * nz + (me_z + dz) % nz

    def pack_to(dst, d, e):
        for r in range(cap):
            t = idx_ref[0, d * cap + r]
            for c in range(2):
                dst[c, e, r] = asm[t, c]

    def pack(k, c0):
        d = peer(*offset(k))
        pack_to(sendb, d, d)

        @pl.when(k > 0)
        def _():
            p = peer(*offset(jnp.maximum(k - 1, 0)))
            first_hop(0, p).start()
            first_hop(1, p).start()
        return c0

    relays = (nx - 1) * (nz - 1)
    lax.fori_loop(0, relays, pack, 0)
    axis_peers = [(dx, 0) for dx in range(1, nx)] + [(0, dz) for dz in range(1, nz)]
    for n, (dx, dz) in enumerate(axis_peers):
        d = peer(dx, dz)
        pack_to(sendb, d, d)
        if n == 0:
            p = peer(*offset(relays - 1))
            first_hop(0, p).start()
            first_hop(1, p).start()
        else:
            p = peer(*axis_peers[n - 1])
            direct(0, p).start()
            direct(1, p).start()
    pack_to(recvb, me_c, me_c)
    direct(0, peer(*axis_peers[-1])).start()
    direct(1, peer(*axis_peers[-1])).start()

    def relay(k, c0):
        dx, dz = offset(k)
        for c in range(2):
            relay_in(c, dx, dz).wait_recv()
            relay_out(c, dx, dz).start()
        return c0

    lax.fori_loop(0, relays, relay, 0)

    def lab_wait(k, c):
        s = (me_c + k) % cols_n
        remote(lab_ref, labs.at[s], lab_s.at[s], lab_r.at[s], me_r, s).wait_recv()
        return c

    lax.fori_loop(1, cols_n, lab_wait, 0)
    seen = labs[:, 0, :]
    lane = lax.broadcasted_iota(jnp.int32, seen.shape, 1) - me_c * cap
    code = lax.broadcasted_iota(jnp.int32, seen.shape, 0) * cap + lane
    code = jnp.where((lane >= 0) & (lane < cap), code, 0)
    valid = jnp.where((lane >= 0) & (lane < cap), seen, -1)

    def find(t, c):
        place[t] = jnp.minimum(jnp.sum(jnp.where(valid == t, code, 0)), cols_n * cap - 1)
        return c

    lax.fori_loop(0, row_tiles * CBLK, find, 0)

    def a_wait(k, c):
        s = (me_c + k) % cols_n
        for h in range(2):
            remote(sendb.at[h, s], recvb.at[h, s], a_s.at[h, s], a_r.at[h, s], me_r, s).wait_recv()
        return c

    lax.fori_loop(1, cols_n, a_wait, 0)

    def put(i, c):
        rows = pl.ds(pl.multiple_of(i * NB, NB), NB)
        for m in range(CBLK):
            at = place[i * CBLK + m]
            s = at // cap
            r = at - s * cap
            re = recvb[0, s, r]
            im = recvb[1, s, r]
            mat[rows, m * NB:(m + 1) * NB] = re
            mat[rows, (CBLK + m) * NB:(CBLK + m + 1) * NB] = im
            if m == 0:
                pb[i // nz, i % nz, :, 0:NB] = re
                pb[i // nz, i % nz, :, NB:2 * NB] = im
        return c

    lax.fori_loop(0, row_tiles, put, 0)
    m_out = pltpu.make_async_copy(mat, m_hbm, out_sem.at[0])
    m_out.start()

    piece = NB // (2 * CHUNKS)

    def part_rows(kind, ch):
        return pl.ds((kind * CHUNKS + ch) * piece, piece)

    def root(b):
        return b // nz, b % nz

    def out_x(b, ch, dx):
        return remote(pb.at[dx, :, part_rows(0, ch), :], st.at[0, ch, b, pl.ds(0, nz)], sx_s.at[0, ch, dx],
                      st_r.at[0, ch, b], me_r, dx * nz + root(b)[1])

    def out_z(b, ch, dz):
        return remote(pb.at[:, dz, part_rows(1, ch), :], st.at[1, ch, b, pl.ds(0, nx)], sx_s.at[1, ch, dz],
                      st_r.at[1, ch, b], me_r, root(b)[0] * nz + dz)

    def to_tile(b, kind, ch, src, ssem, dx, dz):
        return remote(src, ag.at[b, dx, dz, part_rows(kind, ch), :], ssem, sc_r.at[kind, ch, b], me_r, dx * nz + dz)

    def root_copies(b, ch):
        x0, z0 = root(b)
        copies = []
        for k in range(1, max(nx, nz)):
            if k < nx:
                copies.append(out_x(b, ch, (x0 + k) % nx))
            if k < nz:
                copies.append(out_z(b, ch, (z0 + k) % nz))
        for k in range(1, nz):
            dz = (z0 + k) % nz
            copies.append(to_tile(b, 0, ch, pb.at[x0, dz, part_rows(0, ch), :], sd_s.at[0, ch, dz], x0, dz))
        for k in range(1, nx):
            dx = (x0 + k) % nx
            copies.append(to_tile(b, 1, ch, pb.at[dx, z0, part_rows(1, ch), :], sd_s.at[1, ch, dx], dx, z0))
        return copies

    def relay_x_copies(b, ch):
        z0 = root(b)[1]
        return [to_tile(b, 0, ch, st.at[0, ch, b, (z0 + k) % nz], sr_s.at[0, ch, b, k], me_x, (z0 + k) % nz)
                for k in range(1, nz)]

    def relay_z_copies(b, ch):
        x0 = root(b)[0]
        return [to_tile(b, 1, ch, st.at[1, ch, b, (x0 + k) % nx], sr_s.at[1, ch, b, k], (x0 + k) % nx, me_z)
                for k in range(1, nx)]

    def is_relay_x(b):
        x0, z0 = root(b)
        return (me_z == z0) & (me_x != x0)

    def is_relay_z(b):
        x0, z0 = root(b)
        return (me_x == x0) & (me_z != z0)

    for b in range(2):
        @pl.when(me_c == b)
        def _():
            for ch in range(CHUNKS):
                for copy in root_copies(b, ch):
                    copy.start()
            ag[b, root(b)[0], root(b)[1]] = pb[root(b)[0], root(b)[1]]

    def pass_on(ch):
        for b in range(2):
            x0, z0 = root(b)

            @pl.when(is_relay_x(b))
            def _():
                part = st.at[0, ch, b, pl.ds(0, nz)]
                remote(part, part, sr_s.at[0, ch, b, 0], st_r.at[0, ch, b], me_r, b).wait_recv()
                for copy in relay_x_copies(b, ch):
                    copy.start()
                ag[b, me_x, z0, part_rows(0, ch), :] = st[0, ch, b, z0]

            @pl.when(is_relay_z(b))
            def _():
                part = st.at[1, ch, b, pl.ds(0, nx)]
                remote(part, part, sr_s.at[1, ch, b, 0], st_r.at[1, ch, b], me_r, b).wait_recv()
                for copy in relay_z_copies(b, ch):
                    copy.start()
                ag[b, x0, me_z, part_rows(1, ch), :] = st[1, ch, b, x0]

    def g1x(ch, dx):
        part = ag.at[:, me_x, me_z, part_rows(0, ch), :]
        return remote(part, part, g1_s.at[0, ch, dx], g1_r.at[0, ch, me_x], me_r, dx * nz + me_z)

    def g1z(ch, dz):
        part = ag.at[:, me_x, me_z, part_rows(1, ch), :]
        return remote(part, part, g1_s.at[1, ch, dz], g1_r.at[1, ch, me_z], me_r, me_x * nz + dz)

    def g2z(ch, dz):
        part = ag.at[:, :, me_z, part_rows(0, ch), :]
        return remote(part, part, g2_s.at[0, ch, dz], g2_r.at[0, ch, me_z], me_r, me_x * nz + dz)

    def g2x(ch, dx):
        part = ag.at[:, me_x, :, part_rows(1, ch), :]
        return remote(part, part, g2_s.at[1, ch, dx], g2_r.at[1, ch, me_x], me_r, dx * nz + me_z)

    def gather_first(ch):
        for b in range(2):
            z0 = root(b)[1]

            @pl.when(me_z != z0)
            def _():
                part = ag.at[b, me_x, me_z, part_rows(0, ch), :]
                remote(part, part, sd_s.at[0, ch, 0], sc_r.at[0, ch, b], me_r, me_x * nz + z0).wait_recv()

        for k in range(1, nx):
            g1x(ch, (me_x + k) % nx).start()
        for b in range(2):
            x0 = root(b)[0]

            @pl.when(me_x != x0)
            def _():
                part = ag.at[b, me_x, me_z, part_rows(1, ch), :]
                remote(part, part, sd_s.at[1, ch, 0], sc_r.at[1, ch, b], me_r, x0 * nz + me_z).wait_recv()

        for k in range(1, nz):
            g1z(ch, (me_z + k) % nz).start()

    def gather_second(ch):
        for k in range(1, nx):
            sx = (me_x + k) % nx
            part = ag.at[:, sx, me_z, part_rows(0, ch), :]
            remote(part, part, g1_s.at[0, ch, sx], g1_r.at[0, ch, sx], me_r, sx * nz + me_z).wait_recv()
        for k in range(1, nz):
            g2z(ch, (me_z + k) % nz).start()
        for k in range(1, nz):
            sz = (me_z + k) % nz
            part = ag.at[:, me_x, sz, part_rows(1, ch), :]
            remote(part, part, g1_s.at[1, ch, sz], g1_r.at[1, ch, sz], me_r, me_x * nz + sz).wait_recv()
        for k in range(1, nx):
            g2x(ch, (me_x + k) % nx).start()

    def gather_end(ch):
        for k in range(1, nz):
            sz = (me_z + k) % nz
            part = ag.at[:, :, sz, part_rows(0, ch), :]
            remote(part, part, g2_s.at[0, ch, sz], g2_r.at[0, ch, sz], me_r, me_x * nz + sz).wait_recv()
        for k in range(1, nx):
            sx = (me_x + k) % nx
            part = ag.at[:, sx, :, part_rows(1, ch), :]
            remote(part, part, g2_s.at[1, ch, sx], g2_r.at[1, ch, sx], me_r, sx * nz + me_z).wait_recv()

    def t_copy(s, d):
        rows = pl.ds(pl.multiple_of(d * sl, sl), sl)
        return remote(mat.at[rows, :], fin.at[2 + s, rows, :], t_s.at[d], t_r.at[s], d, me_c)

    for s in range(2):
        @pl.when(me_r == s)
        def _():
            def go(k, c):
                t_copy(s, (s + k) % rows_n).start()
                return c
            lax.fori_loop(1, rows_n, go, 0)
            fin[2 + s, s * sl:(s + 1) * sl, :] = mat[s * sl:(s + 1) * sl, :]

    def pick(d, c):
        def one(jj, c2):
            for k in range(2):
                r = piv_ref[k, d * sl + jj]
                tile = r // NB
                mine = (tile % rows_n) == me_r
                loc = tile // rows_n * NB + r % NB
                row = mat[pl.ds(loc, 1), :]
                pk[d % 2, d // 2, pl.ds(k * sl + jj, 1), :] = jnp.where(mine, row, 0.0)
            return c2
        return lax.fori_loop(0, sl, one, c)

    lax.fori_loop(0, rows_n, pick, 0)
    me_y = me_r // 2
    me_k = me_r % 2
    partner = me_y * 2 + 1 - me_k
    ny = rows_n // 2

    pk_copy = remote(pk.at[1 - me_k], pr, pk_s, pk_r, partner, me_c)
    pk_copy.start()

    pass_on(0)

    remote(pr, pr, pk_s, pk_r, partner, me_c).wait_recv()
    ps[...] = pk[me_k] + pr[...]

    def rs_copy(ty):
        return remote(ps.at[ty], rb.at[me_y], rs_s.at[ty], rs_r.at[me_y], ty * 2 + me_k, me_c)

    for k in range(1, ny):
        rs_copy((me_y + k) % ny).start()

    gather_first(0)
    for ch in range(1, CHUNKS):
        pass_on(ch)

    mine_rows = pl.ds(pl.multiple_of(me_r * sl, sl), sl)
    total = ps[me_y]
    for k in range(1, ny):
        sy = (me_y + k) % ny
        remote(ps.at[sy], rb.at[sy], rs_s.at[sy], rs_r.at[sy], sy * 2 + me_k, me_c).wait_recv()
        total = total + rb[sy]
    fin[0, mine_rows, :] = total[:sl]
    fin[1, mine_rows, :] = total[sl:]
    for s in range(2):
        @pl.when(me_r != s)
        def _():
            part = fin.at[2 + s, mine_rows, :]
            remote(part, part, t_s.at[s], t_r.at[s], s, me_c).wait_recv()

    def wb_copy(b, d):
        part = wfin.at[b, :, mine_rows, :]
        return remote(part, part, wb_s.at[d], wb_r.at[b], me_r, d)

    for b in range(2):
        @pl.when(me_c == b)
        def _():
            wfin[b, :, mine_rows, 0:NB] = fin[:, mine_rows, 0:NB]
            wfin[b, :, mine_rows, NB:2 * NB] = fin[:, mine_rows, CBLK * NB:(CBLK + 1) * NB]

            def go(k, c):
                wb_copy(b, (b + k) % cols_n).start()
                return c
            lax.fori_loop(1, cols_n, go, 0)

    def rows_of(w, r):
        rows = pl.ds(pl.multiple_of(r * sl, sl), sl)
        return wfin.at[:, :, rows, :] if w else fin.at[:, rows, :]

    def y_copy(w, ty):
        part = rows_of(w, me_r)
        return remote(part, part, y_s.at[w, ty], y_r.at[w, me_y], ty * 2 + me_k, me_c)

    def k_copy(w, sy):
        part = rows_of(w, sy * 2 + me_k)
        return remote(part, part, k_s.at[w, sy], k_r.at[w, sy], partner, me_c)

    def y_start(w):
        for k in range(1, ny):
            y_copy(w, (me_y + k) % ny).start()
        k_copy(w, me_y).start()

    def y_pass(w):
        for k in range(1, ny):
            sy = (me_y + k) % ny
            part = rows_of(w, sy * 2 + me_k)
            remote(part, part, y_s.at[w, sy], y_r.at[w, sy], sy * 2 + me_k, me_c).wait_recv()
            k_copy(w, sy).start()

    def y_end(w):
        for sy in range(ny):
            part = rows_of(w, sy * 2 + 1 - me_k)
            remote(part, part, k_s.at[w, sy], k_r.at[w, sy], partner, me_c).wait_recv()

    y_start(0)

    gather_second(0)
    for ch in range(1, CHUNKS):
        gather_first(ch)
        gather_second(ch)

    for b in range(2):
        @pl.when(me_c != b)
        def _():
            part = wfin.at[b, :, mine_rows, :]
            remote(part, part, wb_s.at[b], wb_r.at[b], me_r, b).wait_recv()

    y_start(1)
    y_pass(0)
    y_end(0)
    y_pass(1)
    y_end(1)
    factors(piv_row, inv_ref, fin, wfin, me_c, h, h_hi, h_lo, done, tops)
    small = [pltpu.make_async_copy(v, w, out_sem.at[1 + k]) for k, (v, w) in enumerate(
        ((h_hi, hh_hbm), (h_lo, hl_hbm), (done, done_hbm), (tops, tops_hbm)))]
    for copy in small:
        copy.start()
    for ch in range(CHUNKS):
        gather_end(ch)
    g_out = pltpu.make_async_copy(ag, ag_hbm, out_sem.at[5])
    g_out.start()

    def sent_col(k, c):
        d = (me_c + k) % cols_n
        lab_copy(d).wait_send()
        direct(0, d).wait_send()
        direct(1, d).wait_send()
        return c

    lax.fori_loop(1, cols_n, sent_col, 0)

    def sent_relay(k, c0):
        for c in range(2):
            relay_out(c, *offset(k)).wait_send()
        return c0

    lax.fori_loop(0, relays, sent_relay, 0)
    pk_copy.wait_send()
    for k in range(1, ny):
        rs_copy((me_y + k) % ny).wait_send()
    for w in range(2):
        for k in range(1, ny):
            y_copy(w, (me_y + k) % ny).wait_send()
        for sy in range(ny):
            k_copy(w, sy).wait_send()
    for b in range(2):
        @pl.when(me_c == b)
        def _():
            for ch in range(CHUNKS):
                for copy in root_copies(b, ch):
                    copy.wait_send()

            def go(k, c):
                wb_copy(b, (b + k) % cols_n).wait_send()
                return c
            lax.fori_loop(1, cols_n, go, 0)

        @pl.when(is_relay_x(b))
        def _():
            for ch in range(CHUNKS):
                for copy in relay_x_copies(b, ch):
                    copy.wait_send()

        @pl.when(is_relay_z(b))
        def _():
            for ch in range(CHUNKS):
                for copy in relay_z_copies(b, ch):
                    copy.wait_send()

        @pl.when(me_r == b)
        def _():
            def go(k, c):
                t_copy(b, (b + k) % rows_n).wait_send()
                return c
            lax.fori_loop(1, rows_n, go, 0)
    for ch in range(CHUNKS):
        for k in range(1, nx):
            g1x(ch, (me_x + k) % nx).wait_send()
            g2x(ch, (me_x + k) % nx).wait_send()
        for k in range(1, nz):
            g1z(ch, (me_z + k) % nz).wait_send()
            g2z(ch, (me_z + k) % nz).wait_send()
    m_out.wait()
    for copy in small:
        copy.wait()
    g_out.wait()


def cmat(v):
    h = v.shape[1] // 2
    re, im = v[:, :h], v[:, h:]
    return jnp.concatenate([v, jnp.concatenate([-im, re], 1)], 0)


def dot(a, b):
    return jnp.dot(a, b, precision=HI, preferred_element_type=jnp.float32)


def mm(a, b):
    return jnp.dot(a, b, preferred_element_type=jnp.float32)


def split(v):
    hi = v.astype(jnp.bfloat16)
    return hi, (v - hi.astype(jnp.float32)).astype(jnp.bfloat16)


def finished(own, panel, h_hi, h_lo, my_col):
    wide = own.shape[1]
    hi, lo = split(panel)
    update = mm(hi, h_hi[...]) + (mm(hi, h_lo[...]) + mm(lo, h_hi[...]))
    lane = lax.broadcasted_iota(jnp.int32, own.shape, 1)
    first = ((lane % (wide // 2)) < NB) & (my_col < 2)
    return jnp.where(first, 0.0, own) - update


def factors(piv_ref, inv_ref, fin, wfin, my_col, h, h_hi, h_lo, done, tops):
    wide = fin.shape[2]
    f32 = jnp.float32
    spots = (slice(0, NB), slice(wide // 2, wide // 2 + NB))
    first = jnp.broadcast_to(piv_ref[0:1, :].astype(f32), (NB, NB))
    second = jnp.broadcast_to(piv_ref[1:2, :].astype(f32), (NB, NB)).T
    both = jnp.where(first == second, 1.0, 0.0)
    from_t = dot(both, jnp.concatenate([fin[2], wfin[0, 2], wfin[1, 2]], 1))
    taken = jnp.max(both, axis=1, keepdims=True) > 0
    p1 = jnp.where(taken, from_t, jnp.concatenate([fin[1], wfin[0, 1], wfin[1, 1]], 1))
    i0 = jnp.concatenate([inv_ref[0, 0], inv_ref[0, 1]], 1)
    i1 = jnp.concatenate([inv_ref[1, 0], inv_ref[1, 1]], 1)
    c0 = cmat(fin[0])
    l0p1 = dot(p1[:, wide:wide + 2 * NB], cmat(i0))
    u1 = p1[:, :wide] - dot(l0p1, c0)
    c1 = cmat(u1)
    g = dot(dot(i0, cmat(wfin[1, 0])), cmat(i1))
    h[0:2 * NB] = cmat(dot(i0, c0) - dot(g, c1))
    h[2 * NB:] = cmat(dot(i1, c1))
    tops[0] = fin[0]
    tops[1] = u1

    @pl.when(my_col == 0)
    def _():
        ci = cmat(i0)
        for k, lanes in enumerate(spots):
            h[0:2 * NB, lanes] = -ci[:, k * NB:(k + 1) * NB]
            h[2 * NB:, lanes] = jnp.zeros((2 * NB, NB), f32)
            tops[1, :, lanes] = l0p1[:, k * NB:(k + 1) * NB]

    @pl.when(my_col == 1)
    def _():
        cg = cmat(g)
        ci = cmat(i1)
        for k, lanes in enumerate(spots):
            h[0:2 * NB, lanes] = cg[:, k * NB:(k + 1) * NB]
            h[2 * NB:, lanes] = -ci[:, k * NB:(k + 1) * NB]

    high, low = split(h[...])
    h_hi[...] = high
    h_lo[...] = low
    rest = jnp.concatenate([fin[2], fin[3]], 0)
    panel = jnp.concatenate([jnp.concatenate([wfin[b, 2], wfin[b, 3]], 0) for b in range(2)], 1)
    rest = finished(rest, panel, h_hi, h_lo, my_col)
    high, low = split(rest)
    done[0] = high
    done[1] = low


def finish_kernel(rows_n, tiles_step, piv_ref, h_hi, h_lo, done, tops, m_ref, g_ref, o_ref):
    i = pl.program_id(0)
    my_col = lax.axis_index("pcol")
    my_row = lax.axis_index("prow")
    wide = m_ref.shape[1]
    bf16 = jnp.bfloat16
    step = tiles_step * NB
    r = lax.broadcasted_iota(jnp.int32, (step, NB), 0)
    row = ((i * tiles_step + r // NB) * rows_n + my_row) * NB + r % NB
    moved = row >= 2 * NB
    hit0 = jnp.where((row == piv_ref[0:1, :]) & moved, 1.0, 0.0)
    hit1 = jnp.where((row == piv_ref[1:2, :]) & moved, 1.0, 0.0)
    in0 = jnp.max(hit0, axis=1, keepdims=True)
    in1 = jnp.max(hit1, axis=1, keepdims=True)
    s = jnp.concatenate([hit0 * (1.0 - in1), hit1], 1).astype(bf16)
    swap = mm(s, done[0]) + mm(s, done[1])
    panel = jnp.concatenate([g_ref[0].reshape(step, 2 * NB), g_ref[1].reshape(step, 2 * NB)], 1)
    out = jnp.where(in0 + in1 > 0, swap, finished(m_ref[...], panel, h_hi, h_lo, my_col))
    for c in range(2):
        o_ref[c] = out[:, c * (wide // 2):(c + 1) * (wide // 2)]

    @pl.when((i == 0) & (my_row == 0))
    def _():
        for c in range(2):
            o_ref[c, 0:NB] = tops[0, :, c * (wide // 2):(c + 1) * (wide // 2)]

    @pl.when((i == 0) & (my_row == 1))
    def _():
        for c in range(2):
            o_ref[c, 0:NB] = tops[1, :, c * (wide // 2):(c + 1) * (wide // 2)]


def per_device(dims, assembly, slot_tile, pivots, inverses):
    rows_n, nx, nz, cap, row_tiles = dims
    cols_n = nx * nz
    tiles = assembly[0]
    slots = tiles.shape[0]
    sl = NB // rows_n
    rows = row_tiles * NB
    wide = 2 * CBLK * NB
    f32 = jnp.float32
    dma = pltpu.SemaphoreType.DMA
    hbm = pl.BlockSpec(memory_space=pl.ANY)
    smem = pl.BlockSpec(memory_space=pltpu.SMEM)
    vmem = pl.BlockSpec(memory_space=pltpu.VMEM)
    n = max(nx, nz)
    ny = rows_n // 2
    bf16 = jnp.bfloat16
    m_raw, ag, hh, hl, done, tops = pl.pallas_call(
        functools.partial(comm_kernel, dims),
        out_shape=(
            jax.ShapeDtypeStruct((rows, wide), f32),
            jax.ShapeDtypeStruct((2, nx, nz, NB, 2 * NB), f32),
            jax.ShapeDtypeStruct((4 * NB, wide), bf16),
            jax.ShapeDtypeStruct((4 * NB, wide), bf16),
            jax.ShapeDtypeStruct((2, 2 * NB, wide), bf16),
            jax.ShapeDtypeStruct((2, NB, wide), f32),
        ),
        in_specs=[vmem, smem, vmem, vmem, hbm],
        out_specs=(hbm,) * 6,
        scratch_shapes=[
            pltpu.VMEM((slots, 2, NB, NB), f32),
            pltpu.VMEM((2, cols_n, cap, NB, NB), f32),
            pltpu.VMEM((2, cols_n, cap, NB, NB), f32),
            pltpu.VMEM((2, cols_n, cap, NB, NB), f32),
            pltpu.VMEM((cols_n, 8, 128), jnp.int32),
            pltpu.VMEM((rows, wide), f32),
            pltpu.VMEM((nx, nz, NB, 2 * NB), f32),
            pltpu.VMEM((2, nx, nz, NB, 2 * NB), f32),
            pltpu.VMEM((2, CHUNKS, 2, n, NB // (2 * CHUNKS), 2 * NB), f32),
            pltpu.VMEM((2, ny, 2 * sl, wide), f32),
            pltpu.VMEM((ny, 2 * sl, wide), f32),
            pltpu.VMEM((ny, 2 * sl, wide), f32),
            pltpu.VMEM((ny, 2 * sl, wide), f32),
            pltpu.VMEM((4, NB, wide), f32),
            pltpu.VMEM((2, 4, NB, 2 * NB), f32),
            pltpu.VMEM((4 * NB, wide), f32),
            pltpu.VMEM((4 * NB, wide), bf16),
            pltpu.VMEM((4 * NB, wide), bf16),
            pltpu.VMEM((2, 2 * NB, wide), bf16),
            pltpu.VMEM((2, NB, wide), f32),
            pltpu.VMEM((8, NB), jnp.int32),
            pltpu.VMEM((8, NB), jnp.int32),
            pltpu.SMEM((8, NB), jnp.int32),
            pltpu.SMEM((slots,), jnp.int32),
            dma((7,)),
            dma((cols_n,)), dma((cols_n,)),
            dma((2, cols_n)), dma((2, cols_n)),
            dma((2, cols_n)), dma((2, cols_n)),
            dma((2, CHUNKS, n)), dma((2, CHUNKS, n)), dma((2, CHUNKS, 2, n)), dma((2, CHUNKS, 2)), dma((2, CHUNKS, 2)),
            dma, dma,
            dma((ny,)), dma((ny,)),
            dma((rows_n,)), dma((2,)),
            dma((2, ny)), dma((2, ny)), dma((2, ny)), dma((2, ny)),
            dma((cols_n,)), dma((2,)),
            dma((2, CHUNKS, n)), dma((2, CHUNKS, n)),
            dma((2, CHUNKS, n)), dma((2, CHUNKS, n)),
        ],
        compiler_params=pltpu.CompilerParams(
            collective_id=0, has_side_effects=True, vmem_limit_bytes=63 * 1024 * 1024),
        name="exchange",
    )(slot_tile, pivots, pivots, inverses, tiles)

    tiles_step = 2
    step = tiles_step * NB
    whole = lambda *shape: pl.BlockSpec(shape, lambda i: (0,) * len(shape))
    return pl.pallas_call(
        functools.partial(finish_kernel, rows_n, tiles_step),
        grid=(row_tiles // tiles_step,),
        out_shape=jax.ShapeDtypeStruct((2, rows, CBLK * NB), f32),
        in_specs=[
            whole(2, NB), whole(4 * NB, wide), whole(4 * NB, wide), whole(2, 2 * NB, wide), whole(2, NB, wide),
            pl.BlockSpec((step, wide), lambda i: (i, 0)),
            pl.BlockSpec((2, tiles_step, NB, 2 * NB), lambda i: (0, i, 0, 0)),
        ],
        out_specs=pl.BlockSpec((2, step, CBLK * NB), lambda i: (0, i, 0)),
        compiler_params=pltpu.CompilerParams(dimension_semantics=("arbitrary",), vmem_limit_bytes=63 * 1024 * 1024),
        name="finish",
    )(pivots, hh, hl, done, tops, m_raw, ag.reshape(2, row_tiles, NB, 2 * NB))


def grid_of(cols_n):
    nx = 1
    while nx * nx < cols_n:
        nx *= 2
    return nx, cols_n // nx


def solution(mesh):
    rows_n, cols_n = mesh.shape["prow"], mesh.shape["pcol"]
    nx, nz = grid_of(cols_n)

    def body(assembly, slot_tile, pivots, inverses):
        slots = assembly.shape[1]
        cap = (slots + cols_n - 1) // cols_n + 1
        dims = (rows_n, nx, nz, cap, slots // CBLK)
        return per_device(dims, assembly, slot_tile, pivots, inverses)

    in_specs = (P("prow", "pcol", None, None, None), P("prow", "pcol"), P(), P())
    out_specs = P(None, "prow", "pcol")
    return jax.shard_map(body, mesh=mesh, in_specs=in_specs, out_specs=out_specs, check_vma=False)
```

```python
import functools

import jax
import jax.numpy as jnp
from jax import lax
from jax.experimental import pallas as pl
from jax.experimental.pallas import tpu as pltpu
from jax.sharding import PartitionSpec as P

CBLK = 2
NB = 128
CHUNKS = 1
MESH = pl.DeviceIdType.MESH
HI = lax.Precision.HIGHEST


def comm_kernel(
    dims, slot_ref, piv_ref, piv_row, inv_ref, asm_hbm,
    m_hbm, ag_hbm, right_hbm, tops_hbm,
    asm, sendb, mid, recvb, labs, mat, pb, ag, st, pk, pr, ps, rb, fin, wfin, h, right, tops, plan, lab_ref, idx_ref, place,
    out_sem, lab_s, lab_r, a_s, a_r, b_s, b_r, sx_s, sd_s, sr_s, st_r, sc_r, pk_s, pk_r, rs_s, rs_r, t_s, t_r,
    y_s, y_r, k_s, k_r, wb_s, wb_r, g1_s, g1_r, g2_s, g2_r, g_sem,
):
    rows_n, nx, nz, cap, row_tiles = dims
    cols_n = nx * nz
    sl = NB // rows_n
    half = NB // 2
    me_r = lax.axis_index("prow")
    me_c = lax.axis_index("pcol")
    me_x = me_c // nz
    me_z = me_c % nz

    def remote(src, dst, ssem, rsem, row, col):
        return pltpu.make_async_remote_copy(
            src_ref=src, dst_ref=dst, send_sem=ssem, recv_sem=rsem,
            device_id=(row, col), device_id_type=MESH)

    load = pltpu.make_async_copy(asm_hbm, asm, out_sem.at[6])
    load.start()

    slots = slot_ref.shape[1]
    ident = slot_ref[...]
    column_tile = ident % (CBLK * cols_n)
    target = column_tile % cols_n
    local = ident // (CBLK * cols_n) * CBLK + column_tile // cols_n
    across = jnp.broadcast_to(target, (slots, slots))
    down = across.T
    before = lax.broadcasted_iota(jnp.int32, (slots, slots), 1) < lax.broadcasted_iota(jnp.int32, (slots, slots), 0)
    rank = jnp.sum(jnp.where((across == down) & before, 1, 0), axis=1, keepdims=True)
    position = down[:, 0:1] * cap + rank
    hit = position == lax.broadcasted_iota(jnp.int32, (slots, NB), 1)
    slot_at = lax.broadcasted_iota(jnp.int32, (slots, NB), 0)
    local_at = jnp.broadcast_to(local, (slots, slots)).T[:, 0:1]
    order = jnp.sum(jnp.where(hit, slot_at, 0), axis=0, keepdims=True)
    names = jnp.sum(jnp.where(hit, local_at + 1, 0), axis=0, keepdims=True) - 1
    plan[...] = jnp.broadcast_to(order, (8, NB))
    lab_ref[...] = jnp.broadcast_to(names, (8, NB))
    to_smem = pltpu.make_async_copy(plan, idx_ref, out_sem.at[0])
    to_smem.start()

    barrier = pltpu.get_barrier_semaphore()

    def greet_col(k, c):
        pl.semaphore_signal(barrier, inc=1, device_id=(me_r, (me_c + k) % cols_n), device_id_type=MESH)
        return c

    def greet_row(k, c):
        pl.semaphore_signal(barrier, inc=1, device_id=((me_r + k) % rows_n, me_c), device_id_type=MESH)
        return c

    lax.fori_loop(1, cols_n, greet_col, 0)
    lax.fori_loop(1, rows_n, greet_row, 0)
    pl.semaphore_wait(barrier, cols_n - 1 + rows_n - 1)

    def lab_copy(d):
        return remote(lab_ref, labs.at[me_c], lab_s.at[d], lab_r.at[me_c], me_r, d)

    def lab_start(k, c):
        lab_copy((me_c + k) % cols_n).start()
        return c

    lax.fori_loop(1, cols_n, lab_start, 0)
    labs[me_c] = lab_ref[...]
    to_smem.wait()
    load.wait()

    def first_hop(c, d):
        dx, dz = d // nz, d % nz
        if c == 0:
            return remote(sendb.at[0, d], mid.at[0, me_x * nz + dz], a_s.at[0, d], b_r.at[0, me_x * nz + dz],
                          me_r, dx * nz + me_z)
        return remote(sendb.at[1, d], mid.at[1, dx * nz + me_z], a_s.at[1, d], b_r.at[1, dx * nz + me_z],
                      me_r, me_x * nz + dz)

    def direct(c, d):
        return remote(sendb.at[c, d], recvb.at[c, me_c], a_s.at[c, d], a_r.at[c, me_c], me_r, d)

    def relay_in(c, dx, dz):
        if c == 0:
            sx = (me_x + nx - dx) % nx
            at = sx * nz + (me_z + dz) % nz
            return remote(sendb.at[0, at], mid.at[0, at], b_s.at[0, at], b_r.at[0, at], me_r, sx * nz + me_z)
        sz = (me_z + nz - dz) % nz
        at = (me_x + dx) % nx * nz + sz
        return remote(sendb.at[1, at], mid.at[1, at], b_s.at[1, at], b_r.at[1, at], me_r, me_x * nz + sz)

    def relay_out(c, dx, dz):
        if c == 0:
            sx = (me_x + nx - dx) % nx
            tz = (me_z + dz) % nz
            at = sx * nz + tz
            src = sx * nz + me_z
            return remote(mid.at[0, at], recvb.at[0, src], b_s.at[0, at], a_r.at[0, src], me_r, me_x * nz + tz)
        sz = (me_z + nz - dz) % nz
        tx = (me_x + dx) % nx
        at = tx * nz + sz
        src = me_x * nz + sz
        return remote(mid.at[1, at], recvb.at[1, src], b_s.at[1, at], a_r.at[1, src], me_r, tx * nz + me_z)

    def offset(k):
        return k % (nx - 1) + 1, k // (nx - 1) + 1

    def peer(dx, dz):
        return (me_x + dx) % nx * nz + (me_z + dz) % nz

    def pack_to(dst, d, e):
        for r in range(cap):
            t = idx_ref[0, d * cap + r]
            for c in range(2):
                dst[c, e, r] = asm[t, c]

    def pack(k, c0):
        d = peer(*offset(k))
        pack_to(sendb, d, d)

        @pl.when(k > 0)
        def _():
            p = peer(*offset(jnp.maximum(k - 1, 0)))
            first_hop(0, p).start()
            first_hop(1, p).start()
        return c0

    relays = (nx - 1) * (nz - 1)
    lax.fori_loop(0, relays, pack, 0)
    axis_peers = [(dx, 0) for dx in range(1, nx)] + [(0, dz) for dz in range(1, nz)]
    for n, (dx, dz) in enumerate(axis_peers):
        d = peer(dx, dz)
        pack_to(sendb, d, d)
        if n == 0:
            p = peer(*offset(relays - 1))
            first_hop(0, p).start()
            first_hop(1, p).start()
        else:
            p = peer(*axis_peers[n - 1])
            direct(0, p).start()
            direct(1, p).start()
    pack_to(recvb, me_c, me_c)
    direct(0, peer(*axis_peers[-1])).start()
    direct(1, peer(*axis_peers[-1])).start()

    def relay(k, c0):
        dx, dz = offset(k)
        for c in range(2):
            relay_in(c, dx, dz).wait_recv()
            relay_out(c, dx, dz).start()
        return c0

    lax.fori_loop(0, relays, relay, 0)

    def lab_wait(k, c):
        s = (me_c + k) % cols_n
        remote(lab_ref, labs.at[s], lab_s.at[s], lab_r.at[s], me_r, s).wait_recv()
        return c

    lax.fori_loop(1, cols_n, lab_wait, 0)
    seen = labs[:, 0, :]
    lane = lax.broadcasted_iota(jnp.int32, seen.shape, 1) - me_c * cap
    code = lax.broadcasted_iota(jnp.int32, seen.shape, 0) * cap + lane
    code = jnp.where((lane >= 0) & (lane < cap), code, 0)
    valid = jnp.where((lane >= 0) & (lane < cap), seen, -1)

    def find(t, c):
        place[t] = jnp.minimum(jnp.sum(jnp.where(valid == t, code, 0)), cols_n * cap - 1)
        return c

    lax.fori_loop(0, row_tiles * CBLK, find, 0)

    def a_wait(k, c):
        s = (me_c + k) % cols_n
        for h in range(2):
            remote(sendb.at[h, s], recvb.at[h, s], a_s.at[h, s], a_r.at[h, s], me_r, s).wait_recv()
        return c

    lax.fori_loop(1, cols_n, a_wait, 0)

    def put(i, c):
        rows = pl.ds(pl.multiple_of(i * NB, NB), NB)
        for m in range(CBLK):
            at = place[i * CBLK + m]
            s = at // cap
            r = at - s * cap
            re = recvb[0, s, r]
            im = recvb[1, s, r]
            mat[rows, m * NB:(m + 1) * NB] = re
            mat[rows, (CBLK + m) * NB:(CBLK + m + 1) * NB] = im
            if m == 0:
                pb[i // nz, i % nz, :, 0:NB] = re
                pb[i // nz, i % nz, :, NB:2 * NB] = im
        return c

    lax.fori_loop(0, row_tiles, put, 0)
    m_out = pltpu.make_async_copy(mat, m_hbm, out_sem.at[0])
    m_out.start()

    piece = NB // (2 * CHUNKS)

    def part_rows(kind, ch):
        return pl.ds((kind * CHUNKS + ch) * piece, piece)

    def root(b):
        return b // nz, b % nz

    def out_x(b, ch, dx):
        return remote(pb.at[dx, :, part_rows(0, ch), :], st.at[0, ch, b, pl.ds(0, nz)], sx_s.at[0, ch, dx],
                      st_r.at[0, ch, b], me_r, dx * nz + root(b)[1])

    def out_z(b, ch, dz):
        return remote(pb.at[:, dz, part_rows(1, ch), :], st.at[1, ch, b, pl.ds(0, nx)], sx_s.at[1, ch, dz],
                      st_r.at[1, ch, b], me_r, root(b)[0] * nz + dz)

    def to_tile(b, kind, ch, src, ssem, dx, dz):
        return remote(src, ag.at[b, dx, dz, part_rows(kind, ch), :], ssem, sc_r.at[kind, ch, b], me_r, dx * nz + dz)

    def root_copies(b, ch):
        x0, z0 = root(b)
        copies = []
        for k in range(1, max(nx, nz)):
            if k < nx:
                copies.append(out_x(b, ch, (x0 + k) % nx))
            if k < nz:
                copies.append(out_z(b, ch, (z0 + k) % nz))
        for k in range(1, nz):
            dz = (z0 + k) % nz
            copies.append(to_tile(b, 0, ch, pb.at[x0, dz, part_rows(0, ch), :], sd_s.at[0, ch, dz], x0, dz))
        for k in range(1, nx):
            dx = (x0 + k) % nx
            copies.append(to_tile(b, 1, ch, pb.at[dx, z0, part_rows(1, ch), :], sd_s.at[1, ch, dx], dx, z0))
        return copies

    def relay_x_copies(b, ch):
        z0 = root(b)[1]
        return [to_tile(b, 0, ch, st.at[0, ch, b, (z0 + k) % nz], sr_s.at[0, ch, b, k], me_x, (z0 + k) % nz)
                for k in range(1, nz)]

    def relay_z_copies(b, ch):
        x0 = root(b)[0]
        return [to_tile(b, 1, ch, st.at[1, ch, b, (x0 + k) % nx], sr_s.at[1, ch, b, k], (x0 + k) % nx, me_z)
                for k in range(1, nx)]

    def is_relay_x(b):
        x0, z0 = root(b)
        return (me_z == z0) & (me_x != x0)

    def is_relay_z(b):
        x0, z0 = root(b)
        return (me_x == x0) & (me_z != z0)

    for b in range(2):
        @pl.when(me_c == b)
        def _():
            for ch in range(CHUNKS):
                for copy in root_copies(b, ch):
                    copy.start()
            ag[b, root(b)[0], root(b)[1]] = pb[root(b)[0], root(b)[1]]

    def pass_on(ch):
        for b in range(2):
            x0, z0 = root(b)

            @pl.when(is_relay_x(b))
            def _():
                part = st.at[0, ch, b, pl.ds(0, nz)]
                remote(part, part, sr_s.at[0, ch, b, 0], st_r.at[0, ch, b], me_r, b).wait_recv()
                for copy in relay_x_copies(b, ch):
                    copy.start()
                ag[b, me_x, z0, part_rows(0, ch), :] = st[0, ch, b, z0]

            @pl.when(is_relay_z(b))
            def _():
                part = st.at[1, ch, b, pl.ds(0, nx)]
                remote(part, part, sr_s.at[1, ch, b, 0], st_r.at[1, ch, b], me_r, b).wait_recv()
                for copy in relay_z_copies(b, ch):
                    copy.start()
                ag[b, x0, me_z, part_rows(1, ch), :] = st[1, ch, b, x0]

    def g1x(ch, dx):
        part = ag.at[:, me_x, me_z, part_rows(0, ch), :]
        return remote(part, part, g1_s.at[0, ch, dx], g1_r.at[0, ch, me_x], me_r, dx * nz + me_z)

    def g1z(ch, dz):
        part = ag.at[:, me_x, me_z, part_rows(1, ch), :]
        return remote(part, part, g1_s.at[1, ch, dz], g1_r.at[1, ch, me_z], me_r, me_x * nz + dz)

    def g2z(ch, dz):
        part = ag.at[:, :, me_z, part_rows(0, ch), :]
        return remote(part, part, g2_s.at[0, ch, dz], g2_r.at[0, ch, me_z], me_r, me_x * nz + dz)

    def g2x(ch, dx):
        part = ag.at[:, me_x, :, part_rows(1, ch), :]
        return remote(part, part, g2_s.at[1, ch, dx], g2_r.at[1, ch, me_x], me_r, dx * nz + me_z)

    def gather_first(ch):
        for b in range(2):
            z0 = root(b)[1]

            @pl.when(me_z != z0)
            def _():
                part = ag.at[b, me_x, me_z, part_rows(0, ch), :]
                remote(part, part, sd_s.at[0, ch, 0], sc_r.at[0, ch, b], me_r, me_x * nz + z0).wait_recv()

        for k in range(1, nx):
            g1x(ch, (me_x + k) % nx).start()
        for b in range(2):
            x0 = root(b)[0]

            @pl.when(me_x != x0)
            def _():
                part = ag.at[b, me_x, me_z, part_rows(1, ch), :]
                remote(part, part, sd_s.at[1, ch, 0], sc_r.at[1, ch, b], me_r, x0 * nz + me_z).wait_recv()

        for k in range(1, nz):
            g1z(ch, (me_z + k) % nz).start()

    def gather_second(ch):
        for k in range(1, nx):
            sx = (me_x + k) % nx
            part = ag.at[:, sx, me_z, part_rows(0, ch), :]
            remote(part, part, g1_s.at[0, ch, sx], g1_r.at[0, ch, sx], me_r, sx * nz + me_z).wait_recv()
        for k in range(1, nz):
            g2z(ch, (me_z + k) % nz).start()
        for k in range(1, nz):
            sz = (me_z + k) % nz
            part = ag.at[:, me_x, sz, part_rows(1, ch), :]
            remote(part, part, g1_s.at[1, ch, sz], g1_r.at[1, ch, sz], me_r, me_x * nz + sz).wait_recv()
        for k in range(1, nx):
            g2x(ch, (me_x + k) % nx).start()

    def t_copy(s, d):
        rows = pl.ds(pl.multiple_of(d * sl, sl), sl)
        return remote(mat.at[rows, :], fin.at[2 + s, rows, :], t_s.at[d], t_r.at[s], d, me_c)

    for s in range(2):
        @pl.when(me_r == s)
        def _():
            def go(k, c):
                t_copy(s, (s + k) % rows_n).start()
                return c
            lax.fori_loop(1, rows_n, go, 0)
            fin[2 + s, s * sl:(s + 1) * sl, :] = mat[s * sl:(s + 1) * sl, :]

    def pick(d, c):
        def one(jj, c2):
            for k in range(2):
                r = piv_ref[k, d * sl + jj]
                tile = r // NB
                mine = (tile % rows_n) == me_r
                loc = tile // rows_n * NB + r % NB
                row = mat[pl.ds(loc, 1), :]
                pk[d % 2, d // 2, pl.ds(k * sl + jj, 1), :] = jnp.where(mine, row, 0.0)
            return c2
        return lax.fori_loop(0, sl, one, c)

    lax.fori_loop(0, rows_n, pick, 0)
    me_y = me_r // 2
    me_k = me_r % 2
    partner = me_y * 2 + 1 - me_k
    ny = rows_n // 2

    pk_copy = remote(pk.at[1 - me_k], pr, pk_s, pk_r, partner, me_c)
    pk_copy.start()

    pass_on(0)

    remote(pr, pr, pk_s, pk_r, partner, me_c).wait_recv()
    ps[...] = pk[me_k] + pr[...]

    def rs_copy(ty):
        return remote(ps.at[ty], rb.at[me_y], rs_s.at[ty], rs_r.at[me_y], ty * 2 + me_k, me_c)

    for k in range(1, ny):
        rs_copy((me_y + k) % ny).start()

    gather_first(0)
    for ch in range(1, CHUNKS):
        pass_on(ch)

    mine_rows = pl.ds(pl.multiple_of(me_r * sl, sl), sl)
    total = ps[me_y]
    for k in range(1, ny):
        sy = (me_y + k) % ny
        remote(ps.at[sy], rb.at[sy], rs_s.at[sy], rs_r.at[sy], sy * 2 + me_k, me_c).wait_recv()
        total = total + rb[sy]
    fin[0, mine_rows, :] = total[:sl]
    fin[1, mine_rows, :] = total[sl:]
    for s in range(2):
        @pl.when(me_r != s)
        def _():
            part = fin.at[2 + s, mine_rows, :]
            remote(part, part, t_s.at[s], t_r.at[s], s, me_c).wait_recv()

    def wb_copy(b, d):
        part = wfin.at[b, :, mine_rows, :]
        return remote(part, part, wb_s.at[b, d], wb_r.at[b], me_r, d)

    def wb_root(b):
        x0, z0 = root(b)
        return ([wb_copy(b, (x0 + k) % nx * nz + z0) for k in range(1, nx)]
                + [wb_copy(b, x0 * nz + (z0 + k) % nz) for k in range(1, nz)])

    def wb_pass(b):
        z0 = root(b)[1]
        return [wb_copy(b, me_x * nz + (z0 + k) % nz) for k in range(1, nz)]

    for b in range(2):
        @pl.when(me_c == b)
        def _():
            wfin[b, :, mine_rows, 0:NB] = fin[:, mine_rows, 0:NB]
            wfin[b, :, mine_rows, NB:2 * NB] = fin[:, mine_rows, CBLK * NB:(CBLK + 1) * NB]

            for copy in wb_root(b):
                copy.start()

    def rows_of(w, r):
        rows = pl.ds(pl.multiple_of(r * sl, sl), sl)
        return wfin.at[:, :, rows, :] if w else fin.at[:, rows, :]

    def y_copy(w, ty):
        part = rows_of(w, me_r)
        return remote(part, part, y_s.at[w, ty], y_r.at[w, me_y], ty * 2 + me_k, me_c)

    def k_copy(w, sy):
        part = rows_of(w, sy * 2 + me_k)
        return remote(part, part, k_s.at[w, sy], k_r.at[w, sy], partner, me_c)

    def y_start(w):
        for k in range(1, ny):
            y_copy(w, (me_y + k) % ny).start()
        k_copy(w, me_y).start()

    def y_pass(w):
        for k in range(1, ny):
            sy = (me_y + k) % ny
            part = rows_of(w, sy * 2 + me_k)
            remote(part, part, y_s.at[w, sy], y_r.at[w, sy], sy * 2 + me_k, me_c).wait_recv()
            k_copy(w, sy).start()

    def y_end(w):
        for sy in range(ny):
            part = rows_of(w, sy * 2 + 1 - me_k)
            remote(part, part, k_s.at[w, sy], k_r.at[w, sy], partner, me_c).wait_recv()

    y_start(0)

    def wb_wait(b):
        part = wfin.at[b, :, mine_rows, :]
        remote(part, part, wb_s.at[b, 0], wb_r.at[b], me_r, b).wait_recv()

    for b in range(2):
        @pl.when(is_relay_x(b))
        def _():
            wb_wait(b)
            for copy in wb_pass(b):
                copy.start()

    gather_second(0)
    for ch in range(1, CHUNKS):
        gather_first(ch)
        gather_second(ch)

    for b in range(2):
        @pl.when((me_c != b) & jnp.logical_not(is_relay_x(b)))
        def _():
            wb_wait(b)

    y_start(1)
    y_pass(0)
    y_end(0)
    y_pass(1)
    y_end(1)
    factors(piv_row, inv_ref, fin, wfin, me_c, h, right, tops)
    small = [pltpu.make_async_copy(v, w, out_sem.at[1 + k]) for k, (v, w) in enumerate(
        ((right, right_hbm), (tops, tops_hbm)))]
    for copy in small:
        copy.start()
    outs = []
    for k in range(nz):
        sz = (me_z + k) % nz
        part = ag.at[:, :, sz, part_rows(0, 0), :]
        if k > 0:
            remote(part, part, g2_s.at[0, 0, sz], g2_r.at[0, 0, sz], me_r, me_x * nz + sz).wait_recv()
        outs.append(pltpu.make_async_copy(part, ag_hbm.at[:, :, sz, part_rows(0, 0), :], g_sem.at[0, k]))
        outs[-1].start()
        if k < nx:
            sx = (me_x + k) % nx
            part = ag.at[:, sx, :, part_rows(1, 0), :]
            if k > 0:
                remote(part, part, g2_s.at[1, 0, sx], g2_r.at[1, 0, sx], me_r, sx * nz + me_z).wait_recv()
            outs.append(pltpu.make_async_copy(part, ag_hbm.at[:, sx, :, part_rows(1, 0), :], g_sem.at[1, k]))
            outs[-1].start()

    def sent_col(k, c):
        d = (me_c + k) % cols_n
        lab_copy(d).wait_send()
        direct(0, d).wait_send()
        direct(1, d).wait_send()
        return c

    lax.fori_loop(1, cols_n, sent_col, 0)

    def sent_relay(k, c0):
        for c in range(2):
            relay_out(c, *offset(k)).wait_send()
        return c0

    lax.fori_loop(0, relays, sent_relay, 0)
    pk_copy.wait_send()
    for k in range(1, ny):
        rs_copy((me_y + k) % ny).wait_send()
    for w in range(2):
        for k in range(1, ny):
            y_copy(w, (me_y + k) % ny).wait_send()
        for sy in range(ny):
            k_copy(w, sy).wait_send()
    for b in range(2):
        @pl.when(me_c == b)
        def _():
            for ch in range(CHUNKS):
                for copy in root_copies(b, ch):
                    copy.wait_send()

            for copy in wb_root(b):
                copy.wait_send()

        @pl.when(is_relay_x(b))
        def _():
            for copy in wb_pass(b):
                copy.wait_send()

        @pl.when(is_relay_x(b))
        def _():
            for ch in range(CHUNKS):
                for copy in relay_x_copies(b, ch):
                    copy.wait_send()

        @pl.when(is_relay_z(b))
        def _():
            for ch in range(CHUNKS):
                for copy in relay_z_copies(b, ch):
                    copy.wait_send()

        @pl.when(me_r == b)
        def _():
            def go(k, c):
                t_copy(b, (b + k) % rows_n).wait_send()
                return c
            lax.fori_loop(1, rows_n, go, 0)
    for ch in range(CHUNKS):
        for k in range(1, nx):
            g1x(ch, (me_x + k) % nx).wait_send()
            g2x(ch, (me_x + k) % nx).wait_send()
        for k in range(1, nz):
            g1z(ch, (me_z + k) % nz).wait_send()
            g2z(ch, (me_z + k) % nz).wait_send()
    m_out.wait()
    for copy in small:
        copy.wait()
    for copy in outs:
        copy.wait()


def cmat(v):
    h = v.shape[1] // 2
    re, im = v[:, :h], v[:, h:]
    return jnp.concatenate([v, jnp.concatenate([-im, re], 1)], 0)


def dot(a, b):
    return jnp.dot(a, b, precision=HI, preferred_element_type=jnp.float32)


def mm(a, b):
    return jnp.dot(a, b, preferred_element_type=jnp.float32)


def split(v):
    hi = v.astype(jnp.bfloat16)
    return hi, (v - hi.astype(jnp.float32)).astype(jnp.bfloat16)


def deep(panel):
    hi, lo = split(panel)
    return jnp.concatenate([hi, hi, lo], 1)


def keep(own, my_col):
    lane = lax.broadcasted_iota(jnp.int32, own.shape, 1)
    first = ((lane % (own.shape[1] // 2)) < NB) & (my_col < 2)
    return jnp.where(first, 0.0, own)


def factors(piv_ref, inv_ref, fin, wfin, my_col, h, right, tops):
    wide = fin.shape[2]
    f32 = jnp.float32
    spots = (slice(0, NB), slice(wide // 2, wide // 2 + NB))
    first = jnp.broadcast_to(piv_ref[0:1, :].astype(f32), (NB, NB))
    second = jnp.broadcast_to(piv_ref[1:2, :].astype(f32), (NB, NB)).T
    both = jnp.where(first == second, 1.0, 0.0)
    from_t = dot(both, jnp.concatenate([fin[2], wfin[0, 2], wfin[1, 2]], 1))
    taken = jnp.max(both, axis=1, keepdims=True) > 0
    p1 = jnp.where(taken, from_t, jnp.concatenate([fin[1], wfin[0, 1], wfin[1, 1]], 1))
    i0 = jnp.concatenate([inv_ref[0, 0], inv_ref[0, 1]], 1)
    i1 = jnp.concatenate([inv_ref[1, 0], inv_ref[1, 1]], 1)
    c0 = cmat(fin[0])
    l0p1 = dot(p1[:, wide:wide + 2 * NB], cmat(i0))
    u1 = p1[:, :wide] - dot(l0p1, c0)
    c1 = cmat(u1)
    g = dot(dot(i0, cmat(wfin[1, 0])), cmat(i1))
    h[0:2 * NB] = cmat(dot(i0, c0) - dot(g, c1))
    h[2 * NB:] = cmat(dot(i1, c1))
    tops[0] = fin[0]
    tops[1] = u1

    @pl.when(my_col == 0)
    def _():
        ci = cmat(i0)
        for k, lanes in enumerate(spots):
            h[0:2 * NB, lanes] = -ci[:, k * NB:(k + 1) * NB]
            h[2 * NB:, lanes] = jnp.zeros((2 * NB, NB), f32)
            tops[1, :, lanes] = l0p1[:, k * NB:(k + 1) * NB]

    @pl.when(my_col == 1)
    def _():
        cg = cmat(g)
        ci = cmat(i1)
        for k, lanes in enumerate(spots):
            h[0:2 * NB, lanes] = cg[:, k * NB:(k + 1) * NB]
            h[2 * NB:, lanes] = -ci[:, k * NB:(k + 1) * NB]

    high, low = split(-h[...])
    right[0:wide] = high
    right[wide:2 * wide] = low
    right[2 * wide:3 * wide] = high
    rest = jnp.concatenate([fin[2], fin[3]], 0)
    panel = jnp.concatenate([jnp.concatenate([wfin[b, 2], wfin[b, 3]], 0) for b in range(2)], 1)
    rest = keep(rest, my_col) + mm(deep(panel), right[0:3 * wide])
    high, low = split(rest)
    right[3 * wide:3 * wide + 2 * NB] = high
    right[3 * wide + 2 * NB:] = low


def finish_kernel(rows_n, tiles_step, piv_ref, right, tops, m_ref, g_ref, o_ref):
    i = pl.program_id(0)
    my_col = lax.axis_index("pcol")
    my_row = lax.axis_index("prow")
    wide = m_ref.shape[1]
    bf16 = jnp.bfloat16
    step = tiles_step * NB
    r = lax.broadcasted_iota(jnp.int32, (step, NB), 0)
    row = ((i * tiles_step + r // NB) * rows_n + my_row) * NB + r % NB
    moved = row >= 2 * NB
    hit0 = jnp.where((row == piv_ref[0:1, :]) & moved, 1.0, 0.0)
    hit1 = jnp.where((row == piv_ref[1:2, :]) & moved, 1.0, 0.0)
    in0 = jnp.max(hit0, axis=1, keepdims=True)
    in1 = jnp.max(hit1, axis=1, keepdims=True)
    s = jnp.concatenate([hit0 * (1.0 - in1), hit1], 1).astype(bf16)
    panel = jnp.concatenate([g_ref[0].reshape(step, 2 * NB), g_ref[1].reshape(step, 2 * NB)], 1)
    still = in0 + in1 == 0
    left = jnp.concatenate([deep(jnp.where(still, panel, 0.0)), s, s], 1)
    out = jnp.where(still, keep(m_ref[...], my_col), 0.0) + mm(left, right[...])
    for c in range(2):
        o_ref[c] = out[:, c * (wide // 2):(c + 1) * (wide // 2)]

    @pl.when((i == 0) & (my_row == 0))
    def _():
        for c in range(2):
            o_ref[c, 0:NB] = tops[0, :, c * (wide // 2):(c + 1) * (wide // 2)]

    @pl.when((i == 0) & (my_row == 1))
    def _():
        for c in range(2):
            o_ref[c, 0:NB] = tops[1, :, c * (wide // 2):(c + 1) * (wide // 2)]


def per_device(dims, assembly, slot_tile, pivots, inverses):
    rows_n, nx, nz, cap, row_tiles = dims
    cols_n = nx * nz
    tiles = assembly[0]
    slots = tiles.shape[0]
    sl = NB // rows_n
    rows = row_tiles * NB
    wide = 2 * CBLK * NB
    f32 = jnp.float32
    dma = pltpu.SemaphoreType.DMA
    hbm = pl.BlockSpec(memory_space=pl.ANY)
    smem = pl.BlockSpec(memory_space=pltpu.SMEM)
    vmem = pl.BlockSpec(memory_space=pltpu.VMEM)
    n = max(nx, nz)
    ny = rows_n // 2
    bf16 = jnp.bfloat16
    m_raw, ag, right, tops = pl.pallas_call(
        functools.partial(comm_kernel, dims),
        out_shape=(
            jax.ShapeDtypeStruct((rows, wide), f32),
            jax.ShapeDtypeStruct((2, nx, nz, NB, 2 * NB), f32),
            jax.ShapeDtypeStruct((3 * wide + 4 * NB, wide), bf16),
            jax.ShapeDtypeStruct((2, NB, wide), f32),
        ),
        in_specs=[vmem, smem, vmem, vmem, hbm],
        out_specs=(hbm,) * 4,
        scratch_shapes=[
            pltpu.VMEM((slots, 2, NB, NB), f32),
            pltpu.VMEM((2, cols_n, cap, NB, NB), f32),
            pltpu.VMEM((2, cols_n, cap, NB, NB), f32),
            pltpu.VMEM((2, cols_n, cap, NB, NB), f32),
            pltpu.VMEM((cols_n, 8, 128), jnp.int32),
            pltpu.VMEM((rows, wide), f32),
            pltpu.VMEM((nx, nz, NB, 2 * NB), f32),
            pltpu.VMEM((2, nx, nz, NB, 2 * NB), f32),
            pltpu.VMEM((2, CHUNKS, 2, n, NB // (2 * CHUNKS), 2 * NB), f32),
            pltpu.VMEM((2, ny, 2 * sl, wide), f32),
            pltpu.VMEM((ny, 2 * sl, wide), f32),
            pltpu.VMEM((ny, 2 * sl, wide), f32),
            pltpu.VMEM((ny, 2 * sl, wide), f32),
            pltpu.VMEM((4, NB, wide), f32),
            pltpu.VMEM((2, 4, NB, 2 * NB), f32),
            pltpu.VMEM((4 * NB, wide), f32),
            pltpu.VMEM((3 * wide + 4 * NB, wide), bf16),
            pltpu.VMEM((2, NB, wide), f32),
            pltpu.VMEM((8, NB), jnp.int32),
            pltpu.VMEM((8, NB), jnp.int32),
            pltpu.SMEM((8, NB), jnp.int32),
            pltpu.SMEM((slots,), jnp.int32),
            dma((7,)),
            dma((cols_n,)), dma((cols_n,)),
            dma((2, cols_n)), dma((2, cols_n)),
            dma((2, cols_n)), dma((2, cols_n)),
            dma((2, CHUNKS, n)), dma((2, CHUNKS, n)), dma((2, CHUNKS, 2, n)), dma((2, CHUNKS, 2)), dma((2, CHUNKS, 2)),
            dma, dma,
            dma((ny,)), dma((ny,)),
            dma((rows_n,)), dma((2,)),
            dma((2, ny)), dma((2, ny)), dma((2, ny)), dma((2, ny)),
            dma((2, cols_n)), dma((2,)),
            dma((2, CHUNKS, n)), dma((2, CHUNKS, n)),
            dma((2, CHUNKS, n)), dma((2, CHUNKS, n)),
            dma((2, n)),
        ],
        compiler_params=pltpu.CompilerParams(
            collective_id=0, has_side_effects=True, vmem_limit_bytes=63 * 1024 * 1024),
        name="exchange",
    )(slot_tile, pivots, pivots, inverses, tiles)

    tiles_step = 4
    step = tiles_step * NB
    whole = lambda *shape: pl.BlockSpec(shape, lambda i: (0,) * len(shape))
    return pl.pallas_call(
        functools.partial(finish_kernel, rows_n, tiles_step),
        grid=(row_tiles // tiles_step,),
        out_shape=jax.ShapeDtypeStruct((2, rows, CBLK * NB), f32),
        in_specs=[
            whole(2, NB), whole(3 * wide + 4 * NB, wide), whole(2, NB, wide),
            pl.BlockSpec((step, wide), lambda i: (i, 0)),
            pl.BlockSpec((2, tiles_step, NB, 2 * NB), lambda i: (0, i, 0, 0)),
        ],
        out_specs=pl.BlockSpec((2, step, CBLK * NB), lambda i: (0, i, 0)),
        compiler_params=pltpu.CompilerParams(dimension_semantics=("arbitrary",), vmem_limit_bytes=63 * 1024 * 1024),
        name="finish",
    )(pivots, right, tops, m_raw, ag.reshape(2, row_tiles, NB, 2 * NB))


def grid_of(cols_n):
    nx = 1
    while nx * nx < cols_n:
        nx *= 2
    return nx, cols_n // nx


def solution(mesh):
    rows_n, cols_n = mesh.shape["prow"], mesh.shape["pcol"]
    nx, nz = grid_of(cols_n)

    def body(assembly, slot_tile, pivots, inverses):
        slots = assembly.shape[1]
        cap = (slots + cols_n - 1) // cols_n + 1
        dims = (rows_n, nx, nz, cap, slots // CBLK)
        return per_device(dims, assembly, slot_tile, pivots, inverses)

    in_specs = (P("prow", "pcol", None, None, None), P("prow", "pcol"), P(), P())
    out_specs = P(None, "prow", "pcol")
    return jax.shard_map(body, mesh=mesh, in_specs=in_specs, out_specs=out_specs, check_vma=False)
```

```python
import functools

import jax
import jax.numpy as jnp
from jax import lax
from jax.experimental import pallas as pl
from jax.experimental.pallas import tpu as pltpu
from jax.sharding import PartitionSpec as P

CBLK = 2
NB = 128
CHUNKS = 1
MESH = pl.DeviceIdType.MESH
HI = lax.Precision.HIGHEST


def comm_kernel(
    dims, slot_ref, piv_ref, piv_row, inv_ref, asm_hbm,
    m_hbm, ag_hbm, right_hbm, tops_hbm,
    asm, sendb, mid, recvb, labs, mat, pb, ag, st, pk, pr, ps, rb, fin, wfin, h, right, tops, plan, lab_ref, idx_ref, place,
    out_sem, lab_s, lab_r, a_s, a_r, b_s, b_r, sx_s, sd_s, sr_s, st_r, sc_r, pk_s, pk_r, rs_s, rs_r, t_s, t_r,
    y_s, y_r, k_s, k_r, wb_s, wb_r, g1_s, g1_r, g2_s, g2_r, g3_s, g_sem,
):
    rows_n, nx, nz, cap, row_tiles = dims
    cols_n = nx * nz
    sl = NB // rows_n
    half = NB // 2
    me_r = lax.axis_index("prow")
    me_c = lax.axis_index("pcol")
    me_x = me_c // nz
    me_z = me_c % nz

    def remote(src, dst, ssem, rsem, row, col):
        return pltpu.make_async_remote_copy(
            src_ref=src, dst_ref=dst, send_sem=ssem, recv_sem=rsem,
            device_id=(row, col), device_id_type=MESH)

    load = pltpu.make_async_copy(asm_hbm, asm, out_sem.at[6])
    load.start()

    slots = slot_ref.shape[1]
    ident = slot_ref[...]
    column_tile = ident % (CBLK * cols_n)
    target = column_tile % cols_n
    local = ident // (CBLK * cols_n) * CBLK + column_tile // cols_n
    across = jnp.broadcast_to(target, (slots, slots))
    down = across.T
    before = lax.broadcasted_iota(jnp.int32, (slots, slots), 1) < lax.broadcasted_iota(jnp.int32, (slots, slots), 0)
    rank = jnp.sum(jnp.where((across == down) & before, 1, 0), axis=1, keepdims=True)
    position = down[:, 0:1] * cap + rank
    hit = position == lax.broadcasted_iota(jnp.int32, (slots, NB), 1)
    slot_at = lax.broadcasted_iota(jnp.int32, (slots, NB), 0)
    local_at = jnp.broadcast_to(local, (slots, slots)).T[:, 0:1]
    order = jnp.sum(jnp.where(hit, slot_at, 0), axis=0, keepdims=True)
    names = jnp.sum(jnp.where(hit, local_at + 1, 0), axis=0, keepdims=True) - 1
    plan[...] = jnp.broadcast_to(order, (8, NB))
    lab_ref[...] = jnp.broadcast_to(names, (8, NB))
    to_smem = pltpu.make_async_copy(plan, idx_ref, out_sem.at[0])
    to_smem.start()

    barrier = pltpu.get_barrier_semaphore()

    def greet_col(k, c):
        pl.semaphore_signal(barrier, inc=1, device_id=(me_r, (me_c + k) % cols_n), device_id_type=MESH)
        return c

    def greet_row(k, c):
        pl.semaphore_signal(barrier, inc=1, device_id=((me_r + k) % rows_n, me_c), device_id_type=MESH)
        return c

    lax.fori_loop(1, cols_n, greet_col, 0)
    lax.fori_loop(1, rows_n, greet_row, 0)
    pl.semaphore_wait(barrier, cols_n - 1 + rows_n - 1)

    def lab_copy(d):
        return remote(lab_ref, labs.at[me_c], lab_s.at[d], lab_r.at[me_c], me_r, d)

    def lab_start(k, c):
        lab_copy((me_c + k) % cols_n).start()
        return c

    lax.fori_loop(1, cols_n, lab_start, 0)
    labs[me_c] = lab_ref[...]
    to_smem.wait()
    load.wait()

    def first_hop(c, d):
        dx, dz = d // nz, d % nz
        if c == 0:
            return remote(sendb.at[0, d], mid.at[0, me_x * nz + dz], a_s.at[0, d], b_r.at[0, me_x * nz + dz],
                          me_r, dx * nz + me_z)
        return remote(sendb.at[1, d], mid.at[1, dx * nz + me_z], a_s.at[1, d], b_r.at[1, dx * nz + me_z],
                      me_r, me_x * nz + dz)

    def direct(c, d):
        return remote(sendb.at[c, d], recvb.at[c, me_c], a_s.at[c, d], a_r.at[c, me_c], me_r, d)

    def relay_in(c, dx, dz):
        if c == 0:
            sx = (me_x + nx - dx) % nx
            at = sx * nz + (me_z + dz) % nz
            return remote(sendb.at[0, at], mid.at[0, at], b_s.at[0, at], b_r.at[0, at], me_r, sx * nz + me_z)
        sz = (me_z + nz - dz) % nz
        at = (me_x + dx) % nx * nz + sz
        return remote(sendb.at[1, at], mid.at[1, at], b_s.at[1, at], b_r.at[1, at], me_r, me_x * nz + sz)

    def relay_out(c, dx, dz):
        if c == 0:
            sx = (me_x + nx - dx) % nx
            tz = (me_z + dz) % nz
            at = sx * nz + tz
            src = sx * nz + me_z
            return remote(mid.at[0, at], recvb.at[0, src], b_s.at[0, at], a_r.at[0, src], me_r, me_x * nz + tz)
        sz = (me_z + nz - dz) % nz
        tx = (me_x + dx) % nx
        at = tx * nz + sz
        src = me_x * nz + sz
        return remote(mid.at[1, at], recvb.at[1, src], b_s.at[1, at], a_r.at[1, src], me_r, tx * nz + me_z)

    def offset(k):
        return k % (nx - 1) + 1, k // (nx - 1) + 1

    def peer(dx, dz):
        return (me_x + dx) % nx * nz + (me_z + dz) % nz

    def pack_to(dst, d, e):
        for r in range(cap):
            t = idx_ref[0, d * cap + r]
            for c in range(2):
                dst[c, e, r] = asm[t, c]

    def pack(k, c0):
        d = peer(*offset(k))
        pack_to(sendb, d, d)

        @pl.when(k > 0)
        def _():
            p = peer(*offset(jnp.maximum(k - 1, 0)))
            first_hop(0, p).start()
            first_hop(1, p).start()
        return c0

    relays = (nx - 1) * (nz - 1)
    lax.fori_loop(0, relays, pack, 0)
    axis_peers = [(dx, 0) for dx in range(1, nx)] + [(0, dz) for dz in range(1, nz)]
    for n, (dx, dz) in enumerate(axis_peers):
        d = peer(dx, dz)
        pack_to(sendb, d, d)
        if n == 0:
            p = peer(*offset(relays - 1))
            first_hop(0, p).start()
            first_hop(1, p).start()
        else:
            p = peer(*axis_peers[n - 1])
            direct(0, p).start()
            direct(1, p).start()
    pack_to(recvb, me_c, me_c)
    direct(0, peer(*axis_peers[-1])).start()
    direct(1, peer(*axis_peers[-1])).start()

    def relay(k, c0):
        dx, dz = offset(k)
        for c in range(2):
            relay_in(c, dx, dz).wait_recv()
            relay_out(c, dx, dz).start()
        return c0

    lax.fori_loop(0, relays, relay, 0)

    def lab_wait(k, c):
        s = (me_c + k) % cols_n
        remote(lab_ref, labs.at[s], lab_s.at[s], lab_r.at[s], me_r, s).wait_recv()
        return c

    lax.fori_loop(1, cols_n, lab_wait, 0)
    seen = labs[:, 0, :]
    lane = lax.broadcasted_iota(jnp.int32, seen.shape, 1) - me_c * cap
    code = lax.broadcasted_iota(jnp.int32, seen.shape, 0) * cap + lane
    code = jnp.where((lane >= 0) & (lane < cap), code, 0)
    valid = jnp.where((lane >= 0) & (lane < cap), seen, -1)

    def find(t, c):
        place[t] = jnp.minimum(jnp.sum(jnp.where(valid == t, code, 0)), cols_n * cap - 1)
        return c

    lax.fori_loop(0, row_tiles * CBLK, find, 0)

    def a_wait(k, c):
        s = (me_c + k) % cols_n
        for h in range(2):
            remote(sendb.at[h, s], recvb.at[h, s], a_s.at[h, s], a_r.at[h, s], me_r, s).wait_recv()
        return c

    lax.fori_loop(1, cols_n, a_wait, 0)

    piece = NB // (2 * CHUNKS)

    def part_rows(kind, ch):
        return pl.ds((kind * CHUNKS + ch) * piece, piece)

    def root(b):
        return b // nz, b % nz

    def out_x(b, ch, dx):
        return remote(pb.at[dx, :, part_rows(0, ch), :], st.at[0, ch, b, pl.ds(0, nz)], sx_s.at[0, ch, dx],
                      st_r.at[0, ch, b], me_r, dx * nz + root(b)[1])

    def out_z(b, ch, dz):
        return remote(pb.at[:, dz, part_rows(1, ch), :], st.at[1, ch, b, pl.ds(0, nx)], sx_s.at[1, ch, dz],
                      st_r.at[1, ch, b], me_r, root(b)[0] * nz + dz)

    def to_tile(b, kind, ch, src, ssem, dx, dz):
        return remote(src, ag.at[b, dx, dz, part_rows(kind, ch), :], ssem, sc_r.at[kind, ch, b], me_r, dx * nz + dz)

    def root_copies(b, ch):
        x0, z0 = root(b)
        copies = []
        for k in sorted(range(1, max(nx, nz)), key=lambda k: abs(k - nx // 2)):
            if k < nx:
                copies.append(out_x(b, ch, (x0 + k) % nx))
            if k < nz:
                copies.append(out_z(b, ch, (z0 + k) % nz))
        for k in range(1, nz):
            dz = (z0 + k) % nz
            copies.append(to_tile(b, 0, ch, pb.at[x0, dz, part_rows(0, ch), :], sd_s.at[0, ch, dz], x0, dz))
        for k in range(1, nx):
            dx = (x0 + k) % nx
            copies.append(to_tile(b, 1, ch, pb.at[dx, z0, part_rows(1, ch), :], sd_s.at[1, ch, dx], dx, z0))
        return copies

    def relay_x_copies(b, ch):
        z0 = root(b)[1]
        return [to_tile(b, 0, ch, st.at[0, ch, b, (z0 + k) % nz], sr_s.at[0, ch, b, k], me_x, (z0 + k) % nz)
                for k in range(1, nz)]

    def relay_z_copies(b, ch):
        x0 = root(b)[0]
        return [to_tile(b, 1, ch, st.at[1, ch, b, (x0 + k) % nx], sr_s.at[1, ch, b, k], (x0 + k) % nx, me_z)
                for k in range(1, nx)]

    def is_relay_x(b):
        x0, z0 = root(b)
        return (me_z == z0) & (me_x != x0)

    def is_relay_z(b):
        x0, z0 = root(b)
        return (me_x == x0) & (me_z != z0)

    for b in range(2):
        @pl.when(me_c == b)
        def _():
            def panel(i, c):
                at = place[i * CBLK]
                s = at // cap
                r = at - s * cap
                pb[i // nz, i % nz, :, 0:NB] = recvb[0, s, r]
                pb[i // nz, i % nz, :, NB:2 * NB] = recvb[1, s, r]
                return c

            lax.fori_loop(0, row_tiles, panel, 0)
            for ch in range(CHUNKS):
                for copy in root_copies(b, ch):
                    copy.start()
            ag[b, root(b)[0], root(b)[1]] = pb[root(b)[0], root(b)[1]]

    def pass_on(ch):
        for b in range(2):
            x0, z0 = root(b)

            @pl.when(is_relay_x(b))
            def _():
                part = st.at[0, ch, b, pl.ds(0, nz)]
                remote(part, part, sr_s.at[0, ch, b, 0], st_r.at[0, ch, b], me_r, b).wait_recv()
                for copy in relay_x_copies(b, ch):
                    copy.start()
                ag[b, me_x, z0, part_rows(0, ch), :] = st[0, ch, b, z0]

            @pl.when(is_relay_z(b))
            def _():
                part = st.at[1, ch, b, pl.ds(0, nx)]
                remote(part, part, sr_s.at[1, ch, b, 0], st_r.at[1, ch, b], me_r, b).wait_recv()
                for copy in relay_z_copies(b, ch):
                    copy.start()
                ag[b, x0, me_z, part_rows(1, ch), :] = st[1, ch, b, x0]

    def g1x(ch, dx):
        part = ag.at[:, me_x, me_z, part_rows(0, ch), :]
        return remote(part, part, g1_s.at[0, ch, dx], g1_r.at[0, ch, me_x], me_r, dx * nz + me_z)

    def g1z(ch, dz):
        part = ag.at[:, me_x, me_z, part_rows(1, ch), :]
        return remote(part, part, g1_s.at[1, ch, dz], g1_r.at[1, ch, me_z], me_r, me_x * nz + dz)

    def g2z(sx, b, way):
        part = ag.at[b, sx, me_z, part_rows(0, 0), :]
        return remote(part, part, g2_s.at[0, sx, b, way], g2_r.at[0, sx, b, me_z],
                      me_r, me_x * nz + (me_z + (1, nz - 1)[way]) % nz)

    def g2x(sz, b, way):
        part = ag.at[b, me_x, sz, part_rows(1, 0), :]
        return remote(part, part, g2_s.at[1, sz, b, way], g2_r.at[1, sz, b, me_x],
                      me_r, (me_x + (1, nx - 1)[way]) % nx * nz + me_z)

    def g2z_in(sx, b, sz):
        part = ag.at[b, sx, sz, part_rows(0, 0), :]
        return remote(part, part, g3_s.at[0, sx, b], g2_r.at[0, sx, b, sz], me_r, me_x * nz + sz)

    def g2x_in(sz, b, sx):
        part = ag.at[b, sx, sz, part_rows(1, 0), :]
        return remote(part, part, g3_s.at[1, sz, b], g2_r.at[1, sz, b, sx], me_r, sx * nz + me_z)

    def g3z(sx, b):
        sz = (me_z + (nz - 1, 1)[b]) % nz
        part = ag.at[b, sx, sz, part_rows(0, 0), :]
        return remote(part, part, g3_s.at[0, sx, b], g2_r.at[0, sx, b, sz],
                      me_r, me_x * nz + (me_z + (1, nz - 1)[b]) % nz)

    def g3x(sz, b):
        sx = (me_x + (nx - 1, 1)[b]) % nx
        part = ag.at[b, sx, sz, part_rows(1, 0), :]
        return remote(part, part, g3_s.at[1, sz, b], g2_r.at[1, sz, b, sx],
                      me_r, (me_x + (1, nx - 1)[b]) % nx * nz + me_z)

    def gather_first(ch):
        for b in range(2):
            z0 = root(b)[1]

            @pl.when(me_z != z0)
            def _():
                part = ag.at[b, me_x, me_z, part_rows(0, ch), :]
                remote(part, part, sd_s.at[0, ch, 0], sc_r.at[0, ch, b], me_r, me_x * nz + z0).wait_recv()

        for k in range(1, nx):
            g1x(ch, (me_x + k) % nx).start()
        for b in range(2):
            for way in range(2):
                g2z(me_x, b, way).start()
        for b in range(2):
            x0 = root(b)[0]

            @pl.when(me_x != x0)
            def _():
                part = ag.at[b, me_x, me_z, part_rows(1, ch), :]
                remote(part, part, sd_s.at[1, ch, 0], sc_r.at[1, ch, b], me_r, x0 * nz + me_z).wait_recv()

        for k in range(1, nz):
            g1z(ch, (me_z + k) % nz).start()
        for b in range(2):
            for way in range(2):
                g2x(me_z, b, way).start()

    def gather_second(ch):
        for j in range(1, max(nx, nz)):
            sx = (me_x + j) % nx
            part = ag.at[:, sx, me_z, part_rows(0, ch), :]
            remote(part, part, g1_s.at[0, ch, sx], g1_r.at[0, ch, sx], me_r, sx * nz + me_z).wait_recv()
            for b in range(2):
                for way in range(2):
                    g2z(sx, b, way).start()
            sz = (me_z + j) % nz
            part = ag.at[:, me_x, sz, part_rows(1, ch), :]
            remote(part, part, g1_s.at[1, ch, sz], g1_r.at[1, ch, sz], me_r, me_x * nz + sz).wait_recv()
            for b in range(2):
                for way in range(2):
                    g2x(sz, b, way).start()

    def gather_third(ch):
        for j in range(nx):
            for b in range(2):
                sx = (me_x + j) % nx
                g2z_in(sx, b, (me_z + (nz - 1, 1)[b]) % nz).wait_recv()
                g3z(sx, b).start()
                sz = (me_z + j) % nz
                g2x_in(sz, b, (me_x + (nx - 1, 1)[b]) % nx).wait_recv()
                g3x(sz, b).start()

    def put(i, c):
        rows = pl.ds(pl.multiple_of(i * NB, NB), NB)
        for m in range(CBLK):
            at = place[i * CBLK + m]
            s = at // cap
            r = at - s * cap
            re = recvb[0, s, r]
            im = recvb[1, s, r]
            mat[rows, m * NB:(m + 1) * NB] = re
            mat[rows, (CBLK + m) * NB:(CBLK + m + 1) * NB] = im
        return c

    lax.fori_loop(0, row_tiles, put, 0)
    m_out = pltpu.make_async_copy(mat, m_hbm, out_sem.at[0])
    m_out.start()

    def t_copy(s, d):
        rows = pl.ds(pl.multiple_of(d * sl, sl), sl)
        return remote(mat.at[rows, :], fin.at[2 + s, rows, :], t_s.at[d], t_r.at[s], d, me_c)

    for s in range(2):
        @pl.when(me_r == s)
        def _():
            def go(k, c):
                t_copy(s, (s + k) % rows_n).start()
                return c
            lax.fori_loop(1, rows_n, go, 0)
            fin[2 + s, s * sl:(s + 1) * sl, :] = mat[s * sl:(s + 1) * sl, :]

    def pick(d, c):
        def one(jj, c2):
            for k in range(2):
                r = piv_ref[k, d * sl + jj]
                tile = r // NB
                mine = (tile % rows_n) == me_r
                loc = tile // rows_n * NB + r % NB
                row = mat[pl.ds(loc, 1), :]
                pk[d % 2, d // 2, pl.ds(k * sl + jj, 1), :] = jnp.where(mine, row, 0.0)
            return c2
        return lax.fori_loop(0, sl, one, c)

    lax.fori_loop(0, rows_n, pick, 0)
    me_y = me_r // 2
    me_k = me_r % 2
    partner = me_y * 2 + 1 - me_k
    ny = rows_n // 2

    pk_copy = remote(pk.at[1 - me_k], pr, pk_s, pk_r, partner, me_c)
    pk_copy.start()

    pass_on(0)

    remote(pr, pr, pk_s, pk_r, partner, me_c).wait_recv()
    ps[...] = pk[me_k] + pr[...]

    def rs_copy(ty):
        return remote(ps.at[ty], rb.at[me_y], rs_s.at[ty], rs_r.at[me_y], ty * 2 + me_k, me_c)

    for k in range(1, ny):
        rs_copy((me_y + k) % ny).start()

    gather_first(0)
    for ch in range(1, CHUNKS):
        pass_on(ch)

    mine_rows = pl.ds(pl.multiple_of(me_r * sl, sl), sl)
    total = ps[me_y]
    for k in range(1, ny):
        sy = (me_y + k) % ny
        remote(ps.at[sy], rb.at[sy], rs_s.at[sy], rs_r.at[sy], sy * 2 + me_k, me_c).wait_recv()
        total = total + rb[sy]
    fin[0, mine_rows, :] = total[:sl]
    fin[1, mine_rows, :] = total[sl:]
    for s in range(2):
        @pl.when(me_r != s)
        def _():
            part = fin.at[2 + s, mine_rows, :]
            remote(part, part, t_s.at[s], t_r.at[s], s, me_c).wait_recv()

    def wb_copy(b, d):
        part = wfin.at[b, :, mine_rows, :]
        return remote(part, part, wb_s.at[b, d], wb_r.at[b], me_r, d)

    def wb_root(b):
        x0, z0 = root(b)
        return ([wb_copy(b, (x0 + k) % nx * nz + z0) for k in range(1, nx)]
                + [wb_copy(b, x0 * nz + (z0 + k) % nz) for k in range(1, nz)])

    def wb_pass(b):
        z0 = root(b)[1]
        return [wb_copy(b, me_x * nz + (z0 + k) % nz) for k in range(1, nz)]

    for b in range(2):
        @pl.when(me_c == b)
        def _():
            wfin[b, :, mine_rows, 0:NB] = fin[:, mine_rows, 0:NB]
            wfin[b, :, mine_rows, NB:2 * NB] = fin[:, mine_rows, CBLK * NB:(CBLK + 1) * NB]

            for copy in wb_root(b):
                copy.start()

    def rows_of(w, r):
        rows = pl.ds(pl.multiple_of(r * sl, sl), sl)
        return wfin.at[:, :, rows, :] if w else fin.at[:, rows, :]

    def y_copy(w, ty):
        part = rows_of(w, me_r)
        return remote(part, part, y_s.at[w, ty], y_r.at[w, me_y], ty * 2 + me_k, me_c)

    def k_copy(w, sy):
        part = rows_of(w, sy * 2 + me_k)
        return remote(part, part, k_s.at[w, sy], k_r.at[w, sy], partner, me_c)

    def y_start(w):
        for k in range(1, ny):
            y_copy(w, (me_y + k) % ny).start()
        k_copy(w, me_y).start()

    def y_pass(w):
        for k in range(1, ny):
            sy = (me_y + k) % ny
            part = rows_of(w, sy * 2 + me_k)
            remote(part, part, y_s.at[w, sy], y_r.at[w, sy], sy * 2 + me_k, me_c).wait_recv()
            k_copy(w, sy).start()

    def y_end(w):
        for sy in range(ny):
            part = rows_of(w, sy * 2 + 1 - me_k)
            remote(part, part, k_s.at[w, sy], k_r.at[w, sy], partner, me_c).wait_recv()

    y_start(0)

    def wb_wait(b):
        part = wfin.at[b, :, mine_rows, :]
        remote(part, part, wb_s.at[b, 0], wb_r.at[b], me_r, b).wait_recv()

    for b in range(2):
        @pl.when(is_relay_x(b))
        def _():
            wb_wait(b)
            for copy in wb_pass(b):
                copy.start()

    gather_second(0)
    for ch in range(1, CHUNKS):
        gather_first(ch)
        gather_second(ch)

    for b in range(2):
        @pl.when((me_c != b) & jnp.logical_not(is_relay_x(b)))
        def _():
            wb_wait(b)

    y_start(1)
    y_pass(0)
    gather_third(0)
    y_end(0)
    y_pass(1)
    y_end(1)
    factors(piv_row, inv_ref, fin, wfin, me_c, h, right, tops)
    small = [pltpu.make_async_copy(v, w, out_sem.at[1 + k]) for k, (v, w) in enumerate(
        ((right, right_hbm), (tops, tops_hbm)))]
    for copy in small:
        copy.start()
    outs = []

    def out_lo(k, sz):
        outs.append(pltpu.make_async_copy(ag.at[:, :, sz, part_rows(0, 0), :], ag_hbm.at[:, :, sz, part_rows(0, 0), :],
                                          g_sem.at[0, k]))
        outs[-1].start()

    def out_hi(k, sx):
        outs.append(pltpu.make_async_copy(ag.at[:, sx, :, part_rows(1, 0), :], ag_hbm.at[:, sx, :, part_rows(1, 0), :],
                                          g_sem.at[1, k]))
        outs[-1].start()

    out_lo(0, me_z)
    out_hi(0, me_x)
    for k in (1, nz - 1, nz // 2):
        sz = (me_z + k) % nz
        sx = (me_x + k) % nx
        for b in range(2):
            if k == nz // 2 or b == (0 if k == 1 else 1):
                for j in range(nx):
                    g2z_in(j, b, sz).wait_recv()
                    g2x_in(j, b, sx).wait_recv()
        out_lo(k, sz)
        out_hi(k, sx)

    def sent_col(k, c):
        d = (me_c + k) % cols_n
        lab_copy(d).wait_send()
        direct(0, d).wait_send()
        direct(1, d).wait_send()
        return c

    lax.fori_loop(1, cols_n, sent_col, 0)

    def sent_relay(k, c0):
        for c in range(2):
            relay_out(c, *offset(k)).wait_send()
        return c0

    lax.fori_loop(0, relays, sent_relay, 0)
    pk_copy.wait_send()
    for k in range(1, ny):
        rs_copy((me_y + k) % ny).wait_send()
    for w in range(2):
        for k in range(1, ny):
            y_copy(w, (me_y + k) % ny).wait_send()
        for sy in range(ny):
            k_copy(w, sy).wait_send()
    for b in range(2):
        @pl.when(me_c == b)
        def _():
            for ch in range(CHUNKS):
                for copy in root_copies(b, ch):
                    copy.wait_send()

            for copy in wb_root(b):
                copy.wait_send()

        @pl.when(is_relay_x(b))
        def _():
            for copy in wb_pass(b):
                copy.wait_send()

        @pl.when(is_relay_x(b))
        def _():
            for ch in range(CHUNKS):
                for copy in relay_x_copies(b, ch):
                    copy.wait_send()

        @pl.when(is_relay_z(b))
        def _():
            for ch in range(CHUNKS):
                for copy in relay_z_copies(b, ch):
                    copy.wait_send()

        @pl.when(me_r == b)
        def _():
            def go(k, c):
                t_copy(b, (b + k) % rows_n).wait_send()
                return c
            lax.fori_loop(1, rows_n, go, 0)
    for ch in range(CHUNKS):
        for k in range(1, nx):
            g1x(ch, (me_x + k) % nx).wait_send()
        for k in range(1, nz):
            g1z(ch, (me_z + k) % nz).wait_send()
    for j in range(nx):
        for b in range(2):
            for way in range(2):
                g2z(j, b, way).wait_send()
                g2x(j, b, way).wait_send()
            g3z(j, b).wait_send()
            g3x(j, b).wait_send()
    m_out.wait()
    for copy in small:
        copy.wait()
    for copy in outs:
        copy.wait()


def cmat(v):
    h = v.shape[1] // 2
    re, im = v[:, :h], v[:, h:]
    return jnp.concatenate([v, jnp.concatenate([-im, re], 1)], 0)


def dot(a, b):
    return jnp.dot(a, b, precision=HI, preferred_element_type=jnp.float32)


def mm(a, b):
    return jnp.dot(a, b, preferred_element_type=jnp.float32)


def split(v):
    hi = v.astype(jnp.bfloat16)
    return hi, (v - hi.astype(jnp.float32)).astype(jnp.bfloat16)


def deep(panel):
    hi, lo = split(panel)
    return jnp.concatenate([hi, hi, lo], 1)


def keep(own, my_col):
    lane = lax.broadcasted_iota(jnp.int32, own.shape, 1)
    first = ((lane % (own.shape[1] // 2)) < NB) & (my_col < 2)
    return jnp.where(first, 0.0, own)


def factors(piv_ref, inv_ref, fin, wfin, my_col, h, right, tops):
    wide = fin.shape[2]
    f32 = jnp.float32
    spots = (slice(0, NB), slice(wide // 2, wide // 2 + NB))
    first = jnp.broadcast_to(piv_ref[0:1, :].astype(f32), (NB, NB))
    second = jnp.broadcast_to(piv_ref[1:2, :].astype(f32), (NB, NB)).T
    both = jnp.where(first == second, 1.0, 0.0)
    from_t = dot(both, jnp.concatenate([fin[2], wfin[0, 2], wfin[1, 2]], 1))
    taken = jnp.max(both, axis=1, keepdims=True) > 0
    p1 = jnp.where(taken, from_t, jnp.concatenate([fin[1], wfin[0, 1], wfin[1, 1]], 1))
    i0 = jnp.concatenate([inv_ref[0, 0], inv_ref[0, 1]], 1)
    i1 = jnp.concatenate([inv_ref[1, 0], inv_ref[1, 1]], 1)
    c0 = cmat(fin[0])
    l0p1 = dot(p1[:, wide:wide + 2 * NB], cmat(i0))
    u1 = p1[:, :wide] - dot(l0p1, c0)
    c1 = cmat(u1)
    g = dot(dot(i0, cmat(wfin[1, 0])), cmat(i1))
    h[0:2 * NB] = cmat(dot(i0, c0) - dot(g, c1))
    h[2 * NB:] = cmat(dot(i1, c1))
    tops[0] = fin[0]
    tops[1] = u1

    @pl.when(my_col == 0)
    def _():
        ci = cmat(i0)
        for k, lanes in enumerate(spots):
            h[0:2 * NB, lanes] = -ci[:, k * NB:(k + 1) * NB]
            h[2 * NB:, lanes] = jnp.zeros((2 * NB, NB), f32)
            tops[1, :, lanes] = l0p1[:, k * NB:(k + 1) * NB]

    @pl.when(my_col == 1)
    def _():
        cg = cmat(g)
        ci = cmat(i1)
        for k, lanes in enumerate(spots):
            h[0:2 * NB, lanes] = cg[:, k * NB:(k + 1) * NB]
            h[2 * NB:, lanes] = -ci[:, k * NB:(k + 1) * NB]

    high, low = split(-h[...])
    right[0:wide] = high
    right[wide:2 * wide] = low
    right[2 * wide:3 * wide] = high
    rest = jnp.concatenate([fin[2], fin[3]], 0)
    panel = jnp.concatenate([jnp.concatenate([wfin[b, 2], wfin[b, 3]], 0) for b in range(2)], 1)
    rest = keep(rest, my_col) + mm(deep(panel), right[0:3 * wide])
    high, low = split(rest)
    right[3 * wide:3 * wide + 2 * NB] = high
    right[3 * wide + 2 * NB:] = low


def finish_kernel(rows_n, tiles_step, piv_ref, right, tops, m_ref, g_ref, o_ref):
    i = pl.program_id(0)
    my_col = lax.axis_index("pcol")
    my_row = lax.axis_index("prow")
    wide = m_ref.shape[1]
    bf16 = jnp.bfloat16
    step = tiles_step * NB
    r = lax.broadcasted_iota(jnp.int32, (step, NB), 0)
    row = ((i * tiles_step + r // NB) * rows_n + my_row) * NB + r % NB
    moved = row >= 2 * NB
    hit0 = jnp.where((row == piv_ref[0:1, :]) & moved, 1.0, 0.0)
    hit1 = jnp.where((row == piv_ref[1:2, :]) & moved, 1.0, 0.0)
    in0 = jnp.max(hit0, axis=1, keepdims=True)
    in1 = jnp.max(hit1, axis=1, keepdims=True)
    s = jnp.concatenate([hit0 * (1.0 - in1), hit1], 1).astype(bf16)
    panel = jnp.concatenate([g_ref[0].reshape(step, 2 * NB), g_ref[1].reshape(step, 2 * NB)], 1)
    still = in0 + in1 == 0
    left = jnp.concatenate([deep(jnp.where(still, panel, 0.0)), s, s], 1)
    out = jnp.where(still, keep(m_ref[...], my_col), 0.0) + mm(left, right[...])
    for c in range(2):
        o_ref[c] = out[:, c * (wide // 2):(c + 1) * (wide // 2)]

    @pl.when((i == 0) & (my_row == 0))
    def _():
        for c in range(2):
            o_ref[c, 0:NB] = tops[0, :, c * (wide // 2):(c + 1) * (wide // 2)]

    @pl.when((i == 0) & (my_row == 1))
    def _():
        for c in range(2):
            o_ref[c, 0:NB] = tops[1, :, c * (wide // 2):(c + 1) * (wide // 2)]


def per_device(dims, assembly, slot_tile, pivots, inverses):
    rows_n, nx, nz, cap, row_tiles = dims
    cols_n = nx * nz
    tiles = assembly[0]
    slots = tiles.shape[0]
    sl = NB // rows_n
    rows = row_tiles * NB
    wide = 2 * CBLK * NB
    f32 = jnp.float32
    dma = pltpu.SemaphoreType.DMA
    hbm = pl.BlockSpec(memory_space=pl.ANY)
    smem = pl.BlockSpec(memory_space=pltpu.SMEM)
    vmem = pl.BlockSpec(memory_space=pltpu.VMEM)
    n = max(nx, nz)
    ny = rows_n // 2
    bf16 = jnp.bfloat16
    m_raw, ag, right, tops = pl.pallas_call(
        functools.partial(comm_kernel, dims),
        out_shape=(
            jax.ShapeDtypeStruct((rows, wide), f32),
            jax.ShapeDtypeStruct((2, nx, nz, NB, 2 * NB), f32),
            jax.ShapeDtypeStruct((3 * wide + 4 * NB, wide), bf16),
            jax.ShapeDtypeStruct((2, NB, wide), f32),
        ),
        in_specs=[vmem, smem, vmem, vmem, hbm],
        out_specs=(hbm,) * 4,
        scratch_shapes=[
            pltpu.VMEM((slots, 2, NB, NB), f32),
            pltpu.VMEM((2, cols_n, cap, NB, NB), f32),
            pltpu.VMEM((2, cols_n, cap, NB, NB), f32),
            pltpu.VMEM((2, cols_n, cap, NB, NB), f32),
            pltpu.VMEM((cols_n, 8, 128), jnp.int32),
            pltpu.VMEM((rows, wide), f32),
            pltpu.VMEM((nx, nz, NB, 2 * NB), f32),
            pltpu.VMEM((2, nx, nz, NB, 2 * NB), f32),
            pltpu.VMEM((2, CHUNKS, 2, n, NB // (2 * CHUNKS), 2 * NB), f32),
            pltpu.VMEM((2, ny, 2 * sl, wide), f32),
            pltpu.VMEM((ny, 2 * sl, wide), f32),
            pltpu.VMEM((ny, 2 * sl, wide), f32),
            pltpu.VMEM((ny, 2 * sl, wide), f32),
            pltpu.VMEM((4, NB, wide), f32),
            pltpu.VMEM((2, 4, NB, 2 * NB), f32),
            pltpu.VMEM((4 * NB, wide), f32),
            pltpu.VMEM((3 * wide + 4 * NB, wide), bf16),
            pltpu.VMEM((2, NB, wide), f32),
            pltpu.VMEM((8, NB), jnp.int32),
            pltpu.VMEM((8, NB), jnp.int32),
            pltpu.SMEM((8, NB), jnp.int32),
            pltpu.SMEM((slots,), jnp.int32),
            dma((7,)),
            dma((cols_n,)), dma((cols_n,)),
            dma((2, cols_n)), dma((2, cols_n)),
            dma((2, cols_n)), dma((2, cols_n)),
            dma((2, CHUNKS, n)), dma((2, CHUNKS, n)), dma((2, CHUNKS, 2, n)), dma((2, CHUNKS, 2)), dma((2, CHUNKS, 2)),
            dma, dma,
            dma((ny,)), dma((ny,)),
            dma((rows_n,)), dma((2,)),
            dma((2, ny)), dma((2, ny)), dma((2, ny)), dma((2, ny)),
            dma((2, cols_n)), dma((2,)),
            dma((2, CHUNKS, n)), dma((2, CHUNKS, n)),
            dma((2, n, 2, 2)), dma((2, n, 2, n)), dma((2, n, 2)),
            dma((2, n)),
        ],
        compiler_params=pltpu.CompilerParams(
            collective_id=0, has_side_effects=True, vmem_limit_bytes=63 * 1024 * 1024),
        name="exchange",
    )(slot_tile, pivots, pivots, inverses, tiles)

    tiles_step = 4
    step = tiles_step * NB
    whole = lambda *shape: pl.BlockSpec(shape, lambda i: (0,) * len(shape))
    return pl.pallas_call(
        functools.partial(finish_kernel, rows_n, tiles_step),
        grid=(row_tiles // tiles_step,),
        out_shape=jax.ShapeDtypeStruct((2, rows, CBLK * NB), f32),
        in_specs=[
            whole(2, NB), whole(3 * wide + 4 * NB, wide), whole(2, NB, wide),
            pl.BlockSpec((step, wide), lambda i: (i, 0)),
            pl.BlockSpec((2, tiles_step, NB, 2 * NB), lambda i: (0, i, 0, 0)),
        ],
        out_specs=pl.BlockSpec((2, step, CBLK * NB), lambda i: (0, i, 0)),
        compiler_params=pltpu.CompilerParams(dimension_semantics=("arbitrary",), vmem_limit_bytes=63 * 1024 * 1024),
        name="finish",
    )(pivots, right, tops, m_raw, ag.reshape(2, row_tiles, NB, 2 * NB))


def grid_of(cols_n):
    nx = 1
    while nx * nx < cols_n:
        nx *= 2
    return nx, cols_n // nx


def solution(mesh):
    rows_n, cols_n = mesh.shape["prow"], mesh.shape["pcol"]
    nx, nz = grid_of(cols_n)

    def body(assembly, slot_tile, pivots, inverses):
        slots = assembly.shape[1]
        cap = (slots + cols_n - 1) // cols_n + 1
        dims = (rows_n, nx, nz, cap, slots // CBLK)
        return per_device(dims, assembly, slot_tile, pivots, inverses)

    in_specs = (P("prow", "pcol", None, None, None), P("prow", "pcol"), P(), P())
    out_specs = P(None, "prow", "pcol")
    return jax.shard_map(body, mesh=mesh, in_specs=in_specs, out_specs=out_specs, check_vma=False)
```

```python
import functools

import jax
import jax.numpy as jnp
from jax import lax
from jax.experimental import pallas as pl
from jax.experimental.pallas import tpu as pltpu
from jax.sharding import PartitionSpec as P

CBLK = 2
NB = 128
CHUNKS = 1
MESH = pl.DeviceIdType.MESH
HI = lax.Precision.HIGHEST


def comm_kernel(
    dims, slot_ref, piv_ref, piv_row, inv_ref, asm_hbm,
    m_hbm, ag_hbm, right_hbm, tops_hbm,
    asm, sendb, mid, recvb, labs, mat, pb, ag, st, pk, pr, ps, rb, fin, wfin, h, right, tops, plan, lab_ref, idx_ref, place,
    out_sem, lab_s, lab_r, a_s, a_r, b_s, b_r, sx_s, sd_s, sr_s, st_r, sc_r, pk_s, pk_r, rs_s, rs_r, t_s, t_r,
    y_s, y_r, k_s, k_r, wb_s, wb_r, g1_s, g1_r, g2_s, g2_r, g3_s, g_sem,
):
    rows_n, nx, nz, cap, row_tiles = dims
    cols_n = nx * nz
    sl = NB // rows_n
    half = NB // 2
    me_r = lax.axis_index("prow")
    me_c = lax.axis_index("pcol")
    me_x = me_c // nz
    me_z = me_c % nz

    def remote(src, dst, ssem, rsem, row, col):
        return pltpu.make_async_remote_copy(
            src_ref=src, dst_ref=dst, send_sem=ssem, recv_sem=rsem,
            device_id=(row, col), device_id_type=MESH)

    load = pltpu.make_async_copy(asm_hbm, asm, out_sem.at[6])
    load.start()

    slots = slot_ref.shape[1]
    ident = slot_ref[...]
    column_tile = ident % (CBLK * cols_n)
    target = column_tile % cols_n
    local = ident // (CBLK * cols_n) * CBLK + column_tile // cols_n
    across = jnp.broadcast_to(target, (slots, slots))
    down = across.T
    before = lax.broadcasted_iota(jnp.int32, (slots, slots), 1) < lax.broadcasted_iota(jnp.int32, (slots, slots), 0)
    rank = jnp.sum(jnp.where((across == down) & before, 1, 0), axis=1, keepdims=True)
    position = down[:, 0:1] * cap + rank
    hit = position == lax.broadcasted_iota(jnp.int32, (slots, NB), 1)
    slot_at = lax.broadcasted_iota(jnp.int32, (slots, NB), 0)
    local_at = jnp.broadcast_to(local, (slots, slots)).T[:, 0:1]
    order = jnp.sum(jnp.where(hit, slot_at, 0), axis=0, keepdims=True)
    names = jnp.sum(jnp.where(hit, local_at + 1, 0), axis=0, keepdims=True) - 1
    plan[...] = jnp.broadcast_to(order, (8, NB))
    lab_ref[...] = jnp.broadcast_to(names, (8, NB))
    to_smem = pltpu.make_async_copy(plan, idx_ref, out_sem.at[0])
    to_smem.start()

    barrier = pltpu.get_barrier_semaphore()

    def greet_col(k, c):
        pl.semaphore_signal(barrier, inc=1, device_id=(me_r, (me_c + k) % cols_n), device_id_type=MESH)
        return c

    def greet_row(k, c):
        pl.semaphore_signal(barrier, inc=1, device_id=((me_r + k) % rows_n, me_c), device_id_type=MESH)
        return c

    lax.fori_loop(1, cols_n, greet_col, 0)
    lax.fori_loop(1, rows_n, greet_row, 0)
    pl.semaphore_wait(barrier, cols_n - 1 + rows_n - 1)

    def lab_copy(d):
        return remote(lab_ref, labs.at[me_c], lab_s.at[d], lab_r.at[me_c], me_r, d)

    def lab_start(k, c):
        lab_copy((me_c + k) % cols_n).start()
        return c

    lax.fori_loop(1, cols_n, lab_start, 0)
    labs[me_c] = lab_ref[...]
    to_smem.wait()
    load.wait()

    def first_hop(c, d):
        dx, dz = d // nz, d % nz
        if c == 0:
            return remote(sendb.at[0, d], mid.at[0, me_x * nz + dz], a_s.at[0, d], b_r.at[0, me_x * nz + dz],
                          me_r, dx * nz + me_z)
        return remote(sendb.at[1, d], mid.at[1, dx * nz + me_z], a_s.at[1, d], b_r.at[1, dx * nz + me_z],
                      me_r, me_x * nz + dz)

    def direct(c, d):
        return remote(sendb.at[c, d], recvb.at[c, me_c], a_s.at[c, d], a_r.at[c, me_c], me_r, d)

    def relay_in(c, dx, dz):
        if c == 0:
            sx = (me_x + nx - dx) % nx
            at = sx * nz + (me_z + dz) % nz
            return remote(sendb.at[0, at], mid.at[0, at], b_s.at[0, at], b_r.at[0, at], me_r, sx * nz + me_z)
        sz = (me_z + nz - dz) % nz
        at = (me_x + dx) % nx * nz + sz
        return remote(sendb.at[1, at], mid.at[1, at], b_s.at[1, at], b_r.at[1, at], me_r, me_x * nz + sz)

    def relay_out(c, dx, dz):
        if c == 0:
            sx = (me_x + nx - dx) % nx
            tz = (me_z + dz) % nz
            at = sx * nz + tz
            src = sx * nz + me_z
            return remote(mid.at[0, at], recvb.at[0, src], b_s.at[0, at], a_r.at[0, src], me_r, me_x * nz + tz)
        sz = (me_z + nz - dz) % nz
        tx = (me_x + dx) % nx
        at = tx * nz + sz
        src = me_x * nz + sz
        return remote(mid.at[1, at], recvb.at[1, src], b_s.at[1, at], a_r.at[1, src], me_r, tx * nz + me_z)

    def offset(k):
        return k % (nx - 1) + 1, k // (nx - 1) + 1

    def peer(dx, dz):
        return (me_x + dx) % nx * nz + (me_z + dz) % nz

    def pack_to(dst, d, e):
        for r in range(cap):
            t = idx_ref[0, d * cap + r]
            for c in range(2):
                dst[c, e, r] = asm[t, c]

    def pack(k, c0):
        d = peer(*offset(k))
        pack_to(sendb, d, d)

        @pl.when(k > 0)
        def _():
            p = peer(*offset(jnp.maximum(k - 1, 0)))
            first_hop(0, p).start()
            first_hop(1, p).start()
        return c0

    relays = (nx - 1) * (nz - 1)
    lax.fori_loop(0, relays, pack, 0)
    axis_peers = [(dx, 0) for dx in range(1, nx)] + [(0, dz) for dz in range(1, nz)]
    for n, (dx, dz) in enumerate(axis_peers):
        d = peer(dx, dz)
        pack_to(sendb, d, d)
        if n == 0:
            p = peer(*offset(relays - 1))
            first_hop(0, p).start()
            first_hop(1, p).start()
        else:
            p = peer(*axis_peers[n - 1])
            direct(0, p).start()
            direct(1, p).start()
    pack_to(recvb, me_c, me_c)
    direct(0, peer(*axis_peers[-1])).start()
    direct(1, peer(*axis_peers[-1])).start()

    def relay(k, c0):
        dx, dz = offset(k)
        for c in range(2):
            relay_in(c, dx, dz).wait_recv()
            relay_out(c, dx, dz).start()
        return c0

    lax.fori_loop(0, relays, relay, 0)

    def lab_wait(k, c):
        s = (me_c + k) % cols_n
        remote(lab_ref, labs.at[s], lab_s.at[s], lab_r.at[s], me_r, s).wait_recv()
        return c

    lax.fori_loop(1, cols_n, lab_wait, 0)
    seen = labs[:, 0, :]
    lane = lax.broadcasted_iota(jnp.int32, seen.shape, 1) - me_c * cap
    code = lax.broadcasted_iota(jnp.int32, seen.shape, 0) * cap + lane
    code = jnp.where((lane >= 0) & (lane < cap), code, 0)
    valid = jnp.where((lane >= 0) & (lane < cap), seen, -1)

    def find(t, c):
        place[t] = jnp.minimum(jnp.sum(jnp.where(valid == t, code, 0)), cols_n * cap - 1)
        return c

    lax.fori_loop(0, row_tiles * CBLK, find, 0)

    def a_wait(k, c):
        s = (me_c + k) % cols_n
        for h in range(2):
            remote(sendb.at[h, s], recvb.at[h, s], a_s.at[h, s], a_r.at[h, s], me_r, s).wait_recv()
        return c

    lax.fori_loop(1, cols_n, a_wait, 0)

    piece = NB // (2 * CHUNKS)

    def part_rows(kind, ch):
        return pl.ds((kind * CHUNKS + ch) * piece, piece)

    def root(b):
        return b // nz, b % nz

    def out_x(b, ch, dx):
        return remote(pb.at[dx, :, part_rows(0, ch), :], st.at[0, ch, b, pl.ds(0, nz)], sx_s.at[0, ch, dx],
                      st_r.at[0, ch, b], me_r, dx * nz + root(b)[1])

    def out_z(b, ch, dz):
        return remote(pb.at[:, dz, part_rows(1, ch), :], st.at[1, ch, b, pl.ds(0, nx)], sx_s.at[1, ch, dz],
                      st_r.at[1, ch, b], me_r, root(b)[0] * nz + dz)

    def to_tile(b, kind, ch, src, ssem, dx, dz):
        return remote(src, ag.at[b, dx, dz, part_rows(kind, ch), :], ssem, sc_r.at[kind, ch, b], me_r, dx * nz + dz)

    def root_copies(b, ch):
        x0, z0 = root(b)
        copies = []
        for k in sorted(range(1, max(nx, nz)), key=lambda k: abs(k - nx // 2)):
            if k < nx:
                copies.append(out_x(b, ch, (x0 + k) % nx))
            if k < nz:
                copies.append(out_z(b, ch, (z0 + k) % nz))
        for k in range(1, nz):
            dz = (z0 + k) % nz
            copies.append(to_tile(b, 0, ch, pb.at[x0, dz, part_rows(0, ch), :], sd_s.at[0, ch, dz], x0, dz))
        for k in range(1, nx):
            dx = (x0 + k) % nx
            copies.append(to_tile(b, 1, ch, pb.at[dx, z0, part_rows(1, ch), :], sd_s.at[1, ch, dx], dx, z0))
        return copies

    def relay_x_copies(b, ch):
        z0 = root(b)[1]
        return [to_tile(b, 0, ch, st.at[0, ch, b, (z0 + k) % nz], sr_s.at[0, ch, b, k], me_x, (z0 + k) % nz)
                for k in range(1, nz)]

    def relay_z_copies(b, ch):
        x0 = root(b)[0]
        return [to_tile(b, 1, ch, st.at[1, ch, b, (x0 + k) % nx], sr_s.at[1, ch, b, k], (x0 + k) % nx, me_z)
                for k in range(1, nx)]

    def is_relay_x(b):
        x0, z0 = root(b)
        return (me_z == z0) & (me_x != x0)

    def is_relay_z(b):
        x0, z0 = root(b)
        return (me_x == x0) & (me_z != z0)

    for b in range(2):
        @pl.when(me_c == b)
        def _():
            def panel(i, c):
                at = place[i * CBLK]
                s = at // cap
                r = at - s * cap
                pb[i // nz, i % nz, :, 0:NB] = recvb[0, s, r]
                pb[i // nz, i % nz, :, NB:2 * NB] = recvb[1, s, r]
                return c

            lax.fori_loop(0, row_tiles, panel, 0)
            for ch in range(CHUNKS):
                for copy in root_copies(b, ch):
                    copy.start()
            ag[b, root(b)[0], root(b)[1]] = pb[root(b)[0], root(b)[1]]

    def pass_on(ch):
        for b in range(2):
            x0, z0 = root(b)

            @pl.when(is_relay_x(b))
            def _():
                part = st.at[0, ch, b, pl.ds(0, nz)]
                remote(part, part, sr_s.at[0, ch, b, 0], st_r.at[0, ch, b], me_r, b).wait_recv()
                for copy in relay_x_copies(b, ch):
                    copy.start()
                ag[b, me_x, z0, part_rows(0, ch), :] = st[0, ch, b, z0]

            @pl.when(is_relay_z(b))
            def _():
                part = st.at[1, ch, b, pl.ds(0, nx)]
                remote(part, part, sr_s.at[1, ch, b, 0], st_r.at[1, ch, b], me_r, b).wait_recv()
                for copy in relay_z_copies(b, ch):
                    copy.start()
                ag[b, x0, me_z, part_rows(1, ch), :] = st[1, ch, b, x0]

    def g1x(ch, dx):
        part = ag.at[:, me_x, me_z, part_rows(0, ch), :]
        return remote(part, part, g1_s.at[0, ch, dx], g1_r.at[0, ch, me_x], me_r, dx * nz + me_z)

    def g1z(ch, dz):
        part = ag.at[:, me_x, me_z, part_rows(1, ch), :]
        return remote(part, part, g1_s.at[1, ch, dz], g1_r.at[1, ch, me_z], me_r, me_x * nz + dz)

    def g2z(sx, b, way):
        part = ag.at[b, sx, me_z, part_rows(0, 0), :]
        return remote(part, part, g2_s.at[0, sx, b, way], g2_r.at[0, sx, b, me_z],
                      me_r, me_x * nz + (me_z + (1, nz - 1)[way]) % nz)

    def g2x(sz, b, way):
        part = ag.at[b, me_x, sz, part_rows(1, 0), :]
        return remote(part, part, g2_s.at[1, sz, b, way], g2_r.at[1, sz, b, me_x],
                      me_r, (me_x + (1, nx - 1)[way]) % nx * nz + me_z)

    def g2z_in(sx, b, sz):
        part = ag.at[b, sx, sz, part_rows(0, 0), :]
        return remote(part, part, g3_s.at[0, sx, b], g2_r.at[0, sx, b, sz], me_r, me_x * nz + sz)

    def g2x_in(sz, b, sx):
        part = ag.at[b, sx, sz, part_rows(1, 0), :]
        return remote(part, part, g3_s.at[1, sz, b], g2_r.at[1, sz, b, sx], me_r, sx * nz + me_z)

    def g3z(sx, b):
        sz = (me_z + (nz - 1, 1)[b]) % nz
        part = ag.at[b, sx, sz, part_rows(0, 0), :]
        return remote(part, part, g3_s.at[0, sx, b], g2_r.at[0, sx, b, sz],
                      me_r, me_x * nz + (me_z + (1, nz - 1)[b]) % nz)

    def g3x(sz, b):
        sx = (me_x + (nx - 1, 1)[b]) % nx
        part = ag.at[b, sx, sz, part_rows(1, 0), :]
        return remote(part, part, g3_s.at[1, sz, b], g2_r.at[1, sz, b, sx],
                      me_r, (me_x + (1, nx - 1)[b]) % nx * nz + me_z)

    def gather_first(ch):
        for b in range(2):
            z0 = root(b)[1]

            @pl.when(me_z != z0)
            def _():
                part = ag.at[b, me_x, me_z, part_rows(0, ch), :]
                remote(part, part, sd_s.at[0, ch, 0], sc_r.at[0, ch, b], me_r, me_x * nz + z0).wait_recv()

        for k in range(1, nx):
            g1x(ch, (me_x + k) % nx).start()
        for b in range(2):
            for way in range(2):
                g2z(me_x, b, way).start()
        for b in range(2):
            x0 = root(b)[0]

            @pl.when(me_x != x0)
            def _():
                part = ag.at[b, me_x, me_z, part_rows(1, ch), :]
                remote(part, part, sd_s.at[1, ch, 0], sc_r.at[1, ch, b], me_r, x0 * nz + me_z).wait_recv()

        for k in range(1, nz):
            g1z(ch, (me_z + k) % nz).start()
        for b in range(2):
            for way in range(2):
                g2x(me_z, b, way).start()

    def gather_second(ch):
        for j in range(1, max(nx, nz)):
            sx = (me_x + j) % nx
            part = ag.at[:, sx, me_z, part_rows(0, ch), :]
            remote(part, part, g1_s.at[0, ch, sx], g1_r.at[0, ch, sx], me_r, sx * nz + me_z).wait_recv()
            for b in range(2):
                for way in range(2):
                    g2z(sx, b, way).start()
            sz = (me_z + j) % nz
            part = ag.at[:, me_x, sz, part_rows(1, ch), :]
            remote(part, part, g1_s.at[1, ch, sz], g1_r.at[1, ch, sz], me_r, me_x * nz + sz).wait_recv()
            for b in range(2):
                for way in range(2):
                    g2x(sz, b, way).start()

    def gather_third(ch):
        for j in range(nx):
            for b in range(2):
                sx = (me_x + j) % nx
                g2z_in(sx, b, (me_z + (nz - 1, 1)[b]) % nz).wait_recv()
                g3z(sx, b).start()
                sz = (me_z + j) % nz
                g2x_in(sz, b, (me_x + (nx - 1, 1)[b]) % nx).wait_recv()
                g3x(sz, b).start()

    def put(i, c):
        rows = pl.ds(pl.multiple_of(i * NB, NB), NB)
        for m in range(CBLK):
            at = place[i * CBLK + m]
            s = at // cap
            r = at - s * cap
            re = recvb[0, s, r]
            im = recvb[1, s, r]
            mat[rows, m * NB:(m + 1) * NB] = re
            mat[rows, (CBLK + m) * NB:(CBLK + m + 1) * NB] = im
        return c

    lax.fori_loop(0, row_tiles, put, 0)
    m_out = pltpu.make_async_copy(mat, m_hbm, out_sem.at[0])
    m_out.start()

    def t_copy(s, d):
        rows = pl.ds(pl.multiple_of(d * sl, sl), sl)
        return remote(mat.at[rows, :], fin.at[2 + s, rows, :], t_s.at[d], t_r.at[s], d, me_c)

    for s in range(2):
        @pl.when(me_r == s)
        def _():
            def go(k, c):
                t_copy(s, (s + k) % rows_n).start()
                return c
            lax.fori_loop(1, rows_n, go, 0)
            fin[2 + s, s * sl:(s + 1) * sl, :] = mat[s * sl:(s + 1) * sl, :]

    def pick(d, c):
        def one(jj, c2):
            for k in range(2):
                r = piv_ref[k, d * sl + jj]
                tile = r // NB
                mine = (tile % rows_n) == me_r
                loc = tile // rows_n * NB + r % NB
                row = mat[pl.ds(loc, 1), :]
                pk[d % 2, d // 2, pl.ds(k * sl + jj, 1), :] = jnp.where(mine, row, 0.0)
            return c2
        return lax.fori_loop(0, sl, one, c)

    lax.fori_loop(0, rows_n, pick, 0)
    me_y = me_r // 2
    me_k = me_r % 2
    partner = me_y * 2 + 1 - me_k
    ny = rows_n // 2

    pk_copy = remote(pk.at[1 - me_k], pr, pk_s, pk_r, partner, me_c)
    pk_copy.start()

    pass_on(0)

    remote(pr, pr, pk_s, pk_r, partner, me_c).wait_recv()
    ps[...] = pk[me_k] + pr[...]

    def rs_copy(ty):
        return remote(ps.at[ty], rb.at[me_y], rs_s.at[ty], rs_r.at[me_y], ty * 2 + me_k, me_c)

    for k in range(1, ny):
        rs_copy((me_y + k) % ny).start()

    gather_first(0)
    for ch in range(1, CHUNKS):
        pass_on(ch)

    mine_rows = pl.ds(pl.multiple_of(me_r * sl, sl), sl)
    total = ps[me_y]
    for k in range(1, ny):
        sy = (me_y + k) % ny
        remote(ps.at[sy], rb.at[sy], rs_s.at[sy], rs_r.at[sy], sy * 2 + me_k, me_c).wait_recv()
        total = total + rb[sy]
    fin[0, mine_rows, :] = total[:sl]
    fin[1, mine_rows, :] = total[sl:]
    for s in range(2):
        @pl.when(me_r != s)
        def _():
            part = fin.at[2 + s, mine_rows, :]
            remote(part, part, t_s.at[s], t_r.at[s], s, me_c).wait_recv()

    def wb_copy(b, d):
        part = wfin.at[b, :, mine_rows, :]
        return remote(part, part, wb_s.at[b, d], wb_r.at[b], me_r, d)

    def wb_root(b):
        x0, z0 = root(b)
        return ([wb_copy(b, (x0 + k) % nx * nz + z0) for k in range(1, nx)]
                + [wb_copy(b, x0 * nz + (z0 + k) % nz) for k in range(1, nz)])

    def wb_pass(b):
        z0 = root(b)[1]
        return [wb_copy(b, me_x * nz + (z0 + k) % nz) for k in range(1, nz)]

    for b in range(2):
        @pl.when(me_c == b)
        def _():
            wfin[b, :, mine_rows, 0:NB] = fin[:, mine_rows, 0:NB]
            wfin[b, :, mine_rows, NB:2 * NB] = fin[:, mine_rows, CBLK * NB:(CBLK + 1) * NB]

            for copy in wb_root(b):
                copy.start()

    def rows_of(w, r):
        rows = pl.ds(pl.multiple_of(r * sl, sl), sl)
        return wfin.at[:, :, rows, :] if w else fin.at[:, rows, :]

    def y_copy(w, ty):
        part = rows_of(w, me_r)
        return remote(part, part, y_s.at[w, ty], y_r.at[w, me_y], ty * 2 + me_k, me_c)

    def k_copy(w, sy):
        part = rows_of(w, sy * 2 + me_k)
        return remote(part, part, k_s.at[w, sy], k_r.at[w, sy], partner, me_c)

    def y_start(w):
        for k in range(1, ny):
            y_copy(w, (me_y + k) % ny).start()
        k_copy(w, me_y).start()

    def y_pass(w):
        for k in range(1, ny):
            sy = (me_y + k) % ny
            part = rows_of(w, sy * 2 + me_k)
            remote(part, part, y_s.at[w, sy], y_r.at[w, sy], sy * 2 + me_k, me_c).wait_recv()
            k_copy(w, sy).start()

    def y_end(w):
        for sy in range(ny):
            part = rows_of(w, sy * 2 + 1 - me_k)
            remote(part, part, k_s.at[w, sy], k_r.at[w, sy], partner, me_c).wait_recv()

    y_start(0)

    def wb_wait(b):
        part = wfin.at[b, :, mine_rows, :]
        remote(part, part, wb_s.at[b, 0], wb_r.at[b], me_r, b).wait_recv()

    for b in range(2):
        @pl.when(is_relay_x(b))
        def _():
            wb_wait(b)
            for copy in wb_pass(b):
                copy.start()

    gather_second(0)
    for ch in range(1, CHUNKS):
        gather_first(ch)
        gather_second(ch)

    for b in range(2):
        @pl.when((me_c != b) & jnp.logical_not(is_relay_x(b)))
        def _():
            wb_wait(b)

    y_start(1)
    y_pass(0)
    y_end(0)
    y_pass(1)
    gather_third(0)
    y_end(1)
    factors(piv_row, inv_ref, fin, wfin, me_c, h, right, tops)
    small = [pltpu.make_async_copy(v, w, out_sem.at[1 + k]) for k, (v, w) in enumerate(
        ((right, right_hbm), (tops, tops_hbm)))]
    for copy in small:
        copy.start()
    outs = []

    def out_lo(k, sz):
        outs.append(pltpu.make_async_copy(ag.at[:, :, sz, part_rows(0, 0), :], ag_hbm.at[:, :, sz, part_rows(0, 0), :],
                                          g_sem.at[0, k]))
        outs[-1].start()

    def out_hi(k, sx):
        outs.append(pltpu.make_async_copy(ag.at[:, sx, :, part_rows(1, 0), :], ag_hbm.at[:, sx, :, part_rows(1, 0), :],
                                          g_sem.at[1, k]))
        outs[-1].start()

    out_lo(0, me_z)
    out_hi(0, me_x)
    for k in (1, nz - 1, nz // 2):
        sz = (me_z + k) % nz
        sx = (me_x + k) % nx
        for b in range(2):
            if k == nz // 2 or b == (0 if k == 1 else 1):
                for j in range(nx):
                    g2z_in(j, b, sz).wait_recv()
                    g2x_in(j, b, sx).wait_recv()
        out_lo(k, sz)
        out_hi(k, sx)

    def sent_col(k, c):
        d = (me_c + k) % cols_n
        lab_copy(d).wait_send()
        direct(0, d).wait_send()
        direct(1, d).wait_send()
        return c

    lax.fori_loop(1, cols_n, sent_col, 0)

    def sent_relay(k, c0):
        for c in range(2):
            relay_out(c, *offset(k)).wait_send()
        return c0

    lax.fori_loop(0, relays, sent_relay, 0)
    pk_copy.wait_send()
    for k in range(1, ny):
        rs_copy((me_y + k) % ny).wait_send()
    for w in range(2):
        for k in range(1, ny):
            y_copy(w, (me_y + k) % ny).wait_send()
        for sy in range(ny):
            k_copy(w, sy).wait_send()
    for b in range(2):
        @pl.when(me_c == b)
        def _():
            for ch in range(CHUNKS):
                for copy in root_copies(b, ch):
                    copy.wait_send()

            for copy in wb_root(b):
                copy.wait_send()

        @pl.when(is_relay_x(b))
        def _():
            for copy in wb_pass(b):
                copy.wait_send()

        @pl.when(is_relay_x(b))
        def _():
            for ch in range(CHUNKS):
                for copy in relay_x_copies(b, ch):
                    copy.wait_send()

        @pl.when(is_relay_z(b))
        def _():
            for ch in range(CHUNKS):
                for copy in relay_z_copies(b, ch):
                    copy.wait_send()

        @pl.when(me_r == b)
        def _():
            def go(k, c):
                t_copy(b, (b + k) % rows_n).wait_send()
                return c
            lax.fori_loop(1, rows_n, go, 0)
    for ch in range(CHUNKS):
        for k in range(1, nx):
            g1x(ch, (me_x + k) % nx).wait_send()
        for k in range(1, nz):
            g1z(ch, (me_z + k) % nz).wait_send()
    for j in range(nx):
        for b in range(2):
            for way in range(2):
                g2z(j, b, way).wait_send()
                g2x(j, b, way).wait_send()
            g3z(j, b).wait_send()
            g3x(j, b).wait_send()
    m_out.wait()
    for copy in small:
        copy.wait()
    for copy in outs:
        copy.wait()


def cmat(v):
    h = v.shape[1] // 2
    re, im = v[:, :h], v[:, h:]
    return jnp.concatenate([v, jnp.concatenate([-im, re], 1)], 0)


def dot(a, b):
    return jnp.dot(a, b, precision=HI, preferred_element_type=jnp.float32)


def mm(a, b):
    return jnp.dot(a, b, preferred_element_type=jnp.float32)


def split(v):
    hi = v.astype(jnp.bfloat16)
    return hi, (v - hi.astype(jnp.float32)).astype(jnp.bfloat16)


def deep(panel):
    hi, lo = split(panel)
    return jnp.concatenate([hi, hi, lo], 1)


def keep(own, my_col):
    lane = lax.broadcasted_iota(jnp.int32, own.shape, 1)
    first = ((lane % (own.shape[1] // 2)) < NB) & (my_col < 2)
    return jnp.where(first, 0.0, own)


def factors(piv_ref, inv_ref, fin, wfin, my_col, h, right, tops):
    wide = fin.shape[2]
    f32 = jnp.float32
    spots = (slice(0, NB), slice(wide // 2, wide // 2 + NB))
    first = jnp.broadcast_to(piv_ref[0:1, :].astype(f32), (NB, NB))
    second = jnp.broadcast_to(piv_ref[1:2, :].astype(f32), (NB, NB)).T
    both = jnp.where(first == second, 1.0, 0.0)
    from_t = dot(both, jnp.concatenate([fin[2], wfin[0, 2], wfin[1, 2]], 1))
    taken = jnp.max(both, axis=1, keepdims=True) > 0
    p1 = jnp.where(taken, from_t, jnp.concatenate([fin[1], wfin[0, 1], wfin[1, 1]], 1))
    i0 = jnp.concatenate([inv_ref[0, 0], inv_ref[0, 1]], 1)
    i1 = jnp.concatenate([inv_ref[1, 0], inv_ref[1, 1]], 1)
    c0 = cmat(fin[0])
    l0p1 = dot(p1[:, wide:wide + 2 * NB], cmat(i0))
    u1 = p1[:, :wide] - dot(l0p1, c0)
    c1 = cmat(u1)
    g = dot(dot(i0, cmat(wfin[1, 0])), cmat(i1))
    h[0:2 * NB] = cmat(dot(i0, c0) - dot(g, c1))
    h[2 * NB:] = cmat(dot(i1, c1))
    tops[0] = fin[0]
    tops[1] = u1

    @pl.when(my_col == 0)
    def _():
        ci = cmat(i0)
        for k, lanes in enumerate(spots):
            h[0:2 * NB, lanes] = -ci[:, k * NB:(k + 1) * NB]
            h[2 * NB:, lanes] = jnp.zeros((2 * NB, NB), f32)
            tops[1, :, lanes] = l0p1[:, k * NB:(k + 1) * NB]

    @pl.when(my_col == 1)
    def _():
        cg = cmat(g)
        ci = cmat(i1)
        for k, lanes in enumerate(spots):
            h[0:2 * NB, lanes] = cg[:, k * NB:(k + 1) * NB]
            h[2 * NB:, lanes] = -ci[:, k * NB:(k + 1) * NB]

    high, low = split(-h[...])
    right[0:wide] = high
    right[wide:2 * wide] = low
    right[2 * wide:3 * wide] = high
    rest = jnp.concatenate([fin[2], fin[3]], 0)
    panel = jnp.concatenate([jnp.concatenate([wfin[b, 2], wfin[b, 3]], 0) for b in range(2)], 1)
    rest = keep(rest, my_col) + mm(deep(panel), right[0:3 * wide])
    high, low = split(rest)
    right[3 * wide:3 * wide + 2 * NB] = high
    right[3 * wide + 2 * NB:] = low


def finish_kernel(rows_n, tiles_step, piv_ref, right, tops, m_ref, g_ref, o_ref):
    i = pl.program_id(0)
    my_col = lax.axis_index("pcol")
    my_row = lax.axis_index("prow")
    wide = m_ref.shape[1]
    bf16 = jnp.bfloat16
    step = tiles_step * NB
    r = lax.broadcasted_iota(jnp.int32, (step, NB), 0)
    row = ((i * tiles_step + r // NB) * rows_n + my_row) * NB + r % NB
    moved = row >= 2 * NB
    hit0 = jnp.where((row == piv_ref[0:1, :]) & moved, 1.0, 0.0)
    hit1 = jnp.where((row == piv_ref[1:2, :]) & moved, 1.0, 0.0)
    in0 = jnp.max(hit0, axis=1, keepdims=True)
    in1 = jnp.max(hit1, axis=1, keepdims=True)
    s = jnp.concatenate([hit0 * (1.0 - in1), hit1], 1).astype(bf16)
    panel = jnp.concatenate([g_ref[0].reshape(step, 2 * NB), g_ref[1].reshape(step, 2 * NB)], 1)
    still = in0 + in1 == 0
    left = jnp.concatenate([deep(jnp.where(still, panel, 0.0)), s, s], 1)
    out = jnp.where(still, keep(m_ref[...], my_col), 0.0) + mm(left, right[...])
    for c in range(2):
        o_ref[c] = out[:, c * (wide // 2):(c + 1) * (wide // 2)]

    @pl.when((i == 0) & (my_row == 0))
    def _():
        for c in range(2):
            o_ref[c, 0:NB] = tops[0, :, c * (wide // 2):(c + 1) * (wide // 2)]

    @pl.when((i == 0) & (my_row == 1))
    def _():
        for c in range(2):
            o_ref[c, 0:NB] = tops[1, :, c * (wide // 2):(c + 1) * (wide // 2)]


def per_device(dims, assembly, slot_tile, pivots, inverses):
    rows_n, nx, nz, cap, row_tiles = dims
    cols_n = nx * nz
    tiles = assembly[0]
    slots = tiles.shape[0]
    sl = NB // rows_n
    rows = row_tiles * NB
    wide = 2 * CBLK * NB
    f32 = jnp.float32
    dma = pltpu.SemaphoreType.DMA
    hbm = pl.BlockSpec(memory_space=pl.ANY)
    smem = pl.BlockSpec(memory_space=pltpu.SMEM)
    vmem = pl.BlockSpec(memory_space=pltpu.VMEM)
    n = max(nx, nz)
    ny = rows_n // 2
    bf16 = jnp.bfloat16
    m_raw, ag, right, tops = pl.pallas_call(
        functools.partial(comm_kernel, dims),
        out_shape=(
            jax.ShapeDtypeStruct((rows, wide), f32),
            jax.ShapeDtypeStruct((2, nx, nz, NB, 2 * NB), f32),
            jax.ShapeDtypeStruct((3 * wide + 4 * NB, wide), bf16),
            jax.ShapeDtypeStruct((2, NB, wide), f32),
        ),
        in_specs=[vmem, smem, vmem, vmem, hbm],
        out_specs=(hbm,) * 4,
        scratch_shapes=[
            pltpu.VMEM((slots, 2, NB, NB), f32),
            pltpu.VMEM((2, cols_n, cap, NB, NB), f32),
            pltpu.VMEM((2, cols_n, cap, NB, NB), f32),
            pltpu.VMEM((2, cols_n, cap, NB, NB), f32),
            pltpu.VMEM((cols_n, 8, 128), jnp.int32),
            pltpu.VMEM((rows, wide), f32),
            pltpu.VMEM((nx, nz, NB, 2 * NB), f32),
            pltpu.VMEM((2, nx, nz, NB, 2 * NB), f32),
            pltpu.VMEM((2, CHUNKS, 2, n, NB // (2 * CHUNKS), 2 * NB), f32),
            pltpu.VMEM((2, ny, 2 * sl, wide), f32),
            pltpu.VMEM((ny, 2 * sl, wide), f32),
            pltpu.VMEM((ny, 2 * sl, wide), f32),
            pltpu.VMEM((ny, 2 * sl, wide), f32),
            pltpu.VMEM((4, NB, wide), f32),
            pltpu.VMEM((2, 4, NB, 2 * NB), f32),
            pltpu.VMEM((4 * NB, wide), f32),
            pltpu.VMEM((3 * wide + 4 * NB, wide), bf16),
            pltpu.VMEM((2, NB, wide), f32),
            pltpu.VMEM((8, NB), jnp.int32),
            pltpu.VMEM((8, NB), jnp.int32),
            pltpu.SMEM((8, NB), jnp.int32),
            pltpu.SMEM((slots,), jnp.int32),
            dma((7,)),
            dma((cols_n,)), dma((cols_n,)),
            dma((2, cols_n)), dma((2, cols_n)),
            dma((2, cols_n)), dma((2, cols_n)),
            dma((2, CHUNKS, n)), dma((2, CHUNKS, n)), dma((2, CHUNKS, 2, n)), dma((2, CHUNKS, 2)), dma((2, CHUNKS, 2)),
            dma, dma,
            dma((ny,)), dma((ny,)),
            dma((rows_n,)), dma((2,)),
            dma((2, ny)), dma((2, ny)), dma((2, ny)), dma((2, ny)),
            dma((2, cols_n)), dma((2,)),
            dma((2, CHUNKS, n)), dma((2, CHUNKS, n)),
            dma((2, n, 2, 2)), dma((2, n, 2, n)), dma((2, n, 2)),
            dma((2, n)),
        ],
        compiler_params=pltpu.CompilerParams(
            collective_id=0, has_side_effects=True, vmem_limit_bytes=63 * 1024 * 1024),
        name="exchange",
    )(slot_tile, pivots, pivots, inverses, tiles)

    tiles_step = 8
    step = tiles_step * NB
    whole = lambda *shape: pl.BlockSpec(shape, lambda i: (0,) * len(shape))
    return pl.pallas_call(
        functools.partial(finish_kernel, rows_n, tiles_step),
        grid=(row_tiles // tiles_step,),
        out_shape=jax.ShapeDtypeStruct((2, rows, CBLK * NB), f32),
        in_specs=[
            whole(2, NB), whole(3 * wide + 4 * NB, wide), whole(2, NB, wide),
            pl.BlockSpec((step, wide), lambda i: (i, 0)),
            pl.BlockSpec((2, tiles_step, NB, 2 * NB), lambda i: (0, i, 0, 0)),
        ],
        out_specs=pl.BlockSpec((2, step, CBLK * NB), lambda i: (0, i, 0)),
        compiler_params=pltpu.CompilerParams(dimension_semantics=("arbitrary",), vmem_limit_bytes=63 * 1024 * 1024),
        name="finish",
    )(pivots, right, tops, m_raw, ag.reshape(2, row_tiles, NB, 2 * NB))


def grid_of(cols_n):
    nx = 1
    while nx * nx < cols_n:
        nx *= 2
    return nx, cols_n // nx


def solution(mesh):
    rows_n, cols_n = mesh.shape["prow"], mesh.shape["pcol"]
    nx, nz = grid_of(cols_n)

    def body(assembly, slot_tile, pivots, inverses):
        slots = assembly.shape[1]
        cap = (slots + cols_n - 1) // cols_n + 1
        dims = (rows_n, nx, nz, cap, slots // CBLK)
        return per_device(dims, assembly, slot_tile, pivots, inverses)

    in_specs = (P("prow", "pcol", None, None, None), P("prow", "pcol"), P(), P())
    out_specs = P(None, "prow", "pcol")
    return jax.shard_map(body, mesh=mesh, in_specs=in_specs, out_specs=out_specs, check_vma=False)
```
